32 devices in a mesh: ctx: 16 (over z, y, x), fsdp: 2 (over core).
Axes of the slice: x: 2, y: 2, z: 4, core: 2. Of those that a mesh axis runs over, the one named last changes fastest.
Arguments:
- tokens: bfloat16 [2, 2, 2048, 512], P(None, 'fsdp', 'ctx'), may hold values from -6 to 6
- cotangent: bfloat16 [2, 2, 2048, 512], P(None, 'fsdp', 'ctx'), may hold values from -6 to 6
- lengths: int32 [2, 2, 8], P(None, 'fsdp'), may hold values from 1 to 1024, 2048 in all within a row
- deal_order: int32 [2, 2, 2048], P(None, 'fsdp'), may hold values from 0 to 2047, as said below
- w_query: bfloat16 [512, 512], P('fsdp'), may hold values from -0.25 to 0.25
- w_key: bfloat16 [512, 512], P('fsdp'), may hold values from -0.25 to 0.25
- w_value: bfloat16 [512, 512], P('fsdp'), may hold values from -0.25 to 0.25
- w_out: bfloat16 [512, 512], P('fsdp'), may hold values from -1 to 1
- w_up: bfloat16 [512, 2048], P('fsdp'), may hold values from -0.25 to 0.25
- w_down: bfloat16 [2048, 512], P('fsdp'), may hold values from -0.1875 to 0.1875
- b_query: bfloat16 [512], P('fsdp'), may hold values from -1.796875 to 1.796875
- b_value: bfloat16 [512], P('fsdp'), may hold values from -1.796875 to 1.796875
- b_out: bfloat16 [512], P('fsdp'), may hold values from -1.796875 to 1.796875
- b_up: bfloat16 [2048], P('fsdp'), may hold values from -1.796875 to 1.796875
- b_down: bfloat16 [512], P('fsdp'), may hold values from -1.796875 to 1.796875
- gain_one: bfloat16 [512], P('fsdp'), may hold values from 0.5 to 1.5
- shift_one: bfloat16 [512], P('fsdp'), may hold values from -1.796875 to 1.796875
- gain_two: bfloat16 [512], P('fsdp'), may hold values from 0.5 to 1.5
- shift_two: bfloat16 [512], P('fsdp'), may hold values from -1.796875 to 1.796875
- positions: bfloat16 [1024, 512], P('fsdp'), may hold values from -6 to 6
Outputs:
- output: bfloat16 [2, 2, 2048, 512], P(None, 'fsdp', 'ctx')
- grad_tokens: bfloat16 [2, 2, 2048, 512], P(None, 'fsdp', 'ctx')
- grad_w_query: float32 [512, 512], P('fsdp')
- grad_w_key: float32 [512, 512], P('fsdp')
- grad_w_value: float32 [512, 512], P('fsdp')
- grad_w_out: float32 [512, 512], P('fsdp')
- grad_w_up: float32 [512, 2048], P('fsdp')
- grad_w_down: float32 [2048, 512], P('fsdp')
- grad_b_query: float32 [512], P('fsdp')
- grad_b_value: float32 [512], P('fsdp')
- grad_b_out: float32 [512], P('fsdp')
- grad_b_up: float32 [2048], P('fsdp')
- grad_b_down: float32 [512], P('fsdp')
- grad_gain_one: float32 [512], P('fsdp')
- grad_shift_one: float32 [512], P('fsdp')
- grad_gain_two: float32 [512], P('fsdp')
- grad_shift_two: float32 [512], P('fsdp')
- grad_positions: float32 [1024, 512], P('fsdp')
The draws below stay inside these ranges and needn't reach their ends.
Inputs may be any that keep to these rules, and one draw needn't show every extreme that they name: In every micro-batch and stream the 8 lengths sum to 2048, and the largest is exactly 1024. `deal_order`: for every micro-batch and stream, a permutation of the 2048 places. Dealt place p holds a token of initial places b * 128 to (b + 1) * 128 - 1, with b = (p // 8) % 16.
All inputs are finite; a program needn't handle non-finite values.
Results may differ from the reference program's by a relative error of at most 0.015.
The reference program's roundings to bfloat16 on the way count: a program that leaves them out, or rounds other values in their place, can miss the bound.
Values may be sent and summed in bfloat16 or wider, within the bound.
No kernel may reach another device: no remote copies, remote signals or barrier semaphores. Data moves between devices by JAX's collectives and lax.ppermute only.
A program may use at most 448 MiB of HBM per device.

```python
import math
import jax
import jax.numpy as jnp
import numpy as np
from jax import lax

D = 512
HEADS = 8
HEAD_DIM = 64
FF = 2048
TOK_DEV = 128
MICRO = 2
NSEQ = 8
GROUP = 2048
LONGEST = 1024
STREAMS = 2
SLOT = 8


def shuffle_block(block_key):
    return jax.random.permutation(block_key, TOK_DEV)


def draw_deal_order(key, part):
    block_count = GROUP // TOK_DEV
    unit_count = TOK_DEV // SLOT
    key_list = jax.random.split(jax.random.fold_in(key, 7), MICRO * STREAMS * block_count)
    shuffled = jax.vmap(shuffle_block)(key_list).astype(jnp.int32)
    shuffled = shuffled.reshape(MICRO, STREAMS, block_count, unit_count, SLOT)
    offsets = (jnp.arange(block_count, dtype=jnp.int32) * TOK_DEV).reshape(1, 1, block_count, 1, 1)
    source = shuffled + offsets
    return jnp.transpose(source, (0, 1, 3, 2, 4)).reshape(MICRO, STREAMS, GROUP).astype(jnp.int32)


def steps_of(key, shape, pieces, low, top_value):
    loudness = 1.0
    for position, shards_of in pieces:
        heights = jax.random.uniform(jax.random.fold_in(jax.random.fold_in(key, 6), position), (shards_of,), jnp.float32, low / len(pieces), top_value / len(pieces))
        loudness = loudness * jnp.repeat(jnp.exp(heights), shape[position] // shards_of).reshape((-1,) + (1,) * (len(shape) - 1 - position))
    return loudness


def profile(count, total, bound, skew):
    weights = [(1 << 20) // math.isqrt(grade ** skew) + 1 for grade in range(2, count + 1)]
    spare, given = total - bound - (count - 1), [1] * (count - 1)
    while spare > 0:
        candidates = [i for i in range(count - 1) if given[i] < bound]
        pool, budget = sum([weights[i] for i in candidates]), spare
        for i in candidates:
            addition = min(bound - given[i], max(1, budget * weights[i] // pool), spare)
            given[i] = given[i] + addition
            spare = spare - addition
    return np.array([bound] + given)


def uneven_parts(stream_key, count, total, bound, lean):
    if count == 2:
        one = jax.random.randint(stream_key, (), max(1, total - bound), min(bound, total - 1) + 1)
        return jnp.stack([one, total - one])
    sizes = jnp.asarray(profile(count, total, bound, lean), jnp.int32)
    twos = (count - 1) // 2
    source_of, sink = sizes[1:1 + 2 * twos:2], sizes[2:2 + 2 * twos:2]
    margin = jnp.minimum(source_of - 1, bound - sink)
    moved = jax.random.randint(jax.random.fold_in(stream_key, 1), (twos,), 0, 1 << 20) % (margin + 1)
    sizes = sizes.at[1:1 + 2 * twos:2].set(source_of - moved).at[2:2 + 2 * twos:2].set(sink + moved)
    return sizes[jax.random.permutation(jax.random.fold_in(stream_key, 2), count)]


def centred(stream_key, extent, deviation, bound, shards=(), kind=jnp.bfloat16):
    result = deviation * jax.random.normal(stream_key, extent, jnp.float32)
    if shards:
        result = result * steps_of(stream_key, extent, shards, -0.22, 0.18)
    return jnp.clip(result, -bound, bound).astype(kind)


def setup_inputs(seed: int = 0) -> dict:
    keys = jax.random.split(jax.random.key(seed), 21)
    tokens = centred(keys[0], (MICRO, STREAMS, GROUP, D), 1.0, 6.0, ((1, 2), (2, 16)))
    cotangent = centred(keys[1], (MICRO, STREAMS, GROUP, D), 1.0, 6.0, ((1, 2), (2, 16)))
    lengths = jax.vmap(lambda own: uneven_parts(own, NSEQ, GROUP, LONGEST, 2))(jax.random.split(keys[2], MICRO * STREAMS)).reshape((MICRO, STREAMS, NSEQ)).astype(jnp.int32)
    deal_order = draw_deal_order(jax.random.fold_in(keys[20], 71), 0)
    w_query = centred(keys[4], (D, D), D ** -0.5, 0.25, ((0, 2),))
    w_key = centred(keys[5], (D, D), D ** -0.5, 0.25, ((0, 2),))
    w_value = centred(keys[6], (D, D), D ** -0.5, 0.25, ((0, 2),))
    w_out = centred(keys[7], (D, D), (D // 16) ** -0.5, 1.0, ((0, 2),))
    w_up = centred(keys[8], (D, FF), D ** -0.5, 0.25, ((0, 2),))
    w_down = centred(keys[9], (FF, D), (FF // 2) ** -0.5, 0.1875, ((0, 2),))
    b_query = centred(keys[10], (D,), 0.3, 1.796875, ((0, 2),))
    b_value = centred(keys[11], (D,), 0.3, 1.796875, ((0, 2),))
    b_out = centred(keys[12], (D,), 0.3, 1.796875, ((0, 2),))
    b_up = centred(keys[13], (FF,), 0.3, 1.796875, ((0, 2),))
    b_down = centred(keys[14], (D,), 0.3, 1.796875, ((0, 2),))
    gain_one = jnp.clip(1.0 + 0.1 * jax.random.normal(keys[15], (D,), jnp.float32), 0.5, 1.5).astype(jnp.bfloat16)
    shift_one = centred(keys[16], (D,), 0.3, 1.796875, ((0, 2),))
    gain_two = jnp.clip(1.0 + 0.1 * jax.random.normal(keys[17], (D,), jnp.float32), 0.5, 1.5).astype(jnp.bfloat16)
    shift_two = centred(keys[18], (D,), 0.3, 1.796875, ((0, 2),))
    positions = centred(keys[19], (LONGEST, D), 1.0, 6.0, ((0, 2),))
    return {"tokens": tokens, "cotangent": cotangent, "lengths": lengths, "deal_order": deal_order, "w_query": w_query, "w_key": w_key, "w_value": w_value, "w_out": w_out, "w_up": w_up, "w_down": w_down, "b_query": b_query, "b_value": b_value, "b_out": b_out, "b_up": b_up, "b_down": b_down, "gain_one": gain_one, "shift_one": shift_one, "gain_two": gain_two, "shift_two": shift_two, "positions": positions}


epsilon = 1e-05
negative = -1e+30
scale_factor = 0.125
gelu_coeff = 0.7978845608028654
cubic_coeff = 0.044715

@jax.custom_vjp
def low(v):
    return lax.optimization_barrier(v.astype(jnp.bfloat16)).astype(jnp.float32)

@jax.custom_vjp
def low_back(v):
    return v

def low_keep(v):
    return (low(v), None)

def low_pass(kept, grad):
    return (grad,)

def back_keep(v):
    return (v, None)

def back_low(kept, grad):
    return (low(grad),)
low.defvjp(low_keep, low_pass)
low_back.defvjp(back_keep, back_low)

def gelu(values):
    return 0.5 * values * (1.0 + jnp.tanh(gelu_coeff * (values + cubic_coeff * values * values * values)))

def matmul(left_side, right_side):
    return jnp.dot(left_side, right_side, precision=lax.Precision.HIGHEST)

def locate(anchor, seq_lens):
    seg_ends = jnp.cumsum(seq_lens).astype(jnp.int32)
    starts = (seg_ends - seq_lens).astype(jnp.int32)
    segment = lax.optimization_barrier(jnp.sum((anchor[:, None] >= seg_ends[None, :]).astype(jnp.int32), axis=1)).astype(jnp.int32)
    picked = segment[:, None] == jnp.arange(seq_lens.shape[0], dtype=jnp.int32)[None, :]
    seg_first = lax.optimization_barrier(jnp.sum(jnp.where(picked, starts[None, :], 0), axis=1)).astype(jnp.int32)
    return (segment, (anchor - seg_first).astype(jnp.int32))

def normalize(values, gain_vec, shift_vec):
    center = values - lax.optimization_barrier(jnp.mean(values, axis=-1, keepdims=True))
    inv_std = lax.rsqrt(lax.optimization_barrier(jnp.mean(center * center, axis=-1, keepdims=True)) + epsilon)
    normed = center * inv_std
    return normed * gain_vec + shift_vec

def one_layer(rows_in, segment, place, params):
    w_query, w_key, w_value, w_out, w_up, w_down, b_query, b_value, b_out, b_up, b_down, gain_one, shift_one, gain_two, shift_two, positions = params
    hidden = low_back(rows_in) + jnp.take(positions, place, axis=0)
    hidden_low = low(hidden)
    query_rows = low_back(low(matmul(hidden_low, w_query) + b_query))
    key_rows = low_back(low(matmul(hidden_low, w_key)))
    valued = low_back(low(matmul(hidden_low, w_value) + b_value))
    group_rows = rows_in.shape[0]
    key_heads = key_rows.reshape(group_rows, HEADS, HEAD_DIM)
    value_heads = valued.reshape(group_rows, HEADS, HEAD_DIM)
    block_rows = min(512, group_rows)
    blocks = group_rows // block_rows

    def attend(packed_block):
        query_heads, block_seg, block_place = packed_block
        raw_scores = jnp.einsum('qhd,khd->hqk', query_heads, key_heads, precision=lax.Precision.HIGHEST) * scale_factor
        allowed = (block_seg[:, None] == segment[None, :]) & (place[None, :] <= block_place[:, None])
        scores = low_back(jnp.where(allowed[None], raw_scores, negative))
        attn_probs = low(jax.nn.softmax(scores, axis=-1))
        return jnp.einsum('hqk,khd->qhd', attn_probs, value_heads, precision=lax.Precision.HIGHEST)
    attended = lax.map(jax.checkpoint(attend), (query_rows.reshape(blocks, block_rows, HEADS, HEAD_DIM), segment.reshape(blocks, block_rows), place.reshape(blocks, block_rows)))
    attended = low_back(low(attended.reshape(group_rows, D)))
    branch = low_back(matmul(attended, w_out) + b_out)
    first_norm = normalize(hidden + branch, gain_one, shift_one)
    up_pre = low_back(matmul(low(first_norm), w_up) + b_up)
    gelu_low = low(gelu(up_pre))
    ffn_out = low_back(matmul(gelu_low, w_down) + b_down)
    return normalize(first_norm + ffn_out, gain_two, shift_two)

def deal_rows(values, places):
    return jnp.take(values, places, axis=0)

def undeal_rows(values, places):
    return jnp.zeros_like(values).at[places].set(values)

def reference(tokens, cotangent, lengths, deal_order, w_query, w_key, w_value, w_out, w_up, w_down, b_query, b_value, b_out, b_up, b_down, gain_one, shift_one, gain_two, shift_two, positions):
    params = tuple((member.astype(jnp.float32) for member in (w_query, w_key, w_value, w_out, w_up, w_down, b_query, b_value, b_out, b_up, b_down, gain_one, shift_one, gain_two, shift_two, positions)))
    group_count = MICRO * STREAMS
    order_rows = deal_order.reshape(group_count, GROUP).astype(jnp.int32)
    seq_lens = lengths.reshape(group_count, NSEQ).astype(jnp.int32)
    anchor = jnp.arange(GROUP, dtype=jnp.int32)
    segments, places = jax.vmap(locate, in_axes=(None, 0))(anchor, seq_lens)
    inputs = tokens.astype(jnp.float32).reshape(group_count, GROUP, D)

    def forward(inputs, params):

        def single(packed):
            rows_in, segment, place = packed
            return one_layer(rows_in, segment, place, params)
        return lax.map(single, (inputs, segments, places))
    natural, pullback = jax.vjp(forward, inputs, params)
    grad_out = jax.vmap(undeal_rows)(cotangent.astype(jnp.float32).reshape(group_count, GROUP, D), order_rows)
    grad_inputs, grad_params = pullback(grad_out)
    output = jax.vmap(deal_rows)(natural, order_rows).astype(jnp.bfloat16).reshape(MICRO, STREAMS, GROUP, D)
    grad_tokens = grad_inputs.astype(jnp.bfloat16).reshape(MICRO, STREAMS, GROUP, D)
    return (output, grad_tokens, grad_params[0], grad_params[1], grad_params[2], grad_params[3], grad_params[4], grad_params[5], grad_params[6], grad_params[7], grad_params[8], grad_params[9], grad_params[10], grad_params[11], grad_params[12], grad_params[13], grad_params[14], grad_params[15])
```

```python
import functools

import jax
import jax.numpy as jnp
from jax import lax
from jax.experimental import pallas as pl
from jax.experimental.pallas import tpu as pltpu
from jax.sharding import PartitionSpec as P

HEADS = 8
epsilon = 1e-05
gelu_coeff = 0.7978845608028654
cubic_coeff = 0.044715
BF = jnp.bfloat16
F32 = jnp.float32
SWAP = ((0, 1), (1, 0))
BOTH = ("ctx", "fsdp")
FAR = 1 << 30


def dot(a, b):
    return jnp.dot(a, b, preferred_element_type=F32)


def dot_tn(a, b):
    return lax.dot_general(a, b, (((0,), (0,)), ((), ())), preferred_element_type=F32)


def dot_nt(a, b):
    return lax.dot_general(a, b, (((1,), (1,)), ((), ())), preferred_element_type=F32)


def gelu_parts(u):
    inner = gelu_coeff * (u + cubic_coeff * u * u * u)
    bent = jnp.tanh(inner)
    value = 0.5 * u * (1.0 + bent)
    slope = 0.5 * (1.0 + bent) + 0.5 * u * (1.0 - bent * bent) * gelu_coeff * (
        1.0 + 3.0 * cubic_coeff * u * u
    )
    return value, slope


def normalize(z):
    center = z - jnp.mean(z, axis=-1, keepdims=True)
    inv = lax.rsqrt(jnp.mean(center * center, axis=-1, keepdims=True) + epsilon)
    return center * inv, inv


def normalize_back(t, normed, inv):
    return inv * (
        t
        - jnp.mean(t, axis=-1, keepdims=True)
        - normed * jnp.mean(t * normed, axis=-1, keepdims=True)
    )


def first_places(info, spots):
    first, end = jnp.zeros_like(spots), 0
    for n in range(3, info.shape[0]):
        end = end + info[n]
        first = first + jnp.where(spots >= end, info[n], 0)
    return first


def lay(info, whole, own, other):
    n = own.shape[0]
    mine = info[0] == 0
    whole[0:n, :] = jnp.where(mine, own[...], other[...])
    whole[n : 2 * n, :] = jnp.where(mine, other[...], own[...])


def full_row(info, own, other, at, count=1):
    mine = info[0] == 0
    rows = [x[at + n : at + n + 1, :] for x in (own, other) for n in range(count)]
    first = [jnp.where(mine, rows[n], rows[count + n]) for n in range(count)]
    second = [jnp.where(mine, rows[count + n], rows[n]) for n in range(count)]
    return jnp.concatenate(first + second, axis=1)


def stack_vectors(vectors, width):
    row, at = iota((16, width), 0), 0
    table = jnp.zeros((16, width), F32)
    for x in vectors:
        for n in range(x.shape[0] // width):
            part = x[n * width : n * width + width].astype(F32)
            table = jnp.where(row == at, part[None, :], table)
            at += 1
    return table


def iota(shape, axis):
    return lax.broadcasted_iota(jnp.int32, shape, axis)


def params(limit=56):
    return pltpu.CompilerParams(vmem_limit_bytes=limit * 1024 * 1024)


def lasting(us):
    return pl.CostEstimate(flops=us, transcendentals=0, bytes_accessed=us)


def fixed(shape):
    return pl.BlockSpec(shape, lambda *_: (0,) * len(shape), pipeline_mode=pl.Buffered(1))


def paired(rows):
    return pl.BlockSpec((rows, 128), lambda p, *_: (0, p))


def project_kernel(info, *refs, blocks, offset, own):
    toks = refs[:blocks]
    pos_a, pos_b, wk_a, wk_b, wv_a, wv_b, wq_a, wq_b, vec_a, vec_b = refs[blocks : blocks + 10]
    outs = refs[blocks + 10 :]
    k_ref, v_ref = outs[:2]
    wk, wv, wq, tok = outs[-4:]
    step = pl.program_id(0)
    rows = tok.shape[0]

    @pl.when(step == 0)
    def _():
        lay(info, wk, wk_a, wk_b)
        lay(info, wv, wv_a, wv_b)
        if own:
            lay(info, wq, wq_a, wq_b)

    for n in range(blocks):

        @pl.when(step == n)
        def _():
            tok[...] = toks[n][...]

    spots = info[1] + offset + step * rows + iota((rows, 1), 0)
    place = spots - first_places(info, spots)
    hidden = tok[...].astype(F32)
    half = pos_a.shape[0]
    chunk = min(half, 512)
    for part, begin in ((pos_a, info[0] * half), (pos_b, (1 - info[0]) * half)):
        for at in range(0, half, chunk):
            hot = (place - begin - at == iota((rows, chunk), 1)).astype(F32).astype(BF)
            hidden = hidden + dot(hot, part[at : at + chunk, :])
    low = hidden.astype(BF)
    k_ref[...] = dot(low, wk[...]).astype(BF)
    v_ref[...] = (dot(low, wv[...]) + full_row(info, vec_a, vec_b, 7)).astype(BF)
    if own:
        q_ref, hidden_ref, low_ref = outs[2:5]
        q_ref[...] = ((dot(low, wq[...]) + full_row(info, vec_a, vec_b, 6)).astype(BF).astype(F32) * 0.125).astype(BF)
        hidden_ref[...] = hidden
        low_ref[...] = low


def project(info, toks, offset, own, pos, wk, wv, wq, vec):
    rows, width = toks[0].shape
    blocks = len(toks)
    tall = pl.BlockSpec((rows, width), lambda n, *_: (n, 0))
    flat = jax.ShapeDtypeStruct((rows * blocks, width), BF)
    square = pltpu.VMEM((width, width), BF)
    args = (*toks, *pos, *wk, *wv, *wq, *vec)
    return pl.pallas_call(
        functools.partial(project_kernel, blocks=blocks, offset=offset, own=own),
        grid_spec=pltpu.PrefetchScalarGridSpec(
            num_scalar_prefetch=1,
            grid=(blocks,),
            in_specs=[fixed(x.shape) for x in args],
            out_specs=[tall] * (5 if own else 2),
            scratch_shapes=[square, square, square, pltpu.VMEM((rows, width), BF)],
        ),
        out_shape=[flat] * 3 + [jax.ShapeDtypeStruct((rows, width), F32), flat] if own else [flat] * 2,
        compiler_params=params(),
        cost_estimate=lasting(2 * blocks + 2),
        name="project",
    )(info, *args)


def stat_rows(table):
    high = table.astype(BF).astype(F32)
    middle = (table - high).astype(BF).astype(F32)
    low = table - high - middle
    count = table.shape[1] // 128
    rows = [
        part[half : half + 1, 128 * n : 128 * n + 128]
        for part in (high, middle, low)
        for half in range(2)
        for n in range(count)
    ]
    rows.append(jnp.zeros((16 - len(rows), 128), F32))
    return jnp.concatenate(rows, axis=0).astype(BF)


def stat_row(rows16, half, queries):
    count = queries // 128
    wide = rows16.astype(F32)
    total = wide[0 : 2 * count] + wide[2 * count : 4 * count] + wide[4 * count : 6 * count]
    return jnp.concatenate([total[half * count + n : half * count + n + 1] for n in range(count)], axis=1)


def chunks_of(cols):
    step = cols if cols <= 2048 else 768
    return [slice(at, min(at + step, cols)) for at in range(0, cols, step)]


def bias_scratch(rows, cols):
    return pltpu.VMEM((rows, cols) if len(chunks_of(cols)) == 1 else (8, 128), F32)


def query_bias(info, rows, before, chunk):
    spots = info[1] + iota((rows, 1), 0)
    first = first_places(info, spots) - (info[1] - before)
    last = iota((rows, 1), 0) + before
    col = iota((rows, chunk.stop - chunk.start), 1) + chunk.start
    return jnp.where((col >= first) & (col <= last), 0.0, -1e30)


def key_bias(info, rows, chunk):
    spots = info[1] + chunk.start + iota((1, chunk.stop - chunk.start), 1)
    first = jnp.where(spots < info[2], first_places(info, spots) - info[1], FAR)
    shape = (rows, chunk.stop - chunk.start)
    row = iota(shape, 0)
    return jnp.where((row >= first) & (row <= iota(shape, 1) + chunk.start), 0.0, -1e30)


def forward_kernel(info, q_ref, kp_ref, k_ref, vp_ref, v_ref, a_ref, exact_ref, log_ref, stat_ref, bias, keys, values):
    rows, before = q_ref.shape[0], kp_ref.shape[0]

    chunks = chunks_of(keys.shape[0])
    make_bias = functools.partial(query_bias, info, rows, before)

    @pl.when(pl.program_id(0) == 0)
    def _():
        if len(chunks) == 1:
            bias[...] = make_bias(chunks[0])

    keys[0:before, :] = kp_ref[...]
    keys[before:, :] = k_ref[...]
    values[0:before, :] = vp_ref[...]
    values[before:, :] = v_ref[...]
    logs = []
    for half in range(2):
        lanes = slice(64 * half, 64 * half + 64)


        def scores_of(chunk):
            mask = bias[...] if len(chunks) == 1 else make_bias(chunk)
            return dot_nt(q_ref[:, lanes], keys[chunk, lanes]) + mask

        if len(chunks) == 1:
            scores = scores_of(chunks[0])
            top = jnp.max(scores, axis=1, keepdims=True)
            raised = jnp.exp(scores - top)
            total = jnp.sum(raised, axis=1, keepdims=True)
            probs = raised * (1.0 / total)
            low = probs.astype(BF)
            rest = (probs - low.astype(F32)).astype(BF)
            attended = dot(low, values[:, lanes])
            exact = attended + dot(rest, values[:, lanes])
        else:
            top = jnp.full((rows, 1), -1e30, F32)
            for chunk in chunks:
                top = jnp.maximum(top, jnp.max(scores_of(chunk), axis=1, keepdims=True))
            total = jnp.zeros((rows, 1), F32)
            for chunk in chunks:
                total = total + jnp.sum(jnp.exp(scores_of(chunk) - top), axis=1, keepdims=True)
            attended, exact = jnp.zeros((rows, 64), F32), jnp.zeros((rows, 64), F32)
            for chunk in chunks:
                probs = jnp.exp(scores_of(chunk) - top) * (1.0 / total)
                low = probs.astype(BF)
                rest = (probs - low.astype(F32)).astype(BF)
                attended = attended + dot(low, values[chunk, lanes])
                exact = exact + dot(rest, values[chunk, lanes])
            exact = exact + attended
        a_ref[:, lanes] = attended.astype(BF)
        exact_ref[:, lanes] = exact
        logs.append(jnp.broadcast_to(top + jnp.log(total), (rows, 64)))
    wide = jnp.concatenate(logs, axis=1)
    log_ref[...] = wide
    turned = wide.T
    stat_ref[...] = stat_rows(jnp.concatenate([turned[0:1], turned[64:65]], axis=0))


def attend_forward(info, q, kp, k, vp, v):
    rows, width = q.shape
    before = kp.shape[0]
    cols = before + rows
    return pl.pallas_call(
        forward_kernel,
        grid_spec=pltpu.PrefetchScalarGridSpec(
            num_scalar_prefetch=1,
            grid=(width // 128,),
            in_specs=[paired(x.shape[0]) for x in (q, kp, k, vp, v)],
            out_specs=[paired(rows), paired(rows), paired(rows), paired(16)],
            scratch_shapes=[
                bias_scratch(rows, cols),
                pltpu.VMEM((cols, 128), BF),
                pltpu.VMEM((cols, 128), BF),
            ],
        ),
        out_shape=[
            jax.ShapeDtypeStruct((rows, width), BF),
            jax.ShapeDtypeStruct((rows, width), F32),
            jax.ShapeDtypeStruct((rows, width), F32),
            jax.ShapeDtypeStruct((16, width), BF),
        ],
        compiler_params=params(),
        cost_estimate=lasting(12),
        name="attend_forward",
    )(info, q, kp, k, vp, v)


def ffn_kernel(
    info, a_ref, exact_ref, stat_ref, hidden_ref, arrived_ref, row_ref, col_ref, wo_a, wo_b, wu_a, wu_b, wd_a, wd_b, vec_a, vec_b,
    leaving_ref, msg_ref, dz1_ref, active_ref, df_ref, h1_ref, du_ref, do_ref, sums_ref,
    wo, wu, wd, slopes, stats,
):
    lay(info, wo, wo_a, wo_b)
    lay(info, wu, wu_a, wu_b)
    lay(info, wd, wd_a, wd_b)
    rows, width = hidden_ref.shape
    hidden_units = wu.shape[1]
    bo, bd, g1, s1, g2, s2 = (full_row(info, vec_a, vec_b, n) for n in range(6))
    bu = full_row(info, vec_a, vec_b, 8, hidden_units // width)
    pick = (iota((rows, rows), 0) == row_ref[...]).astype(F32).astype(BF)
    pick_back = (col_ref[...] == iota((rows, rows), 1)).astype(F32).astype(BF)
    dy = dot(pick, arrived_ref[...])

    n1, r1 = normalize(hidden_ref[...] + dot(a_ref[...], wo[...]) + bo)
    h1 = n1 * g1 + s1
    h1_low = h1.astype(BF)
    h1_ref[...] = h1_low
    z2 = h1 + bd
    for at in range(0, hidden_units, width):
        block = slice(at, at + width)
        value, slope = gelu_parts(dot(h1_low, wu[:, block]) + bu[:, block])
        slopes[:, block] = slope
        low = value.astype(BF)
        active_ref[:, block] = low
        z2 = z2 + dot(low, wd[block, :])
    n2, r2 = normalize(z2)
    leaving_ref[...] = dot(pick_back, (n2 * g2 + s2).astype(BF)).astype(BF)

    def add(x):
        return jnp.sum(x, axis=0, keepdims=True)

    dz2 = normalize_back(dy * g2, n2, r2)
    df = dz2.astype(BF)
    df_ref[...] = df
    sums_ref[0:1, :] = add(df.astype(F32))
    sums_ref[3:4, :] = add(dy * n2)
    sums_ref[4:5, :] = add(dy)
    dh1 = dz2
    for at in range(0, hidden_units, width):
        block = slice(at, at + width)
        du = (dot_nt(df, wd[block, :]) * slopes[:, block]).astype(BF)
        du_ref[:, block] = du
        n = 7 + at // width
        sums_ref[n : n + 1, :] = add(du.astype(F32))
        dh1 = dh1 + dot_nt(du, wu[:, block])
    dz1 = normalize_back(dh1 * g1, n1, r1)
    dz1_ref[...] = dz1
    sums_ref[1:2, :] = add(dh1 * n1)
    sums_ref[2:3, :] = add(dh1)
    do = dz1.astype(BF)
    do_ref[...] = do
    sums_ref[5:6, :] = add(do.astype(F32))
    sums_ref[6:7, :] = jnp.zeros((1, width), F32)
    sums_ref[11:16, :] = jnp.zeros((5, width), F32)
    da = dot_nt(do, wo[...]).astype(BF)
    msg_ref[0:rows, :] = da
    terms = da.astype(F32) * exact_ref[...]
    head = iota((HEADS, width), 0)
    lane = iota((HEADS, width), 1) // (width // HEADS)
    ones = (head == lane).astype(F32).astype(BF)
    delta = jnp.zeros((HEADS, rows), F32)
    for _ in range(3):
        part = terms.astype(BF)
        terms = terms - part.astype(F32)
        delta = delta + dot_nt(ones, part)
    for p in range(HEADS // 2):
        stats[:, 128 * p : 128 * p + 128] = stat_rows(delta[2 * p : 2 * p + 2, :])
    msg_ref[rows : rows + 16, :] = stat_ref[...]
    msg_ref[rows + 16 : rows + 32, :] = stats[...]


def feed_forward(info, a, exact, log_stats, hidden, arrived, mine, wo, wu, wd, vec):
    rows, width = hidden.shape
    units = wu[0].shape[1]
    args = (a, exact, log_stats, hidden, arrived, mine.reshape(1, rows), mine.reshape(rows, 1), *wo, *wu, *wd, *vec)
    low = jax.ShapeDtypeStruct((rows, width), BF)
    tall = jax.ShapeDtypeStruct((rows, units), BF)
    outs = [
        low,
        jax.ShapeDtypeStruct((rows + 32, width), BF),
        jax.ShapeDtypeStruct((rows, width), F32),
        tall,
        low,
        low,
        tall,
        low,
        jax.ShapeDtypeStruct((16, width), F32),
    ]
    return pl.pallas_call(
        ffn_kernel,
        grid_spec=pltpu.PrefetchScalarGridSpec(
            num_scalar_prefetch=1,
            grid=(1,),
            in_specs=[fixed(x.shape) for x in args],
            out_specs=[fixed(x.shape) for x in outs],
            scratch_shapes=[
                pltpu.VMEM((width, width), BF),
                pltpu.VMEM((width, units), BF),
                pltpu.VMEM((units, width), BF),
                pltpu.VMEM((rows, units), F32),
                pltpu.VMEM((16, width), BF),
            ],
        ),
        out_shape=outs,
        compiler_params=params(),
        cost_estimate=lasting(10),
        name="feed_forward",
    )(info, *args)


def keep_or_send(info, half, mine, send, at, value):
    at, value = pl.multiple_of(at, 8), value.astype(BF)

    @pl.when(info[0] == half)
    def _():
        mine[pl.ds(at, value.shape[0]), :] = value

    @pl.when(info[0] != half)
    def _():
        send[pl.ds(at, value.shape[0]), :] = value


def split_halves(info, mine, send, starts, value):
    half, step = value.shape[0] // 2, value.shape[0] // 8
    first = info[0] == 0
    own = jnp.where(first, value[:half], value[half:]).astype(BF)
    other = jnp.where(first, value[half:], value[:half]).astype(BF)
    for n, at in enumerate(starts):
        mine[at : at + step, :] = own[n * step : n * step + step]
        send[at : at + step, :] = other[n * step : n * step + step]


def grads_kernel(
    info, a_own, a_other, do_ref, active_own, active_other, df_ref, h1_ref, du_ref, sums_ref, mine, send, *, quarter
):
    width = df_ref.shape[1]
    step = pl.program_id(0)
    part = active_own.shape[1]
    mine[0:part, :] = dot_tn(active_own[...], df_ref[...]).astype(BF)
    send[0:part, :] = dot_tn(active_other[...], df_ref[...]).astype(BF)
    up = dot_tn(h1_ref[...], du_ref[...])
    low, high = up[: width // 2].astype(BF), up[width // 2 :].astype(BF)
    at = part + width // 2
    mine[part:at, :] = jnp.where(info[0] == 0, low, high)
    send[part:at, :] = jnp.where(info[0] == 0, high, low)
    for out, a_ref in ((mine, a_own), (send, a_other)):
        both = dot_tn(a_ref[...], do_ref[...]).astype(BF)
        out[at : at + 64, :] = jnp.where(step % 2 == 0, both[:64], both[64:])
        out[at + 64 :, :] = jnp.zeros((quarter - at - 64, width), BF)

        @pl.when(step == 0)
        def _():
            out[at + 64 : at + 80, :] = sums_ref[...].astype(BF)


def ffn_grads(info, a, do, active, df, h1, du, sums, quarter):
    rows, width = df.shape
    units = active.shape[1]
    out = jax.ShapeDtypeStruct((4 * quarter, width), BF)
    columns = lambda n, index: pl.BlockSpec((rows, n), lambda j, info: (0, index(j, info[0])))
    return pl.pallas_call(
        functools.partial(grads_kernel, quarter=quarter),
        grid_spec=pltpu.PrefetchScalarGridSpec(
            num_scalar_prefetch=1,
            grid=(4,),
            in_specs=[
                columns(128, lambda j, core: core * 2 + j // 2),
                columns(128, lambda j, core: (1 - core) * 2 + j // 2),
                fixed(do.shape),
                columns(units // 8, lambda j, core: core * 4 + j),
                columns(units // 8, lambda j, core: (1 - core) * 4 + j),
                fixed(df.shape),
                fixed(h1.shape),
                columns(units // 4, lambda j, core: j),
                fixed(sums.shape),
            ],
            out_specs=[pl.BlockSpec((quarter, width), lambda j, *_: (j, 0))] * 2,
        ),
        out_shape=[out, out],
        compiler_params=params(),
        cost_estimate=lasting(10),
        name="ffn_grads",
    )(info, a, a, do, active, active, df, h1, du, sums)


def query_kernel(
    info, q_ref, kp_ref, k_ref, vp_ref, v_ref, log_ref, da_ref, exact_ref, dz1_ref, wq_a, wq_b,
    dq_ref, dh_ref, bias, keys, values, wq,
):
    rows, before = q_ref.shape[0], kp_ref.shape[0]
    width = dq_ref.shape[1]
    step = pl.program_id(0)
    chunks = chunks_of(keys.shape[0])
    make_bias = functools.partial(query_bias, info, rows, before)

    @pl.when(step == 0)
    def _():
        if len(chunks) == 1:
            bias[...] = make_bias(chunks[0])
        lay(info, wq, wq_a, wq_b)

    keys[0:before, :] = kp_ref[...]
    keys[before:, :] = k_ref[...]
    values[0:before, :] = vp_ref[...]
    values[before:, :] = v_ref[...]
    both = []
    for half in range(2):
        lanes = slice(64 * half, 64 * half + 64)
        delta = jnp.sum(da_ref[:, lanes].astype(F32) * exact_ref[:, lanes], axis=1, keepdims=True)
        dq = jnp.zeros((rows, 64), F32)
        for chunk in chunks:
            mask = bias[...] if len(chunks) == 1 else make_bias(chunk)
            scores = dot_nt(q_ref[:, lanes], keys[chunk, lanes]) + mask
            probs = jnp.exp(scores - log_ref[:, 64 * half : 64 * half + 1])
            dp = dot_nt(da_ref[:, lanes], values[chunk, lanes])
            ds = (probs * (dp - delta)).astype(BF)
            dq = dq + dot(ds, keys[chunk, lanes])
        both.append((dq * 0.125).astype(BF))
    pair = jnp.concatenate(both, axis=1)
    for n in range(width // 128):

        @pl.when(step == n)
        def _():
            dq_ref[:, 128 * n : 128 * n + 128] = pair

    @pl.when(step == pl.num_programs(0) - 1)
    def _():
        dh_ref[...] = dz1_ref[...] + dot_nt(dq_ref[...], wq[...])


def attend_query(info, q, kp, k, vp, v, logs, da, exact, dz1, wq):
    rows, width = q.shape
    before = kp.shape[0]
    cols = before + rows
    outs = [jax.ShapeDtypeStruct((rows, width), BF), jax.ShapeDtypeStruct((rows, width), F32)]
    return pl.pallas_call(
        query_kernel,
        grid_spec=pltpu.PrefetchScalarGridSpec(
            num_scalar_prefetch=1,
            grid=(width // 128,),
            in_specs=[paired(x.shape[0]) for x in (q, kp, k, vp, v, logs)]
            + [paired(rows), paired(rows), fixed(dz1.shape), fixed(wq[0].shape), fixed(wq[1].shape)],
            out_specs=[fixed(x.shape) for x in outs],
            scratch_shapes=[
                bias_scratch(rows, cols),
                pltpu.VMEM((cols, 128), BF),
                pltpu.VMEM((cols, 128), BF),
                pltpu.VMEM((width, width), BF),
            ],
        ),
        out_shape=outs,
        compiler_params=params(),
        cost_estimate=lasting(10),
        name="attend_query",
    )(info, q, kp, k, vp, v, logs, da, exact, dz1, *wq)


def last_kernel(info, *refs, reach, quarter, table):
    count = 2 * reach + 1
    q_parts, da_parts = refs[:count], refs[count : 2 * count]
    k_ref, v_ref, low_ref, dq_ref, dh_ref, wk_a, wk_b, wv_a, wv_b = refs[2 * count : 2 * count + 9]
    mine, send, dh_out, bias, queries, grads, dk_all, dv_all, wk, wv = refs[2 * count + 9 :]
    rows, width = low_ref.shape
    cols = queries.shape[0]
    step = pl.program_id(0)

    chunks = chunks_of(cols)
    make_bias = functools.partial(key_bias, info, rows)

    @pl.when(step == 0)
    def _():
        lay(info, wk, wk_a, wk_b)
        lay(info, wv, wv_a, wv_b)
        if len(chunks) == 1:
            bias[...] = make_bias(chunks[0])

    for n in range(count):
        queries[n * rows : n * rows + rows, :] = q_parts[n][...]
        grads[n * rows : n * rows + rows, :] = da_parts[n][0:rows, :]
    dks, dvs = [], []
    for half in range(2):
        lanes = slice(64 * half, 64 * half + 64)
        logs = jnp.concatenate([stat_row(x[rows : rows + 16, :], half, rows) for x in da_parts], axis=1)
        delta = jnp.concatenate([stat_row(x[rows + 16 : rows + 32, :], half, rows) for x in da_parts], axis=1)
        dk, dv = jnp.zeros((rows, 64), F32), jnp.zeros((rows, 64), F32)
        for chunk in chunks:
            mask = bias[...] if len(chunks) == 1 else make_bias(chunk)
            scores = dot_nt(k_ref[:, lanes], queries[chunk, lanes]) + mask
            probs = jnp.exp(scores - logs[:, chunk])
            dv = dv + dot(probs.astype(BF), grads[chunk, lanes])
            dp = dot_nt(v_ref[:, lanes], grads[chunk, lanes])
            ds = (probs * (dp - delta[:, chunk])).astype(BF)
            dk = dk + dot(ds, queries[chunk, lanes])
        dks.append(dk.astype(BF))
        dvs.append(dv.astype(BF))
    dk_pair, dv_pair = jnp.concatenate(dks, axis=1), jnp.concatenate(dvs, axis=1)
    for n in range(width // 128):

        @pl.when(step == n)
        def _():
            dk_all[:, 128 * n : 128 * n + 128] = dk_pair
            dv_all[:, 128 * n : 128 * n + 128] = dv_pair

    @pl.when(step == pl.num_programs(0) - 1)
    def _():
        dk, dv = dk_all[...], dv_all[...]
        step_rows = width // 8
        split_halves(info, mine, send, [n * quarter for n in range(4)], dot_tn(low_ref[...], dk))
        split_halves(info, mine, send, [n * quarter + step_rows for n in range(4)], dot_tn(low_ref[...], dv))
        dq = dq_ref[...]
        split_halves(info, mine, send, [n * quarter + 2 * step_rows for n in range(4)], dot_tn(low_ref[...], dq))
        dh = dh_ref[...] + dot_nt(dk, wk[...]) + dot_nt(dv, wv[...])
        dh_out[...] = dh.astype(BF)
        parts = []
        for _ in range(3):
            parts.append(dh.astype(BF))
            dh = dh - parts[-1].astype(F32)
        spots = info[1] + iota((1, rows), 1)
        place = spots - first_places(info, spots)
        base = 3 * step_rows
        fourth = table // 8
        for half in range(2):
            for n in range(4):
                hot = (place - (half * 4 + n) * fourth == iota((fourth, rows), 0)).astype(F32).astype(BF)
                total = dot(hot, parts[0]) + dot(hot, parts[1]) + dot(hot, parts[2])
                keep_or_send(info, half, mine, send, n * quarter + base, total)
        base += fourth
        spare = quarter - base
        for n in range(4):
            mine[n * quarter + base : (n + 1) * quarter, :] = jnp.zeros((spare, width), BF)
            send[n * quarter + base : (n + 1) * quarter, :] = jnp.zeros((spare, width), BF)
        total_v = jnp.sum(dv.astype(F32), axis=0, keepdims=True)
        total_q = jnp.sum(dq.astype(F32), axis=0, keepdims=True)
        total = jnp.where(iota((8, width), 0) == 0, total_v, total_q)
        mine[base : base + 8, :] = total.astype(BF)
        send[base : base + 8, :] = total.astype(BF)


def last(info, q_parts, da_parts, k, v, low, dq, dh, wk, wv, quarter, table):
    rows, width = k.shape
    count = len(q_parts)
    cols = count * rows
    outs = [
        jax.ShapeDtypeStruct((4 * quarter, width), BF),
        jax.ShapeDtypeStruct((4 * quarter, width), BF),
        jax.ShapeDtypeStruct((rows, width), BF),
    ]
    rest = (low, dq, dh, *wk, *wv)
    return pl.pallas_call(
        functools.partial(last_kernel, reach=count // 2, quarter=quarter, table=table),
        grid_spec=pltpu.PrefetchScalarGridSpec(
            num_scalar_prefetch=1,
            grid=(width // 128,),
            in_specs=[paired(x.shape[0]) for x in (*q_parts, *da_parts, k, v)] + [fixed(x.shape) for x in rest],
            out_specs=[fixed(x.shape) for x in outs],
            scratch_shapes=[
                bias_scratch(rows, cols),
                pltpu.VMEM((cols, 128), BF),
                pltpu.VMEM((cols, 128), BF),
                pltpu.VMEM((rows, width), BF),
                pltpu.VMEM((rows, width), BF),
                pltpu.VMEM((width, width), BF),
                pltpu.VMEM((width, width), BF),
            ],
        ),
        out_shape=outs,
        compiler_params=params(),
        cost_estimate=lasting(15),
        name="last",
    )(info, *q_parts, *da_parts, k, v, *rest)


def cut_kernel(digit_ref, *refs, terms, radix):
    ins, outs = refs[: terms * radix], refs[terms * radix :]
    for k in range(radix):
        total = ins[k * terms][...].astype(F32)
        for n in range(1, terms):
            total = total + ins[k * terms + n][...].astype(F32)
        outs[k][...] = total.astype(outs[k].dtype)


def cut(terms, digit, radix, kept):
    rows, width = terms[0].shape[0] // radix, terms[0].shape[1]
    subs = max(n for n in (1, 2, 3, 4) if rows % (8 * n) == 0 and rows // n >= 64 or n == 1)
    specs = [
        pl.BlockSpec((rows // subs, width), lambda n, d, k=k: ((d[0] ^ k) * subs + n, 0))
        for k in range(radix)
        for _ in terms
    ]
    return pl.pallas_call(
        functools.partial(cut_kernel, terms=len(terms), radix=radix),
        grid_spec=pltpu.PrefetchScalarGridSpec(
            num_scalar_prefetch=1,
            grid=(subs,),
            in_specs=specs,
            out_specs=[pl.BlockSpec((rows // subs, width), lambda n, d: (n, 0))] * radix,
        ),
        out_shape=[jax.ShapeDtypeStruct((rows, width), BF if k else kept) for k in range(radix)],
        compiler_params=params(),
        cost_estimate=lasting(3),
        name="cut",
    )(digit.reshape(1), *([*terms] * radix))


def place_kernel(digit_ref, *refs, radix, sizes):
    parts, outs = refs[:radix], refs[radix:]
    for k in range(radix):

        @pl.when(pl.program_id(0) == k)
        def _():
            at = 0
            for out, size in zip(outs, sizes):
                out[...] = parts[k][at : at + size, :].astype(out.dtype)
                at += size


def place(parts, digit, sizes, dtype, across):
    radix, (rows, width) = len(parts), parts[0].shape
    below = lambda k, d: (k ^ d[0], 0)
    beside = lambda k, d: (0, k ^ d[0])
    return pl.pallas_call(
        functools.partial(place_kernel, radix=radix, sizes=sizes),
        grid_spec=pltpu.PrefetchScalarGridSpec(
            num_scalar_prefetch=1,
            grid=(radix,),
            in_specs=[fixed((rows, width))] * radix,
            out_specs=[
                pl.BlockSpec((n, width), beside if i == across else below) for i, n in enumerate(sizes)
            ],
        ),
        out_shape=[
            jax.ShapeDtypeStruct((n, width * radix) if i == across else (n * radix, width), dtype)
            for i, n in enumerate(sizes)
        ],
        compiler_params=params(),
        cost_estimate=lasting(3),
        name="place",
    )(digit.reshape(1), *parts)


def exchange(pieces, here, stride, ranks):
    return [
        lax.ppermute(piece, "ctx", [(i, i ^ ((k + 1) * stride)) for i in range(ranks)])
        for k, piece in enumerate(pieces)
    ]


def stages_of(ranks):
    stages, stride = [], 1
    while stride < ranks:
        radix = 4 if (ranks // stride) % 4 == 0 else 2
        stages.append((stride, radix))
        stride *= radix
    return stages


def after(first, then):
    return lax.optimization_barrier((first, then))[1]


class Reduction:
    def __init__(self, here, ranks, sizes, across):
        self.here, self.ranks, self.sizes, self.across = here, ranks, sizes, across
        self.stages = stages_of(ranks)

    def digit(self, level):
        stride, radix = self.stages[level]
        return (self.here // stride) % radix

    def cut(self, terms, level):
        if level == len(self.stages):
            return cut(terms, self.here * 0, 1, BF)
        return cut(terms, self.digit(level), self.stages[level][1], F32)

    def scatter(self, pieces, level):
        return [pieces[0]] + exchange(pieces[1:], self.here, self.stages[level][0], self.ranks)

    def gather(self, held, level):
        stride, radix = self.stages[level]
        return [held] + exchange([held] * (radix - 1), self.here, stride, self.ranks)

    def place(self, parts, level):
        if level:
            return place(parts, self.digit(level), [parts[0].shape[0]], BF, None)[0]
        return place(parts, self.digit(0), self.sizes, F32, self.across)


def padded(rows, ranks):
    step = 2 * ranks
    return -(-rows // step) * step


def swap_core(x):
    return lax.ppermute(x, "fsdp", SWAP)


def by_core(core, own, other):
    return jnp.where(core == 0, jnp.stack([own, other]), jnp.stack([other, own]))


def next_chip(block, chips, step):
    pairs = [(i, i + 4) for i in range(4 * (chips - 1))]
    return lax.ppermute(block, "ctx", pairs if step > 0 else [(b, a) for a, b in pairs])


def send_window(own, reach, chips, step):
    far = [own]
    for k in range(1, reach + 1):
        if step > 0:
            pairs = [(i, i + 4 * k) for i in range(4 * (chips - k))]
        else:
            pairs = [(i + 4 * k, i) for i in range(4 * (chips - k))]
        far.append(lax.ppermute(own, "ctx", pairs))
    return far


def both_cores(far, core, step):
    near = core == (0 if step > 0 else 1)
    parts = []
    for k in range(len(far) - 1):
        parts += [swap_core(jnp.where(near, far[k], far[k + 1])), far[k + 1]]
    return parts


def shards(
    tokens,
    cotangent,
    lengths,
    deal_order,
    w_query,
    w_key,
    w_value,
    w_out,
    w_up,
    w_down,
    b_query,
    b_value,
    b_out,
    b_up,
    b_down,
    gain_one,
    shift_one,
    gain_two,
    shift_two,
    positions,
):
    block, width = tokens.shape[2], tokens.shape[3]
    ranks = lax.axis_size("ctx")
    chips = ranks // 4
    slot = block // ranks
    rows = 2 * block
    group = ranks * block
    longest = 2 * positions.shape[0]
    reach = longest // (2 * rows)
    here = lax.axis_index("ctx")
    core = lax.axis_index("fsdp")
    chip, micro, stream = here // 4, here % 2, (here // 2) % 2
    base = chip * (2 * rows) + core * rows

    index = lambda i, t: 2 * i + t
    straight, crossing = [], []
    for i in range(ranks):
        c, a, b = i // 4, (i // 2) % 2, i % 2
        for t in range(2):
            straight.append((index(i, t), index(4 * c + 2 * t + b, a)))
            crossing.append((index(i, t), index(4 * c + 2 * t + 1 - b, a)))
    even = here % 2 == 0
    same = jnp.where(even, tokens[0, 0], tokens[1, 0])
    cross = jnp.where(even, tokens[1, 0], tokens[0, 0])
    got_same = lax.ppermute(same, BOTH, straight)
    got_cross = lax.ppermute(cross, BOTH, crossing)
    first_half = jnp.where(micro == 0, got_same, got_cross)
    second_half = jnp.where(micro == 0, got_cross, got_same)
    own = jnp.concatenate([first_half, second_half], axis=0)

    table = jnp.concatenate([deal_order[:, 0], lengths[:, 0]], axis=1)
    table = jnp.where(micro == 0, table[0], table[1])
    table = jnp.where(stream == core, table, swap_core(table))
    order, lens = table[:group], table[group:]

    head = jnp.stack([core, base, jnp.int32(group)]).astype(jnp.int32)
    info = jnp.concatenate([head, lens])

    whole = lambda x: (x, swap_core(x))
    pos, wq, wk, wv = whole(positions), whole(w_query), whole(w_key), whole(w_value)
    vectors = [b_out, b_down, gain_one, shift_one, gain_two, shift_two, b_query, b_value, b_up]
    vec = whole(stack_vectors(vectors, width // 2))
    wo, wu, wd = whole(w_out), whole(w_up), whole(w_down)

    mine = order.reshape(ranks, ranks, slot)
    mine = lax.dynamic_slice_in_dim(mine, 4 * chip + 2 * core, 2, axis=1).reshape(rows) - base
    dealt = cotangent[:, 0].reshape(2, chips, 2, 2 * slot, width)
    keep = jnp.where(core == 0, dealt[:, :, 0], dealt[:, :, 1])
    give = jnp.where(core == 0, dealt[:, :, 1], dealt[:, :, 0])
    streams = by_core(core, keep, swap_core(give))
    sends = jnp.transpose(streams, (2, 0, 1, 3, 4)).reshape(rows, width)
    arrived = lax.all_to_all(sends, "ctx", split_axis=0, concat_axis=0, tiled=True)

    own = after(arrived, own)
    fixed_args = (pos, wk, wv, wq, vec)
    far = send_window(own, reach, chips, 1)
    k, v, q, hidden, low = project(info, [own], 0, True, *fixed_args)
    earlier = both_cores(far, core, 1)[::-1]
    before = len(earlier) * rows
    far_q = send_window(after(far[1:], q), reach, chips, -1)
    kp, vp = project(info, earlier, -before, False, *fixed_args)
    att, exact, logs, log_stats = attend_forward(info, q, kp, k, vp, v)
    exact = after(far_q[1:], exact)
    later_q = [q] + both_cores(far_q, core, -1)
    leaving, da_msg, dz1, active, df, h1, du, do, sums = feed_forward(
        info, att, exact, log_stats, hidden, arrived, mine, wo, wu, wd, vec
    )
    far_da = [da_msg, next_chip(da_msg, chips, -1)]

    half = width // 2
    units = 2 * b_up.shape[0]
    sizes = [units // 8, half, width // 8]
    quarter = padded(sum(sizes) + 16, ranks)
    sizes.append(quarter - sum(sizes))
    sizes_last = [width // 8, width // 8, width // 8, longest // 8]
    quarter_last = padded(sum(sizes_last) + 8, ranks)
    sizes_last.append(quarter_last - sum(sizes_last))
    one = Reduction(here, ranks, sizes, 1)
    two = Reduction(here, ranks, sizes_last, None)
    levels = len(one.stages)

    keep, give = ffn_grads(info, att, do, active, df, h1, du, sums, quarter)
    give = after(far_da[1], give)
    for _ in range(reach - 1):
        far_da.append(next_chip(far_da[-1], chips, -1))
    pieces = one.cut([keep, swap_core(give)], 0)
    exact = after(pieces, exact)
    terms = one.scatter(pieces, 0)
    dq, dh = attend_query(info, q, kp, k, vp, v, logs, da_msg, exact, dz1, wq)
    later_da = [da_msg] + both_cores(far_da, core, -1)
    keep, give, dh0_low = last(info, later_q, later_da, k, v, low, dq, dh, wk, wv, quarter_last, longest)

    terms_last = [keep, swap_core(give)]
    for level in range(levels):
        pieces_last = two.cut(terms_last, level)
        terms_last = two.scatter(pieces_last, level)
        pieces = one.cut(after(pieces_last, terms), level + 1)
        if level + 1 < levels:
            terms = one.scatter(pieces, level + 1)
        if level == 0:
            leaving, dh0_low = after(pieces_last, (leaving, dh0_low))
    held = pieces[0]
    (held_last,) = two.cut(terms_last, levels)
    for level in reversed(range(levels)):
        parts = one.gather(held, level)
        parts_last = two.gather(held_last, level)
        held = one.place(parts, level)
        held_last = two.place(parts_last, level)
    g_down, g_up, g_out, early = held
    g_key, g_value, g_query, g_pos, late = held_last
    shard = lambda x: lax.dynamic_slice_in_dim(x, core * half, half)
    gb_down, gg1, gs1, gg2, gs2, gb_out = (shard(early[n]) for n in range(6))
    gb_up = lax.dynamic_slice_in_dim(early[7:11].reshape(-1), core * (units // 2), units // 2)
    gb_value, gb_query = shard(late[0]), shard(late[1])

    landed = lax.all_to_all(leaving, "ctx", split_axis=0, concat_axis=0, tiled=True)
    landed = landed.reshape(chips, 2, 2, 2 * slot, width)
    keep = jnp.where(core == 0, landed[:, 0], landed[:, 1])
    give = jnp.where(core == 0, landed[:, 1], landed[:, 0])
    sides = by_core(core, keep, swap_core(give))
    output = jnp.transpose(sides, (2, 1, 0, 3, 4)).reshape(2, 1, block, width)

    back_same = jnp.where(micro == 0, dh0_low[:block], dh0_low[block:])
    back_cross = jnp.where(micro == 0, dh0_low[block:], dh0_low[:block])
    home_same = lax.ppermute(back_same, BOTH, [(b, a) for a, b in straight])
    home_cross = lax.ppermute(back_cross, BOTH, [(b, a) for a, b in crossing])
    grad_tokens = jnp.where(
        even, jnp.stack([home_same, home_cross]), jnp.stack([home_cross, home_same])
    )[:, None]

    return (
        output,
        grad_tokens,
        g_query,
        g_key,
        g_value,
        g_out,
        g_up,
        g_down,
        gb_query,
        gb_value,
        gb_out,
        gb_up,
        gb_down,
        gg1,
        gs1,
        gg2,
        gs2,
        g_pos,
    )


def solution(mesh):
    data = P(None, "fsdp", "ctx", None)
    groups = P(None, "fsdp", None)
    matrix, vector = P("fsdp", None), P("fsdp")
    return jax.shard_map(
        shards,
        mesh=mesh,
        in_specs=(data, data, groups, groups) + (matrix,) * 6 + (vector,) * 9 + (matrix,),
        out_specs=(data, data) + (matrix,) * 6 + (vector,) * 9 + (matrix,),
        check_vma=False,
    )
```

```python
import functools

import jax
import jax.numpy as jnp
from jax import lax
from jax.experimental import pallas as pl
from jax.experimental.pallas import tpu as pltpu
from jax.sharding import PartitionSpec as P

HEADS = 8
epsilon = 1e-05
gelu_coeff = 0.7978845608028654
cubic_coeff = 0.044715
BF = jnp.bfloat16
F32 = jnp.float32
SWAP = ((0, 1), (1, 0))
BOTH = ("ctx", "fsdp")
FAR = 1 << 30


def dot(a, b):
    return jnp.dot(a, b, preferred_element_type=F32)


def dot_tn(a, b):
    return lax.dot_general(a, b, (((0,), (0,)), ((), ())), preferred_element_type=F32)


def dot_nt(a, b):
    return lax.dot_general(a, b, (((1,), (1,)), ((), ())), preferred_element_type=F32)


def gelu_parts(u):
    inner = gelu_coeff * (u + cubic_coeff * u * u * u)
    bent = jnp.tanh(inner)
    value = 0.5 * u * (1.0 + bent)
    slope = 0.5 * (1.0 + bent) + 0.5 * u * (1.0 - bent * bent) * gelu_coeff * (
        1.0 + 3.0 * cubic_coeff * u * u
    )
    return value, slope


def normalize(z):
    center = z - jnp.mean(z, axis=-1, keepdims=True)
    inv = lax.rsqrt(jnp.mean(center * center, axis=-1, keepdims=True) + epsilon)
    return center * inv, inv


def normalize_back(t, normed, inv):
    return inv * (
        t
        - jnp.mean(t, axis=-1, keepdims=True)
        - normed * jnp.mean(t * normed, axis=-1, keepdims=True)
    )


def first_places(info, spots):
    first, end = jnp.zeros_like(spots), 0
    for n in range(3, info.shape[0]):
        end = end + info[n]
        first = first + jnp.where(spots >= end, info[n], 0)
    return first


def lay(info, whole, own, other):
    n = own.shape[0]
    mine = info[0] == 0
    whole[0:n, :] = jnp.where(mine, own[...], other[...])
    whole[n : 2 * n, :] = jnp.where(mine, other[...], own[...])


def full_row(info, own, other, at, count=1):
    mine = info[0] == 0
    rows = [x[at + n : at + n + 1, :] for x in (own, other) for n in range(count)]
    first = [jnp.where(mine, rows[n], rows[count + n]) for n in range(count)]
    second = [jnp.where(mine, rows[count + n], rows[n]) for n in range(count)]
    return jnp.concatenate(first + second, axis=1)


def stack_vectors(vectors, width):
    row, at = iota((16, width), 0), 0
    table = jnp.zeros((16, width), BF)
    for x in vectors:
        for n in range(x.shape[0] // width):
            part = x[n * width : n * width + width]
            table = jnp.where(row == at, part[None, :], table)
            at += 1
    return table.astype(F32)


def iota(shape, axis):
    return lax.broadcasted_iota(jnp.int32, shape, axis)


def params(cols=0):
    return pltpu.CompilerParams(vmem_limit_bytes=(32 if cols <= 2048 else 56) * 1024 * 1024)


def lasting(us):
    return pl.CostEstimate(flops=us, transcendentals=0, bytes_accessed=us)


def fixed(shape):
    return pl.BlockSpec(shape, lambda *_: (0,) * len(shape), pipeline_mode=pl.Buffered(1))


def paired(rows):
    return pl.BlockSpec((rows, 128), lambda p, *_: (0, p))


def project_kernel(info, *refs, blocks, offset, own):
    toks = refs[:blocks]
    pos_a, pos_b, wk_a, wk_b, wv_a, wv_b, wq_a, wq_b, vec_a, vec_b = refs[blocks : blocks + 10]
    outs = refs[blocks + 10 :]
    k_ref, v_ref = outs[:2]
    wk, wv, wq, tok = outs[-4:]
    step = pl.program_id(0)
    rows = tok.shape[0]

    @pl.when(step == 0)
    def _():
        lay(info, wk, wk_a, wk_b)
        lay(info, wv, wv_a, wv_b)
        if own:
            lay(info, wq, wq_a, wq_b)

    for n in range(blocks):

        @pl.when(step == n)
        def _():
            tok[...] = toks[n][...]

    spots = info[1] + offset + step * rows + iota((rows, 1), 0)
    place = spots - first_places(info, spots)
    hidden = tok[...].astype(F32)
    half = pos_a.shape[0]
    chunk = min(half, 512)
    for part, begin in ((pos_a, info[0] * half), (pos_b, (1 - info[0]) * half)):
        for at in range(0, half, chunk):
            hot = (place - begin - at == iota((rows, chunk), 1)).astype(F32).astype(BF)
            hidden = hidden + dot(hot, part[at : at + chunk, :])
    low = hidden.astype(BF)
    k_ref[...] = dot(low, wk[...]).astype(BF)
    v_ref[...] = (dot(low, wv[...]) + full_row(info, vec_a, vec_b, 7)).astype(BF)
    if own:
        q_ref, hidden_ref, low_ref = outs[2:5]
        q_ref[...] = ((dot(low, wq[...]) + full_row(info, vec_a, vec_b, 6)).astype(BF).astype(F32) * 0.125).astype(BF)
        hidden_ref[...] = hidden
        low_ref[...] = low


def project(info, toks, offset, own, pos, wk, wv, wq, vec):
    rows, width = toks[0].shape
    blocks = len(toks)
    tall = pl.BlockSpec((rows, width), lambda n, *_: (n, 0))
    flat = jax.ShapeDtypeStruct((rows * blocks, width), BF)
    square = pltpu.VMEM((width, width), BF)
    args = (*toks, *pos, *wk, *wv, *wq, *vec)
    return pl.pallas_call(
        functools.partial(project_kernel, blocks=blocks, offset=offset, own=own),
        grid_spec=pltpu.PrefetchScalarGridSpec(
            num_scalar_prefetch=1,
            grid=(blocks,),
            in_specs=[fixed(x.shape) for x in args],
            out_specs=[tall] * (5 if own else 2),
            scratch_shapes=[square, square, square, pltpu.VMEM((rows, width), BF)],
        ),
        out_shape=[flat] * 3 + [jax.ShapeDtypeStruct((rows, width), F32), flat] if own else [flat] * 2,
        compiler_params=params(pos[0].shape[0] + blocks * rows),
        cost_estimate=lasting(2 * blocks + 2),
        name="project",
    )(info, *args)


def stat_rows(table):
    high = table.astype(BF).astype(F32)
    middle = (table - high).astype(BF).astype(F32)
    low = table - high - middle
    count = table.shape[1] // 128
    rows = [
        part[half : half + 1, 128 * n : 128 * n + 128]
        for part in (high, middle, low)
        for half in range(2)
        for n in range(count)
    ]
    rows.append(jnp.zeros((16 - len(rows), 128), F32))
    return jnp.concatenate(rows, axis=0).astype(BF)


def stat_row(rows16, half, queries):
    count = queries // 128
    wide = rows16.astype(F32)
    total = wide[0 : 2 * count] + wide[2 * count : 4 * count] + wide[4 * count : 6 * count]
    return jnp.concatenate([total[half * count + n : half * count + n + 1] for n in range(count)], axis=1)


def chunks_of(cols):
    step = cols if cols <= 2048 else 768
    return [slice(at, min(at + step, cols)) for at in range(0, cols, step)]


def bias_scratch(rows, cols):
    return pltpu.VMEM((rows, cols) if len(chunks_of(cols)) == 1 else (8, 128), F32)


def query_bias(info, rows, before, chunk):
    spots = info[1] + iota((rows, 1), 0)
    first = first_places(info, spots) - (info[1] - before)
    last = iota((rows, 1), 0) + before
    col = iota((rows, chunk.stop - chunk.start), 1) + chunk.start
    return jnp.where((col >= first) & (col <= last), 0.0, -1e30)


def key_bias(info, rows, chunk):
    spots = info[1] + chunk.start + iota((1, chunk.stop - chunk.start), 1)
    first = jnp.where(spots < info[2], first_places(info, spots) - info[1], FAR)
    shape = (rows, chunk.stop - chunk.start)
    row = iota(shape, 0)
    return jnp.where((row >= first) & (row <= iota(shape, 1) + chunk.start), 0.0, -1e30)


def forward_kernel(info, q_ref, kp_ref, k_ref, vp_ref, v_ref, a_ref, exact_ref, log_ref, stat_ref, bias, keys, values):
    rows, before = q_ref.shape[0], kp_ref.shape[0]

    chunks = chunks_of(keys.shape[0])
    make_bias = functools.partial(query_bias, info, rows, before)

    @pl.when(pl.program_id(0) == 0)
    def _():
        if len(chunks) == 1:
            bias[...] = make_bias(chunks[0])

    keys[0:before, :] = kp_ref[...]
    keys[before:, :] = k_ref[...]
    values[0:before, :] = vp_ref[...]
    values[before:, :] = v_ref[...]
    logs = []
    for half in range(2):
        lanes = slice(64 * half, 64 * half + 64)


        def scores_of(chunk):
            mask = bias[...] if len(chunks) == 1 else make_bias(chunk)
            return dot_nt(q_ref[:, lanes], keys[chunk, lanes]) + mask

        if len(chunks) == 1:
            scores = scores_of(chunks[0])
            top = jnp.max(scores, axis=1, keepdims=True)
            raised = jnp.exp(scores - top)
            total = jnp.sum(raised, axis=1, keepdims=True)
            probs = raised * (1.0 / total)
            low = probs.astype(BF)
            rest = (probs - low.astype(F32)).astype(BF)
            attended = dot(low, values[:, lanes])
            exact = attended + dot(rest, values[:, lanes])
        else:
            top = jnp.full((rows, 1), -1e30, F32)
            for chunk in chunks:
                top = jnp.maximum(top, jnp.max(scores_of(chunk), axis=1, keepdims=True))
            total = jnp.zeros((rows, 1), F32)
            for chunk in chunks:
                total = total + jnp.sum(jnp.exp(scores_of(chunk) - top), axis=1, keepdims=True)
            attended, exact = jnp.zeros((rows, 64), F32), jnp.zeros((rows, 64), F32)
            for chunk in chunks:
                probs = jnp.exp(scores_of(chunk) - top) * (1.0 / total)
                low = probs.astype(BF)
                rest = (probs - low.astype(F32)).astype(BF)
                attended = attended + dot(low, values[chunk, lanes])
                exact = exact + dot(rest, values[chunk, lanes])
            exact = exact + attended
        a_ref[:, lanes] = attended.astype(BF)
        exact_ref[:, lanes] = exact
        logs.append(jnp.broadcast_to(top + jnp.log(total), (rows, 64)))
    wide = jnp.concatenate(logs, axis=1)
    log_ref[...] = wide
    turned = wide.T
    stat_ref[...] = stat_rows(jnp.concatenate([turned[0:1], turned[64:65]], axis=0))


def attend_forward(info, q, kp, k, vp, v):
    rows, width = q.shape
    before = kp.shape[0]
    cols = before + rows
    return pl.pallas_call(
        forward_kernel,
        grid_spec=pltpu.PrefetchScalarGridSpec(
            num_scalar_prefetch=1,
            grid=(width // 128,),
            in_specs=[paired(x.shape[0]) for x in (q, kp, k, vp, v)],
            out_specs=[paired(rows), paired(rows), paired(rows), paired(16)],
            scratch_shapes=[
                bias_scratch(rows, cols),
                pltpu.VMEM((cols, 128), BF),
                pltpu.VMEM((cols, 128), BF),
            ],
        ),
        out_shape=[
            jax.ShapeDtypeStruct((rows, width), BF),
            jax.ShapeDtypeStruct((rows, width), F32),
            jax.ShapeDtypeStruct((rows, width), F32),
            jax.ShapeDtypeStruct((16, width), BF),
        ],
        compiler_params=params(cols),
        cost_estimate=lasting(12),
        name="attend_forward",
    )(info, q, kp, k, vp, v)


def ffn_kernel(
    info, a_ref, exact_ref, stat_ref, hidden_ref, arrived_ref, row_ref, col_ref, wo_a, wo_b, wu_a, wu_b, wd_a, wd_b, vec_a, vec_b,
    leaving_ref, msg_ref, dz1_ref, active_ref, df_ref, h1_ref, du_ref, do_ref, sums_ref,
    wo, wu, wd, slopes, stats,
):
    lay(info, wo, wo_a, wo_b)
    lay(info, wu, wu_a, wu_b)
    lay(info, wd, wd_a, wd_b)
    rows, width = hidden_ref.shape
    hidden_units = wu.shape[1]
    bo, bd, g1, s1, g2, s2 = (full_row(info, vec_a, vec_b, n) for n in range(6))
    bu = full_row(info, vec_a, vec_b, 8, hidden_units // width)
    pick = (iota((rows, rows), 0) == row_ref[...]).astype(F32).astype(BF)
    pick_back = (col_ref[...] == iota((rows, rows), 1)).astype(F32).astype(BF)
    dy = dot(pick, arrived_ref[...])

    n1, r1 = normalize(hidden_ref[...] + dot(a_ref[...], wo[...]) + bo)
    h1 = n1 * g1 + s1
    h1_low = h1.astype(BF)
    h1_ref[...] = h1_low
    z2 = h1 + bd
    for at in range(0, hidden_units, width):
        block = slice(at, at + width)
        value, slope = gelu_parts(dot(h1_low, wu[:, block]) + bu[:, block])
        slopes[:, block] = slope
        low = value.astype(BF)
        active_ref[:, block] = low
        z2 = z2 + dot(low, wd[block, :])
    n2, r2 = normalize(z2)
    leaving_ref[...] = dot(pick_back, (n2 * g2 + s2).astype(BF)).astype(BF)

    def add(x):
        return jnp.sum(x, axis=0, keepdims=True)

    dz2 = normalize_back(dy * g2, n2, r2)
    df = dz2.astype(BF)
    df_ref[...] = df
    sums_ref[0:1, :] = add(df.astype(F32))
    sums_ref[3:4, :] = add(dy * n2)
    sums_ref[4:5, :] = add(dy)
    dh1 = dz2
    for at in range(0, hidden_units, width):
        block = slice(at, at + width)
        du = (dot_nt(df, wd[block, :]) * slopes[:, block]).astype(BF)
        du_ref[:, block] = du
        n = 7 + at // width
        sums_ref[n : n + 1, :] = add(du.astype(F32))
        dh1 = dh1 + dot_nt(du, wu[:, block])
    dz1 = normalize_back(dh1 * g1, n1, r1)
    dz1_ref[...] = dz1
    sums_ref[1:2, :] = add(dh1 * n1)
    sums_ref[2:3, :] = add(dh1)
    do = dz1.astype(BF)
    do_ref[...] = do
    sums_ref[5:6, :] = add(do.astype(F32))
    sums_ref[6:7, :] = jnp.zeros((1, width), F32)
    sums_ref[11:16, :] = jnp.zeros((5, width), F32)
    da = dot_nt(do, wo[...]).astype(BF)
    msg_ref[0:rows, :] = da
    terms = da.astype(F32) * exact_ref[...]
    head = iota((HEADS, width), 0)
    lane = iota((HEADS, width), 1) // (width // HEADS)
    ones = (head == lane).astype(F32).astype(BF)
    delta = jnp.zeros((HEADS, rows), F32)
    for _ in range(3):
        part = terms.astype(BF)
        terms = terms - part.astype(F32)
        delta = delta + dot_nt(ones, part)
    for p in range(HEADS // 2):
        stats[:, 128 * p : 128 * p + 128] = stat_rows(delta[2 * p : 2 * p + 2, :])
    msg_ref[rows : rows + 16, :] = stat_ref[...]
    msg_ref[rows + 16 : rows + 32, :] = stats[...]


def feed_forward(info, a, exact, log_stats, hidden, arrived, mine, wo, wu, wd, vec):
    rows, width = hidden.shape
    units = wu[0].shape[1]
    args = (a, exact, log_stats, hidden, arrived, mine.reshape(1, rows), mine.reshape(rows, 1), *wo, *wu, *wd, *vec)
    low = jax.ShapeDtypeStruct((rows, width), BF)
    tall = jax.ShapeDtypeStruct((rows, units), BF)
    outs = [
        low,
        jax.ShapeDtypeStruct((rows + 32, width), BF),
        jax.ShapeDtypeStruct((rows, width), F32),
        tall,
        low,
        low,
        tall,
        low,
        jax.ShapeDtypeStruct((16, width), F32),
    ]
    return pl.pallas_call(
        ffn_kernel,
        grid_spec=pltpu.PrefetchScalarGridSpec(
            num_scalar_prefetch=1,
            grid=(1,),
            in_specs=[fixed(x.shape) for x in args],
            out_specs=[fixed(x.shape) for x in outs],
            scratch_shapes=[
                pltpu.VMEM((width, width), BF),
                pltpu.VMEM((width, units), BF),
                pltpu.VMEM((units, width), BF),
                pltpu.VMEM((rows, units), F32),
                pltpu.VMEM((16, width), BF),
            ],
        ),
        out_shape=outs,
        compiler_params=params(),
        cost_estimate=lasting(10),
        name="feed_forward",
    )(info, *args)


def keep_or_send(info, half, mine, send, at, value):
    at, value = pl.multiple_of(at, 8), value.astype(BF)

    @pl.when(info[0] == half)
    def _():
        mine[pl.ds(at, value.shape[0]), :] = value

    @pl.when(info[0] != half)
    def _():
        send[pl.ds(at, value.shape[0]), :] = value


def split_halves(info, mine, send, starts, value):
    half, step = value.shape[0] // 2, value.shape[0] // 8
    first = info[0] == 0
    own = jnp.where(first, value[:half], value[half:]).astype(BF)
    other = jnp.where(first, value[half:], value[:half]).astype(BF)
    for n, at in enumerate(starts):
        mine[at : at + step, :] = own[n * step : n * step + step]
        send[at : at + step, :] = other[n * step : n * step + step]


def grads_kernel(
    info, a_own, a_other, do_ref, active_own, active_other, df_ref, h1_ref, du_ref, sums_ref, mine, send, *, quarter
):
    width = df_ref.shape[1]
    step = pl.program_id(0)
    part = active_own.shape[1]
    mine[0:part, :] = dot_tn(active_own[...], df_ref[...]).astype(BF)
    send[0:part, :] = dot_tn(active_other[...], df_ref[...]).astype(BF)
    up = dot_tn(h1_ref[...], du_ref[...])
    low, high = up[: width // 2].astype(BF), up[width // 2 :].astype(BF)
    at = part + width // 2
    mine[part:at, :] = jnp.where(info[0] == 0, low, high)
    send[part:at, :] = jnp.where(info[0] == 0, high, low)
    for out, a_ref in ((mine, a_own), (send, a_other)):
        both = dot_tn(a_ref[...], do_ref[...]).astype(BF)
        out[at : at + 64, :] = jnp.where(step % 2 == 0, both[:64], both[64:])
        out[at + 64 :, :] = jnp.zeros((quarter - at - 64, width), BF)

        @pl.when(step == 0)
        def _():
            out[at + 64 : at + 80, :] = sums_ref[...].astype(BF)


def ffn_grads(info, a, do, active, df, h1, du, sums, quarter):
    rows, width = df.shape
    units = active.shape[1]
    out = jax.ShapeDtypeStruct((4 * quarter, width), BF)
    columns = lambda n, index: pl.BlockSpec((rows, n), lambda j, info: (0, index(j, info[0])))
    return pl.pallas_call(
        functools.partial(grads_kernel, quarter=quarter),
        grid_spec=pltpu.PrefetchScalarGridSpec(
            num_scalar_prefetch=1,
            grid=(4,),
            in_specs=[
                columns(128, lambda j, core: core * 2 + j // 2),
                columns(128, lambda j, core: (1 - core) * 2 + j // 2),
                fixed(do.shape),
                columns(units // 8, lambda j, core: core * 4 + j),
                columns(units // 8, lambda j, core: (1 - core) * 4 + j),
                fixed(df.shape),
                fixed(h1.shape),
                columns(units // 4, lambda j, core: j),
                fixed(sums.shape),
            ],
            out_specs=[pl.BlockSpec((quarter, width), lambda j, *_: (j, 0))] * 2,
        ),
        out_shape=[out, out],
        compiler_params=params(),
        cost_estimate=lasting(10),
        name="ffn_grads",
    )(info, a, a, do, active, active, df, h1, du, sums)


def query_kernel(
    info, q_ref, kp_ref, k_ref, vp_ref, v_ref, log_ref, da_ref, exact_ref, dz1_ref, wq_a, wq_b,
    dq_ref, dh_ref, bias, keys, values, wq,
):
    rows, before = q_ref.shape[0], kp_ref.shape[0]
    width = dq_ref.shape[1]
    step = pl.program_id(0)
    chunks = chunks_of(keys.shape[0])
    make_bias = functools.partial(query_bias, info, rows, before)

    @pl.when(step == 0)
    def _():
        if len(chunks) == 1:
            bias[...] = make_bias(chunks[0])
        lay(info, wq, wq_a, wq_b)

    keys[0:before, :] = kp_ref[...]
    keys[before:, :] = k_ref[...]
    values[0:before, :] = vp_ref[...]
    values[before:, :] = v_ref[...]
    both = []
    for half in range(2):
        lanes = slice(64 * half, 64 * half + 64)
        delta = jnp.sum(da_ref[:, lanes].astype(F32) * exact_ref[:, lanes], axis=1, keepdims=True)
        dq = jnp.zeros((rows, 64), F32)
        for chunk in chunks:
            mask = bias[...] if len(chunks) == 1 else make_bias(chunk)
            scores = dot_nt(q_ref[:, lanes], keys[chunk, lanes]) + mask
            probs = jnp.exp(scores - log_ref[:, 64 * half : 64 * half + 1])
            dp = dot_nt(da_ref[:, lanes], values[chunk, lanes])
            ds = (probs * (dp - delta)).astype(BF)
            dq = dq + dot(ds, keys[chunk, lanes])
        both.append((dq * 0.125).astype(BF))
    pair = jnp.concatenate(both, axis=1)
    for n in range(width // 128):

        @pl.when(step == n)
        def _():
            dq_ref[:, 128 * n : 128 * n + 128] = pair

    @pl.when(step == pl.num_programs(0) - 1)
    def _():
        dh_ref[...] = dz1_ref[...] + dot_nt(dq_ref[...], wq[...])


def attend_query(info, q, kp, k, vp, v, logs, da, exact, dz1, wq):
    rows, width = q.shape
    before = kp.shape[0]
    cols = before + rows
    outs = [jax.ShapeDtypeStruct((rows, width), BF), jax.ShapeDtypeStruct((rows, width), F32)]
    return pl.pallas_call(
        query_kernel,
        grid_spec=pltpu.PrefetchScalarGridSpec(
            num_scalar_prefetch=1,
            grid=(width // 128,),
            in_specs=[paired(x.shape[0]) for x in (q, kp, k, vp, v, logs)]
            + [paired(rows), paired(rows), fixed(dz1.shape), fixed(wq[0].shape), fixed(wq[1].shape)],
            out_specs=[fixed(x.shape) for x in outs],
            scratch_shapes=[
                bias_scratch(rows, cols),
                pltpu.VMEM((cols, 128), BF),
                pltpu.VMEM((cols, 128), BF),
                pltpu.VMEM((width, width), BF),
            ],
        ),
        out_shape=outs,
        compiler_params=params(cols),
        cost_estimate=lasting(10),
        name="attend_query",
    )(info, q, kp, k, vp, v, logs, da, exact, dz1, *wq)


def last_kernel(info, *refs, reach, quarter, table):
    count = 2 * reach + 1
    q_parts, da_parts = refs[:count], refs[count : 2 * count]
    k_ref, v_ref, low_ref, dq_ref, dh_ref, wk_a, wk_b, wv_a, wv_b = refs[2 * count : 2 * count + 9]
    mine, send, dh_out, bias, queries, grads, dk_all, dv_all, wk, wv = refs[2 * count + 9 :]
    rows, width = low_ref.shape
    cols = queries.shape[0]
    step = pl.program_id(0)

    chunks = chunks_of(cols)
    make_bias = functools.partial(key_bias, info, rows)

    @pl.when(step == 0)
    def _():
        lay(info, wk, wk_a, wk_b)
        lay(info, wv, wv_a, wv_b)
        if len(chunks) == 1:
            bias[...] = make_bias(chunks[0])

    for n in range(count):
        queries[n * rows : n * rows + rows, :] = q_parts[n][...]
        grads[n * rows : n * rows + rows, :] = da_parts[n][0:rows, :]
    dks, dvs = [], []
    for half in range(2):
        lanes = slice(64 * half, 64 * half + 64)
        logs = jnp.concatenate([stat_row(x[rows : rows + 16, :], half, rows) for x in da_parts], axis=1)
        delta = jnp.concatenate([stat_row(x[rows + 16 : rows + 32, :], half, rows) for x in da_parts], axis=1)
        dk, dv = jnp.zeros((rows, 64), F32), jnp.zeros((rows, 64), F32)
        for chunk in chunks:
            mask = bias[...] if len(chunks) == 1 else make_bias(chunk)
            scores = dot_nt(k_ref[:, lanes], queries[chunk, lanes]) + mask
            probs = jnp.exp(scores - logs[:, chunk])
            dv = dv + dot(probs.astype(BF), grads[chunk, lanes])
            dp = dot_nt(v_ref[:, lanes], grads[chunk, lanes])
            ds = (probs * (dp - delta[:, chunk])).astype(BF)
            dk = dk + dot(ds, queries[chunk, lanes])
        dks.append(dk.astype(BF))
        dvs.append(dv.astype(BF))
    dk_pair, dv_pair = jnp.concatenate(dks, axis=1), jnp.concatenate(dvs, axis=1)
    for n in range(width // 128):

        @pl.when(step == n)
        def _():
            dk_all[:, 128 * n : 128 * n + 128] = dk_pair
            dv_all[:, 128 * n : 128 * n + 128] = dv_pair

    @pl.when(step == pl.num_programs(0) - 1)
    def _():
        dk, dv = dk_all[...], dv_all[...]
        step_rows = width // 8
        split_halves(info, mine, send, [n * quarter for n in range(4)], dot_tn(low_ref[...], dk))
        split_halves(info, mine, send, [n * quarter + step_rows for n in range(4)], dot_tn(low_ref[...], dv))
        dq = dq_ref[...]
        split_halves(info, mine, send, [n * quarter + 2 * step_rows for n in range(4)], dot_tn(low_ref[...], dq))
        dh = dh_ref[...] + dot_nt(dk, wk[...]) + dot_nt(dv, wv[...])
        dh_out[...] = dh.astype(BF)
        parts = []
        for _ in range(3):
            parts.append(dh.astype(BF))
            dh = dh - parts[-1].astype(F32)
        spots = info[1] + iota((1, rows), 1)
        place = spots - first_places(info, spots)
        base = 3 * step_rows
        fourth = table // 8
        for half in range(2):
            for n in range(4):
                hot = (place - (half * 4 + n) * fourth == iota((fourth, rows), 0)).astype(F32).astype(BF)
                total = dot(hot, parts[0]) + dot(hot, parts[1]) + dot(hot, parts[2])
                keep_or_send(info, half, mine, send, n * quarter + base, total)
        base += fourth
        spare = quarter - base
        for n in range(4):
            mine[n * quarter + base : (n + 1) * quarter, :] = jnp.zeros((spare, width), BF)
            send[n * quarter + base : (n + 1) * quarter, :] = jnp.zeros((spare, width), BF)
        total_v = jnp.sum(dv.astype(F32), axis=0, keepdims=True)
        total_q = jnp.sum(dq.astype(F32), axis=0, keepdims=True)
        total = jnp.where(iota((8, width), 0) == 0, total_v, total_q)
        mine[base : base + 8, :] = total.astype(BF)
        send[base : base + 8, :] = total.astype(BF)


def last(info, q_parts, da_parts, k, v, low, dq, dh, wk, wv, quarter, table):
    rows, width = k.shape
    count = len(q_parts)
    cols = count * rows
    outs = [
        jax.ShapeDtypeStruct((4 * quarter, width), BF),
        jax.ShapeDtypeStruct((4 * quarter, width), BF),
        jax.ShapeDtypeStruct((rows, width), BF),
    ]
    rest = (low, dq, dh, *wk, *wv)
    return pl.pallas_call(
        functools.partial(last_kernel, reach=count // 2, quarter=quarter, table=table),
        grid_spec=pltpu.PrefetchScalarGridSpec(
            num_scalar_prefetch=1,
            grid=(width // 128,),
            in_specs=[paired(x.shape[0]) for x in (*q_parts, *da_parts, k, v)] + [fixed(x.shape) for x in rest],
            out_specs=[fixed(x.shape) for x in outs],
            scratch_shapes=[
                bias_scratch(rows, cols),
                pltpu.VMEM((cols, 128), BF),
                pltpu.VMEM((cols, 128), BF),
                pltpu.VMEM((rows, width), BF),
                pltpu.VMEM((rows, width), BF),
                pltpu.VMEM((width, width), BF),
                pltpu.VMEM((width, width), BF),
            ],
        ),
        out_shape=outs,
        compiler_params=params(cols),
        cost_estimate=lasting(15),
        name="last",
    )(info, *q_parts, *da_parts, k, v, *rest)


def cut_kernel(digit_ref, *refs, terms, radix):
    ins, outs = refs[: terms * radix], refs[terms * radix :]
    for k in range(radix):
        total = ins[k * terms][...].astype(F32)
        for n in range(1, terms):
            total = total + ins[k * terms + n][...].astype(F32)
        outs[k][...] = total.astype(outs[k].dtype)


def cut(terms, digit, radix, kept):
    rows, width = terms[0].shape[0] // radix, terms[0].shape[1]
    subs = max(n for n in (1, 2, 3, 4) if rows % (8 * n) == 0 and rows // n >= 64 or n == 1)
    specs = [
        pl.BlockSpec((rows // subs, width), lambda n, d, k=k: ((d[0] ^ k) * subs + n, 0))
        for k in range(radix)
        for _ in terms
    ]
    return pl.pallas_call(
        functools.partial(cut_kernel, terms=len(terms), radix=radix),
        grid_spec=pltpu.PrefetchScalarGridSpec(
            num_scalar_prefetch=1,
            grid=(subs,),
            in_specs=specs,
            out_specs=[pl.BlockSpec((rows // subs, width), lambda n, d: (n, 0))] * radix,
        ),
        out_shape=[jax.ShapeDtypeStruct((rows, width), BF if k else kept) for k in range(radix)],
        compiler_params=params(),
        cost_estimate=lasting(3),
        name="cut",
    )(digit.reshape(1), *([*terms] * radix))


def place_kernel(digit_ref, *refs, radix, sizes):
    parts, outs = refs[:radix], refs[radix:]
    for k in range(radix):

        @pl.when(pl.program_id(0) == k)
        def _():
            at = 0
            for out, size in zip(outs, sizes):
                out[...] = parts[k][at : at + size, :].astype(out.dtype)
                at += size


def place(parts, digit, sizes, dtype, across):
    radix, (rows, width) = len(parts), parts[0].shape
    below = lambda k, d: (k ^ d[0], 0)
    beside = lambda k, d: (0, k ^ d[0])
    return pl.pallas_call(
        functools.partial(place_kernel, radix=radix, sizes=sizes),
        grid_spec=pltpu.PrefetchScalarGridSpec(
            num_scalar_prefetch=1,
            grid=(radix,),
            in_specs=[fixed((rows, width))] * radix,
            out_specs=[
                pl.BlockSpec((n, width), beside if i == across else below) for i, n in enumerate(sizes)
            ],
        ),
        out_shape=[
            jax.ShapeDtypeStruct((n, width * radix) if i == across else (n * radix, width), dtype)
            for i, n in enumerate(sizes)
        ],
        compiler_params=params(),
        cost_estimate=lasting(3),
        name="place",
    )(digit.reshape(1), *parts)


def exchange(pieces, here, stride, ranks):
    return [
        lax.ppermute(piece, "ctx", [(i, i ^ ((k + 1) * stride)) for i in range(ranks)])
        for k, piece in enumerate(pieces)
    ]


def stages_of(ranks):
    stages, stride = [], 1
    while stride < ranks:
        radix = 4 if (ranks // stride) % 4 == 0 else 2
        stages.append((stride, radix))
        stride *= radix
    return stages


def after(first, then):
    return lax.optimization_barrier((first, then))[1]


class Reduction:
    def __init__(self, here, ranks, sizes, across):
        self.here, self.ranks, self.sizes, self.across = here, ranks, sizes, across
        self.stages = stages_of(ranks)

    def digit(self, level):
        stride, radix = self.stages[level]
        return (self.here // stride) % radix

    def cut(self, terms, level):
        if level == len(self.stages):
            return cut(terms, self.here * 0, 1, BF)
        return cut(terms, self.digit(level), self.stages[level][1], F32)

    def scatter(self, pieces, level):
        return [pieces[0]] + exchange(pieces[1:], self.here, self.stages[level][0], self.ranks)

    def gather(self, held, level):
        stride, radix = self.stages[level]
        return [held] + exchange([held] * (radix - 1), self.here, stride, self.ranks)

    def place(self, parts, level):
        if level:
            return place(parts, self.digit(level), [parts[0].shape[0]], BF, None)[0]
        return place(parts, self.digit(0), self.sizes, F32, self.across)


def padded(rows, ranks):
    step = 2 * ranks
    return -(-rows // step) * step


def swap_core(x):
    return lax.ppermute(x, "fsdp", SWAP)


def by_core(core, own, other):
    return jnp.where(core == 0, jnp.stack([own, other]), jnp.stack([other, own]))


def next_chip(block, chips, step):
    pairs = [(i, i + 4) for i in range(4 * (chips - 1))]
    return lax.ppermute(block, "ctx", pairs if step > 0 else [(b, a) for a, b in pairs])


def send_window(own, reach, chips, step):
    far = [own]
    for k in range(1, reach + 1):
        if step > 0:
            pairs = [(i, i + 4 * k) for i in range(4 * (chips - k))]
        else:
            pairs = [(i + 4 * k, i) for i in range(4 * (chips - k))]
        far.append(lax.ppermute(own, "ctx", pairs))
    return far


def both_cores(far, core, step):
    near = core == (0 if step > 0 else 1)
    parts = []
    for k in range(len(far) - 1):
        parts += [swap_core(jnp.where(near, far[k], far[k + 1])), far[k + 1]]
    return parts


def shards(
    tokens,
    cotangent,
    lengths,
    deal_order,
    w_query,
    w_key,
    w_value,
    w_out,
    w_up,
    w_down,
    b_query,
    b_value,
    b_out,
    b_up,
    b_down,
    gain_one,
    shift_one,
    gain_two,
    shift_two,
    positions,
):
    block, width = tokens.shape[2], tokens.shape[3]
    ranks = lax.axis_size("ctx")
    chips = ranks // 4
    slot = block // ranks
    rows = 2 * block
    group = ranks * block
    longest = 2 * positions.shape[0]
    reach = longest // (2 * rows)
    here = lax.axis_index("ctx")
    core = lax.axis_index("fsdp")
    chip, micro, stream = here // 4, here % 2, (here // 2) % 2
    base = chip * (2 * rows) + core * rows

    index = lambda i, t: 2 * i + t
    straight, crossing = [], []
    for i in range(ranks):
        c, a, b = i // 4, (i // 2) % 2, i % 2
        for t in range(2):
            straight.append((index(i, t), index(4 * c + 2 * t + b, a)))
            crossing.append((index(i, t), index(4 * c + 2 * t + 1 - b, a)))
    even = here % 2 == 0
    same = jnp.where(even, tokens[0, 0], tokens[1, 0])
    cross = jnp.where(even, tokens[1, 0], tokens[0, 0])
    got_same = lax.ppermute(same, BOTH, straight)
    got_cross = lax.ppermute(cross, BOTH, crossing)
    first_half = jnp.where(micro == 0, got_same, got_cross)
    second_half = jnp.where(micro == 0, got_cross, got_same)
    own = jnp.concatenate([first_half, second_half], axis=0)

    table = jnp.concatenate([deal_order[:, 0], lengths[:, 0]], axis=1)
    table = jnp.where(micro == 0, table[0], table[1])
    table = jnp.where(stream == core, table, swap_core(table))
    order, lens = table[:group], table[group:]

    head = jnp.stack([core, base, jnp.int32(group)]).astype(jnp.int32)
    info = jnp.concatenate([head, lens])

    whole = lambda x: (x, swap_core(x))
    pos, wq, wk, wv = whole(positions), whole(w_query), whole(w_key), whole(w_value)
    vectors = [b_out, b_down, gain_one, shift_one, gain_two, shift_two, b_query, b_value, b_up]
    vec = whole(stack_vectors(vectors, width // 2))
    wo, wu, wd = whole(w_out), whole(w_up), whole(w_down)

    mine = order.reshape(ranks, ranks, slot)
    mine = lax.dynamic_slice_in_dim(mine, 4 * chip + 2 * core, 2, axis=1).reshape(rows) - base
    dealt = cotangent[:, 0].reshape(2, chips, 2, 2 * slot, width)
    keep = jnp.where(core == 0, dealt[:, :, 0], dealt[:, :, 1])
    give = jnp.where(core == 0, dealt[:, :, 1], dealt[:, :, 0])
    streams = by_core(core, keep, swap_core(give))
    sends = jnp.transpose(streams, (2, 0, 1, 3, 4)).reshape(rows, width)
    arrived = lax.all_to_all(sends, "ctx", split_axis=0, concat_axis=0, tiled=True)

    fixed_args = (pos, wk, wv, wq, vec)
    far = send_window(own, reach, chips, 1)
    own = after(arrived, own)
    k, v, q, hidden, low = project(info, [own], 0, True, *fixed_args)
    far[1:] = after(k, far[1:])

    earlier = both_cores(far, core, 1)[::-1]
    before = len(earlier) * rows
    kp, vp = project(info, earlier, -before, False, *fixed_args)
    far_q = send_window(after(kp, q), reach, chips, -1)
    att, exact, logs, log_stats = attend_forward(info, q, kp, k, vp, v)
    leaving, da_msg, dz1, active, df, h1, du, do, sums = feed_forward(
        info, att, exact, log_stats, hidden, arrived, mine, wo, wu, wd, vec
    )
    da_msg, do, leaving = after(far_q[1:], (da_msg, do, leaving))
    far_da = [da_msg, next_chip(da_msg, chips, -1)]

    half = width // 2
    units = 2 * b_up.shape[0]
    sizes = [units // 8, half, width // 8]
    quarter = padded(sum(sizes) + 16, ranks)
    sizes.append(quarter - sum(sizes))
    sizes_last = [width // 8, width // 8, width // 8, longest // 8]
    quarter_last = padded(sum(sizes_last) + 8, ranks)
    sizes_last.append(quarter_last - sum(sizes_last))
    one = Reduction(here, ranks, sizes, 1)
    two = Reduction(here, ranks, sizes_last, None)
    levels = len(one.stages)

    keep, give = ffn_grads(info, att, do, active, df, h1, du, sums, quarter)
    give = after(far_da[1], give)
    for _ in range(reach - 1):
        far_da.append(next_chip(far_da[-1], chips, -1))
    pieces = one.cut([keep, swap_core(give)], 0)
    exact = after(pieces, exact)
    terms = one.scatter(pieces, 0)
    dq, dh = attend_query(info, q, kp, k, vp, v, logs, da_msg, exact, dz1, wq)
    far_da[1:], far_q[1:] = after(dq, (far_da[1:], far_q[1:]))
    later_da = [da_msg] + both_cores(far_da, core, -1)
    later_q = [q] + both_cores(far_q, core, -1)
    keep, give, dh0_low = last(info, later_q, later_da, k, v, low, dq, dh, wk, wv, quarter_last, longest)

    keep, give, dh0_low = after(terms[1:], (keep, give, dh0_low))
    terms_last = [keep, swap_core(give)]
    for level in range(levels):
        pieces = one.cut(terms, level + 1)
        if level + 1 < levels:
            terms = one.scatter(pieces, level + 1)
        pieces_last = two.cut(after(pieces, terms_last), level)
        terms_last = two.scatter(pieces_last, level)
        if level == 0:
            leaving, dh0_low = after(pieces_last, (leaving, dh0_low))
    held = pieces[0]
    parts = one.gather(held, levels - 1)
    for level in reversed(range(levels)):
        if level == levels - 1:
            held = one.place(after(pieces_last, parts), level)
            (held_last,) = two.cut(after(held, terms_last), levels)
        else:
            held = one.place(parts, level)
        parts_last = two.gather(held_last, level)
        if level:
            parts = one.gather(held, level - 1)
            parts_last = after(parts[1:], parts_last)
        held_last = two.place(parts_last, level)
    g_down, g_up, g_out, early = held
    g_key, g_value, g_query, g_pos, late = held_last
    shard = lambda x: lax.dynamic_slice_in_dim(x, core * half, half)
    gb_down, gg1, gs1, gg2, gs2, gb_out = (shard(early[n]) for n in range(6))
    gb_up = lax.dynamic_slice_in_dim(early[7:11].reshape(-1), core * (units // 2), units // 2)
    gb_value, gb_query = shard(late[0]), shard(late[1])

    landed = lax.all_to_all(leaving, "ctx", split_axis=0, concat_axis=0, tiled=True)
    landed = landed.reshape(chips, 2, 2, 2 * slot, width)
    keep = jnp.where(core == 0, landed[:, 0], landed[:, 1])
    give = jnp.where(core == 0, landed[:, 1], landed[:, 0])
    sides = by_core(core, keep, swap_core(give))
    output = jnp.transpose(sides, (2, 1, 0, 3, 4)).reshape(2, 1, block, width)

    back_same = jnp.where(micro == 0, dh0_low[:block], dh0_low[block:])
    back_cross = jnp.where(micro == 0, dh0_low[block:], dh0_low[:block])
    home_same = lax.ppermute(back_same, BOTH, [(b, a) for a, b in straight])
    home_cross = lax.ppermute(back_cross, BOTH, [(b, a) for a, b in crossing])
    grad_tokens = jnp.where(
        even, jnp.stack([home_same, home_cross]), jnp.stack([home_cross, home_same])
    )[:, None]

    return (
        output,
        grad_tokens,
        g_query,
        g_key,
        g_value,
        g_out,
        g_up,
        g_down,
        gb_query,
        gb_value,
        gb_out,
        gb_up,
        gb_down,
        gg1,
        gs1,
        gg2,
        gs2,
        g_pos,
    )


def solution(mesh):
    data = P(None, "fsdp", "ctx", None)
    groups = P(None, "fsdp", None)
    matrix, vector = P("fsdp", None), P("fsdp")
    return jax.shard_map(
        shards,
        mesh=mesh,
        in_specs=(data, data, groups, groups) + (matrix,) * 6 + (vector,) * 9 + (matrix,),
        out_specs=(data, data) + (matrix,) * 6 + (vector,) * 9 + (matrix,),
        check_vma=False,
    )
```

```python
import functools

import jax
import jax.numpy as jnp
from jax import lax
from jax.experimental import pallas as pl
from jax.experimental.pallas import tpu as pltpu
from jax.sharding import PartitionSpec as P

HEADS = 8
epsilon = 1e-05
gelu_coeff = 0.7978845608028654
cubic_coeff = 0.044715
BF = jnp.bfloat16
F32 = jnp.float32
SWAP = ((0, 1), (1, 0))
BOTH = ("ctx", "fsdp")
FAR = 1 << 30


def dot(a, b):
    return jnp.dot(a, b, preferred_element_type=F32)


def dot_tn(a, b):
    return lax.dot_general(a, b, (((0,), (0,)), ((), ())), preferred_element_type=F32)


def dot_nt(a, b):
    return lax.dot_general(a, b, (((1,), (1,)), ((), ())), preferred_element_type=F32)


def gelu_parts(u):
    inner = gelu_coeff * (u + cubic_coeff * u * u * u)
    bent = jnp.tanh(inner)
    value = 0.5 * u * (1.0 + bent)
    slope = 0.5 * (1.0 + bent) + 0.5 * u * (1.0 - bent * bent) * gelu_coeff * (
        1.0 + 3.0 * cubic_coeff * u * u
    )
    return value, slope


def normalize(z):
    center = z - jnp.mean(z, axis=-1, keepdims=True)
    inv = lax.rsqrt(jnp.mean(center * center, axis=-1, keepdims=True) + epsilon)
    return center * inv, inv


def normalize_back(t, normed, inv):
    return inv * (
        t
        - jnp.mean(t, axis=-1, keepdims=True)
        - normed * jnp.mean(t * normed, axis=-1, keepdims=True)
    )


def first_places(info, spots):
    first, end = jnp.zeros_like(spots), 0
    for n in range(3, info.shape[0]):
        end = end + info[n]
        first = first + jnp.where(spots >= end, info[n], 0)
    return first


def lay(info, whole, own, other):
    n = own.shape[0]
    mine = info[0] == 0
    whole[0:n, :] = jnp.where(mine, own[...], other[...])
    whole[n : 2 * n, :] = jnp.where(mine, other[...], own[...])


def full_row(info, own, other, at, count=1):
    mine = info[0] == 0
    rows = [x[at + n : at + n + 1, :] for x in (own, other) for n in range(count)]
    first = [jnp.where(mine, rows[n], rows[count + n]) for n in range(count)]
    second = [jnp.where(mine, rows[count + n], rows[n]) for n in range(count)]
    return jnp.concatenate(first + second, axis=1)


def stack_vectors(vectors, width):
    row, at = iota((16, width), 0), 0
    table = jnp.zeros((16, width), BF)
    for x in vectors:
        for n in range(x.shape[0] // width):
            part = x[n * width : n * width + width]
            table = jnp.where(row == at, part[None, :], table)
            at += 1
    return table.astype(F32)


def iota(shape, axis):
    return lax.broadcasted_iota(jnp.int32, shape, axis)


def params(cols=0):
    return pltpu.CompilerParams(vmem_limit_bytes=(32 if cols <= 2048 else 56) * 1024 * 1024)


def lasting(us):
    return pl.CostEstimate(flops=us, transcendentals=0, bytes_accessed=us)


def fixed(shape):
    return pl.BlockSpec(shape, lambda *_: (0,) * len(shape), pipeline_mode=pl.Buffered(1))


def paired(rows):
    return pl.BlockSpec((rows, 128), lambda p, *_: (0, p))


def project_kernel(info, *refs, blocks, offset, own):
    toks = refs[:blocks]
    pos_a, pos_b, wk_a, wk_b, wv_a, wv_b, wq_a, wq_b, vec_a, vec_b = refs[blocks : blocks + 10]
    outs = refs[blocks + 10 :]
    k_ref, v_ref = outs[:2]
    wk, wv, wq, tok = outs[-4:]
    step = pl.program_id(0)
    rows = tok.shape[0]

    @pl.when(step == 0)
    def _():
        lay(info, wk, wk_a, wk_b)
        lay(info, wv, wv_a, wv_b)
        if own:
            lay(info, wq, wq_a, wq_b)

    for n in range(blocks):

        @pl.when(step == n)
        def _():
            tok[...] = toks[n][...]

    spots = info[1] + offset + step * rows + iota((rows, 1), 0)
    place = spots - first_places(info, spots)
    hidden = tok[...].astype(F32)
    half = pos_a.shape[0]
    chunk = min(half, 512)
    for part, begin in ((pos_a, info[0] * half), (pos_b, (1 - info[0]) * half)):
        for at in range(0, half, chunk):
            hot = (place - begin - at == iota((rows, chunk), 1)).astype(F32).astype(BF)
            hidden = hidden + dot(hot, part[at : at + chunk, :])
    low = hidden.astype(BF)
    k_ref[...] = dot(low, wk[...]).astype(BF)
    v_ref[...] = (dot(low, wv[...]) + full_row(info, vec_a, vec_b, 7)).astype(BF)
    if own:
        q_ref, hidden_ref, low_ref = outs[2:5]
        q_ref[...] = ((dot(low, wq[...]) + full_row(info, vec_a, vec_b, 6)).astype(BF).astype(F32) * 0.125).astype(BF)
        hidden_ref[...] = hidden
        low_ref[...] = low


def project(info, toks, offset, own, pos, wk, wv, wq, vec):
    rows, width = toks[0].shape
    blocks = len(toks)
    tall = pl.BlockSpec((rows, width), lambda n, *_: (n, 0))
    flat = jax.ShapeDtypeStruct((rows * blocks, width), BF)
    square = pltpu.VMEM((width, width), BF)
    args = (*toks, *pos, *wk, *wv, *wq, *vec)
    return pl.pallas_call(
        functools.partial(project_kernel, blocks=blocks, offset=offset, own=own),
        grid_spec=pltpu.PrefetchScalarGridSpec(
            num_scalar_prefetch=1,
            grid=(blocks,),
            in_specs=[fixed(x.shape) for x in args],
            out_specs=[tall] * (5 if own else 2),
            scratch_shapes=[square, square, square, pltpu.VMEM((rows, width), BF)],
        ),
        out_shape=[flat] * 3 + [jax.ShapeDtypeStruct((rows, width), F32), flat] if own else [flat] * 2,
        compiler_params=pltpu.CompilerParams(vmem_limit_bytes=60 * 1024 * 1024),
        cost_estimate=lasting(2 * blocks + 2),
        name="project",
    )(info, *args)


def stat_rows(table):
    high = table.astype(BF).astype(F32)
    middle = (table - high).astype(BF).astype(F32)
    low = table - high - middle
    count = table.shape[1] // 128
    rows = [
        part[half : half + 1, 128 * n : 128 * n + 128]
        for part in (high, middle, low)
        for half in range(2)
        for n in range(count)
    ]
    rows.append(jnp.zeros((16 - len(rows), 128), F32))
    return jnp.concatenate(rows, axis=0).astype(BF)


def stat_row(rows16, half, queries):
    count = queries // 128
    wide = rows16.astype(F32)
    total = wide[0 : 2 * count] + wide[2 * count : 4 * count] + wide[4 * count : 6 * count]
    return jnp.concatenate([total[half * count + n : half * count + n + 1] for n in range(count)], axis=1)


def chunks_of(cols):
    step = cols if cols <= 2048 else 768
    return [slice(at, min(at + step, cols)) for at in range(0, cols, step)]


def bias_scratch(rows, cols):
    return pltpu.VMEM((rows, cols) if len(chunks_of(cols)) == 1 else (8, 128), F32)


def query_bias(info, rows, before, chunk):
    spots = info[1] + iota((rows, 1), 0)
    first = first_places(info, spots) - (info[1] - before)
    last = iota((rows, 1), 0) + before
    col = iota((rows, chunk.stop - chunk.start), 1) + chunk.start
    return jnp.where((col >= first) & (col <= last), 0.0, -1e30)


def key_bias(info, rows, chunk):
    spots = info[1] + chunk.start + iota((1, chunk.stop - chunk.start), 1)
    first = jnp.where(spots < info[2], first_places(info, spots) - info[1], FAR)
    shape = (rows, chunk.stop - chunk.start)
    row = iota(shape, 0)
    return jnp.where((row >= first) & (row <= iota(shape, 1) + chunk.start), 0.0, -1e30)


def forward_kernel(info, q_ref, kp_ref, k_ref, vp_ref, v_ref, a_ref, exact_ref, log_ref, stat_ref, bias, keys, values):
    rows, before = q_ref.shape[0], kp_ref.shape[0]

    chunks = chunks_of(keys.shape[0])
    make_bias = functools.partial(query_bias, info, rows, before)

    @pl.when(pl.program_id(0) == 0)
    def _():
        if len(chunks) == 1:
            bias[...] = make_bias(chunks[0])

    keys[0:before, :] = kp_ref[...]
    keys[before:, :] = k_ref[...]
    values[0:before, :] = vp_ref[...]
    values[before:, :] = v_ref[...]
    logs = []
    for half in range(2):
        lanes = slice(64 * half, 64 * half + 64)


        def scores_of(chunk):
            mask = bias[...] if len(chunks) == 1 else make_bias(chunk)
            return dot_nt(q_ref[:, lanes], keys[chunk, lanes]) + mask

        if len(chunks) == 1:
            scores = scores_of(chunks[0])
            top = jnp.max(scores, axis=1, keepdims=True)
            raised = jnp.exp(scores - top)
            total = jnp.sum(raised, axis=1, keepdims=True)
            probs = raised * (1.0 / total)
            low = probs.astype(BF)
            attended = dot(low, values[:, lanes])
            weight = jnp.sum(low.astype(F32), axis=1, keepdims=True)
        else:
            top = jnp.full((rows, 1), -1e30, F32)
            for chunk in chunks:
                top = jnp.maximum(top, jnp.max(scores_of(chunk), axis=1, keepdims=True))
            total = jnp.zeros((rows, 1), F32)
            for chunk in chunks:
                total = total + jnp.sum(jnp.exp(scores_of(chunk) - top), axis=1, keepdims=True)
            attended, weight = jnp.zeros((rows, 64), F32), jnp.zeros((rows, 1), F32)
            for chunk in chunks:
                probs = jnp.exp(scores_of(chunk) - top) * (1.0 / total)
                low = probs.astype(BF)
                attended = attended + dot(low, values[chunk, lanes])
                weight = weight + jnp.sum(low.astype(F32), axis=1, keepdims=True)
        a_ref[:, lanes] = attended.astype(BF)
        exact_ref[:, lanes] = attended / weight
        logs.append(jnp.broadcast_to(top + jnp.log(total), (rows, 64)))
    wide = jnp.concatenate(logs, axis=1)
    log_ref[...] = wide
    turned = wide.T
    stat_ref[...] = stat_rows(jnp.concatenate([turned[0:1], turned[64:65]], axis=0))


def attend_forward(info, q, kp, k, vp, v):
    rows, width = q.shape
    before = kp.shape[0]
    cols = before + rows
    return pl.pallas_call(
        forward_kernel,
        grid_spec=pltpu.PrefetchScalarGridSpec(
            num_scalar_prefetch=1,
            grid=(width // 128,),
            in_specs=[paired(x.shape[0]) for x in (q, kp, k, vp, v)],
            out_specs=[paired(rows), paired(rows), paired(rows), paired(16)],
            scratch_shapes=[
                bias_scratch(rows, cols),
                pltpu.VMEM((cols, 128), BF),
                pltpu.VMEM((cols, 128), BF),
            ],
        ),
        out_shape=[
            jax.ShapeDtypeStruct((rows, width), BF),
            jax.ShapeDtypeStruct((rows, width), F32),
            jax.ShapeDtypeStruct((rows, width), F32),
            jax.ShapeDtypeStruct((16, width), BF),
        ],
        compiler_params=params(cols),
        cost_estimate=lasting(12),
        name="attend_forward",
    )(info, q, kp, k, vp, v)


def ffn_kernel(
    info, a_ref, exact_ref, stat_ref, hidden_ref, arrived_ref, row_ref, col_ref, wo_a, wo_b, wu_a, wu_b, wd_a, wd_b, vec_a, vec_b,
    leaving_ref, msg_ref, dz1_ref, active_ref, df_ref, h1_ref, du_ref, do_ref, sums_ref,
    wo, wu, wd, slopes, stats,
):
    lay(info, wo, wo_a, wo_b)
    lay(info, wu, wu_a, wu_b)
    lay(info, wd, wd_a, wd_b)
    rows, width = hidden_ref.shape
    hidden_units = wu.shape[1]
    bo, bd, g1, s1, g2, s2 = (full_row(info, vec_a, vec_b, n) for n in range(6))
    bu = full_row(info, vec_a, vec_b, 8, hidden_units // width)
    pick = (iota((rows, rows), 0) == row_ref[...]).astype(F32).astype(BF)
    pick_back = (col_ref[...] == iota((rows, rows), 1)).astype(F32).astype(BF)
    dy = dot(pick, arrived_ref[...])

    n1, r1 = normalize(hidden_ref[...] + dot(a_ref[...], wo[...]) + bo)
    h1 = n1 * g1 + s1
    h1_low = h1.astype(BF)
    h1_ref[...] = h1_low
    z2 = h1 + bd
    for at in range(0, hidden_units, width):
        block = slice(at, at + width)
        value, slope = gelu_parts(dot(h1_low, wu[:, block]) + bu[:, block])
        slopes[:, block] = slope
        low = value.astype(BF)
        active_ref[:, block] = low
        z2 = z2 + dot(low, wd[block, :])
    n2, r2 = normalize(z2)
    leaving_ref[...] = dot(pick_back, (n2 * g2 + s2).astype(BF)).astype(BF)

    def add(x):
        return jnp.sum(x, axis=0, keepdims=True)

    dz2 = normalize_back(dy * g2, n2, r2)
    df = dz2.astype(BF)
    df_ref[...] = df
    sums_ref[0:1, :] = add(df.astype(F32))
    sums_ref[3:4, :] = add(dy * n2)
    sums_ref[4:5, :] = add(dy)
    dh1 = dz2
    for at in range(0, hidden_units, width):
        block = slice(at, at + width)
        du = (dot_nt(df, wd[block, :]) * slopes[:, block]).astype(BF)
        du_ref[:, block] = du
        n = 7 + at // width
        sums_ref[n : n + 1, :] = add(du.astype(F32))
        dh1 = dh1 + dot_nt(du, wu[:, block])
    dz1 = normalize_back(dh1 * g1, n1, r1)
    dz1_ref[...] = dz1
    sums_ref[1:2, :] = add(dh1 * n1)
    sums_ref[2:3, :] = add(dh1)
    do = dz1.astype(BF)
    do_ref[...] = do
    sums_ref[5:6, :] = add(do.astype(F32))
    sums_ref[6:7, :] = jnp.zeros((1, width), F32)
    sums_ref[11:16, :] = jnp.zeros((5, width), F32)
    da = dot_nt(do, wo[...]).astype(BF)
    msg_ref[0:rows, :] = da
    terms = da.astype(F32) * exact_ref[...]
    head = iota((HEADS, width), 0)
    lane = iota((HEADS, width), 1) // (width // HEADS)
    ones = (head == lane).astype(F32).astype(BF)
    delta = jnp.zeros((HEADS, rows), F32)
    for _ in range(3):
        part = terms.astype(BF)
        terms = terms - part.astype(F32)
        delta = delta + dot_nt(ones, part)
    for p in range(HEADS // 2):
        stats[:, 128 * p : 128 * p + 128] = stat_rows(delta[2 * p : 2 * p + 2, :])
    msg_ref[rows : rows + 16, :] = stat_ref[...]
    msg_ref[rows + 16 : rows + 32, :] = stats[...]


def feed_forward(info, a, exact, log_stats, hidden, arrived, mine, wo, wu, wd, vec):
    rows, width = hidden.shape
    units = wu[0].shape[1]
    args = (a, exact, log_stats, hidden, arrived, *mine, *wo, *wu, *wd, *vec)
    low = jax.ShapeDtypeStruct((rows, width), BF)
    tall = jax.ShapeDtypeStruct((rows, units), BF)
    outs = [
        low,
        jax.ShapeDtypeStruct((rows + 32, width), BF),
        jax.ShapeDtypeStruct((rows, width), F32),
        tall,
        low,
        low,
        tall,
        low,
        jax.ShapeDtypeStruct((16, width), F32),
    ]
    return pl.pallas_call(
        ffn_kernel,
        grid_spec=pltpu.PrefetchScalarGridSpec(
            num_scalar_prefetch=1,
            grid=(1,),
            in_specs=[fixed(x.shape) for x in args],
            out_specs=[fixed(x.shape) for x in outs],
            scratch_shapes=[
                pltpu.VMEM((width, width), BF),
                pltpu.VMEM((width, units), BF),
                pltpu.VMEM((units, width), BF),
                pltpu.VMEM((rows, units), F32),
                pltpu.VMEM((16, width), BF),
            ],
        ),
        out_shape=outs,
        compiler_params=params(),
        cost_estimate=lasting(10),
        name="feed_forward",
    )(info, *args)


def keep_or_send(info, half, mine, send, at, value):
    at, value = pl.multiple_of(at, 8), value.astype(BF)

    @pl.when(info[0] == half)
    def _():
        mine[pl.ds(at, value.shape[0]), :] = value

    @pl.when(info[0] != half)
    def _():
        send[pl.ds(at, value.shape[0]), :] = value


def split_halves(info, mine, send, starts, value):
    half, step = value.shape[0] // 2, value.shape[0] // 8
    first = info[0] == 0
    own = jnp.where(first, value[:half], value[half:]).astype(BF)
    other = jnp.where(first, value[half:], value[:half]).astype(BF)
    for n, at in enumerate(starts):
        mine[at : at + step, :] = own[n * step : n * step + step]
        send[at : at + step, :] = other[n * step : n * step + step]


def grads_kernel(
    info, a_own, a_other, do_ref, active_own, active_other, df_ref, h1_ref, du_ref, mine, send, *, quarter
):
    width = df_ref.shape[1]
    step = pl.program_id(0)
    part = active_own.shape[1]
    mine[0:part, :] = dot_tn(active_own[...], df_ref[...]).astype(BF)
    send[0:part, :] = dot_tn(active_other[...], df_ref[...]).astype(BF)
    up = dot_tn(h1_ref[...], du_ref[...])
    low, high = up[: width // 2].astype(BF), up[width // 2 :].astype(BF)
    at = part + width // 2
    mine[part:at, :] = jnp.where(info[0] == 0, low, high)
    send[part:at, :] = jnp.where(info[0] == 0, high, low)
    for out, a_ref in ((mine, a_own), (send, a_other)):
        both = dot_tn(a_ref[...], do_ref[...]).astype(BF)
        out[at : at + 64, :] = jnp.where(step % 2 == 0, both[:64], both[64:])
        if quarter > at + 64:
            out[at + 64 :, :] = jnp.zeros((quarter - at - 64, width), BF)


def ffn_grads(info, a, do, active, df, h1, du, quarter):
    rows, width = df.shape
    units = active.shape[1]
    out = jax.ShapeDtypeStruct((4 * quarter, width), BF)
    columns = lambda n, index: pl.BlockSpec((rows, n), lambda j, info: (0, index(j, info[0])))
    return pl.pallas_call(
        functools.partial(grads_kernel, quarter=quarter),
        grid_spec=pltpu.PrefetchScalarGridSpec(
            num_scalar_prefetch=1,
            grid=(4,),
            in_specs=[
                columns(128, lambda j, core: core * 2 + j // 2),
                columns(128, lambda j, core: (1 - core) * 2 + j // 2),
                fixed(do.shape),
                columns(units // 8, lambda j, core: core * 4 + j),
                columns(units // 8, lambda j, core: (1 - core) * 4 + j),
                fixed(df.shape),
                fixed(h1.shape),
                columns(units // 4, lambda j, core: j),
            ],
            out_specs=[pl.BlockSpec((quarter, width), lambda j, *_: (j, 0))] * 2,
        ),
        out_shape=[out, out],
        compiler_params=params(),
        cost_estimate=lasting(10),
        name="ffn_grads",
    )(info, a, a, do, active, active, df, h1, du)


def query_kernel(
    info, q_ref, kp_ref, k_ref, vp_ref, v_ref, log_ref, da_ref, exact_ref, dq_ref, bias, keys, values
):
    rows, before = q_ref.shape[0], kp_ref.shape[0]
    chunks = chunks_of(keys.shape[0])
    make_bias = functools.partial(query_bias, info, rows, before)

    @pl.when(pl.program_id(0) == 0)
    def _():
        if len(chunks) == 1:
            bias[...] = make_bias(chunks[0])

    keys[0:before, :] = kp_ref[...]
    keys[before:, :] = k_ref[...]
    values[0:before, :] = vp_ref[...]
    values[before:, :] = v_ref[...]
    for half in range(2):
        lanes = slice(64 * half, 64 * half + 64)
        delta = jnp.sum(da_ref[:, lanes].astype(F32) * exact_ref[:, lanes], axis=1, keepdims=True)
        dq = jnp.zeros((rows, 64), F32)
        for chunk in chunks:
            mask = bias[...] if len(chunks) == 1 else make_bias(chunk)
            scores = dot_nt(q_ref[:, lanes], keys[chunk, lanes]) + mask
            probs = jnp.exp(scores - log_ref[:, 64 * half : 64 * half + 1])
            dp = dot_nt(da_ref[:, lanes], values[chunk, lanes])
            ds = (probs * (dp - delta)).astype(BF)
            dq = dq + dot(ds, keys[chunk, lanes])
        dq_ref[:, lanes] = (dq * 0.125).astype(BF)


def attend_query(info, first, count, q, kp, k, vp, v, logs, da, exact):
    rows = q.shape[0]
    before = kp.shape[0]
    cols = before + rows
    some = lambda n: pl.BlockSpec((n, 128), lambda p, *_: (0, p + first))
    return pl.pallas_call(
        query_kernel,
        grid_spec=pltpu.PrefetchScalarGridSpec(
            num_scalar_prefetch=1,
            grid=(count,),
            in_specs=[some(x.shape[0]) for x in (q, kp, k, vp, v, logs)] + [some(rows), some(rows)],
            out_specs=paired(rows),
            scratch_shapes=[
                bias_scratch(rows, cols),
                pltpu.VMEM((cols, 128), BF),
                pltpu.VMEM((cols, 128), BF),
            ],
        ),
        out_shape=jax.ShapeDtypeStruct((rows, 128 * count), BF),
        compiler_params=params(cols),
        cost_estimate=lasting(5),
        name="attend_query",
    )(info, q, kp, k, vp, v, logs, da, exact)


def last_kernel(info, *refs, reach, quarter, table):
    count = 2 * reach + 1
    q_parts, da_parts = refs[:count], refs[count : 2 * count]
    k_ref, v_ref, low_ref, dq_a, dq_b, dz1_ref, sums_ref, wq_a, wq_b, wk_a, wk_b, wv_a, wv_b = refs[2 * count : 2 * count + 13]
    mine, send, dh_out, bias, queries, grads, dk_all, dv_all, wq, wk, wv = refs[2 * count + 13 :]
    rows, width = low_ref.shape
    cols = queries.shape[0]
    step = pl.program_id(0)

    chunks = chunks_of(cols)
    make_bias = functools.partial(key_bias, info, rows)

    @pl.when(step == 0)
    def _():
        lay(info, wq, wq_a, wq_b)
        lay(info, wk, wk_a, wk_b)
        lay(info, wv, wv_a, wv_b)
        if len(chunks) == 1:
            bias[...] = make_bias(chunks[0])

    for n in range(count):
        queries[n * rows : n * rows + rows, :] = q_parts[n][...]
        grads[n * rows : n * rows + rows, :] = da_parts[n][0:rows, :]
    dks, dvs = [], []
    for half in range(2):
        lanes = slice(64 * half, 64 * half + 64)
        logs = jnp.concatenate([stat_row(x[rows : rows + 16, :], half, rows) for x in da_parts], axis=1)
        delta = jnp.concatenate([stat_row(x[rows + 16 : rows + 32, :], half, rows) for x in da_parts], axis=1)
        dk, dv = jnp.zeros((rows, 64), F32), jnp.zeros((rows, 64), F32)
        for chunk in chunks:
            mask = bias[...] if len(chunks) == 1 else make_bias(chunk)
            scores = dot_nt(k_ref[:, lanes], queries[chunk, lanes]) + mask
            probs = jnp.exp(scores - logs[:, chunk])
            dv = dv + dot(probs.astype(BF), grads[chunk, lanes])
            dp = dot_nt(v_ref[:, lanes], grads[chunk, lanes])
            ds = (probs * (dp - delta[:, chunk])).astype(BF)
            dk = dk + dot(ds, queries[chunk, lanes])
        dks.append(dk.astype(BF))
        dvs.append(dv.astype(BF))
    dk_pair, dv_pair = jnp.concatenate(dks, axis=1), jnp.concatenate(dvs, axis=1)
    for n in range(width // 128):

        @pl.when(step == n)
        def _():
            dk_all[:, 128 * n : 128 * n + 128] = dk_pair
            dv_all[:, 128 * n : 128 * n + 128] = dv_pair

    @pl.when(step == pl.num_programs(0) - 1)
    def _():
        dk, dv = dk_all[...], dv_all[...]
        step_rows = width // 8
        split_halves(info, mine, send, [n * quarter for n in range(4)], dot_tn(low_ref[...], dk))
        split_halves(info, mine, send, [n * quarter + step_rows for n in range(4)], dot_tn(low_ref[...], dv))
        dq = jnp.concatenate([dq_a[...], dq_b[...]], axis=1)
        split_halves(info, mine, send, [n * quarter + 2 * step_rows for n in range(4)], dot_tn(low_ref[...], dq))
        dh = dz1_ref[...] + dot_nt(dq, wq[...]) + dot_nt(dk, wk[...]) + dot_nt(dv, wv[...])
        dh_out[...] = dh.astype(BF)
        parts = []
        for _ in range(3):
            parts.append(dh.astype(BF))
            dh = dh - parts[-1].astype(F32)
        spots = info[1] + iota((1, rows), 1)
        place = spots - first_places(info, spots)
        base = 3 * step_rows
        fourth = table // 8
        for half in range(2):
            for n in range(4):
                hot = (place - (half * 4 + n) * fourth == iota((fourth, rows), 0)).astype(F32).astype(BF)
                total = dot(hot, parts[0]) + dot(hot, parts[1]) + dot(hot, parts[2])
                keep_or_send(info, half, mine, send, n * quarter + base, total)
        base += fourth
        spare = quarter - base
        for n in range(4):
            mine[n * quarter + base : (n + 1) * quarter, :] = jnp.zeros((spare, width), BF)
            send[n * quarter + base : (n + 1) * quarter, :] = jnp.zeros((spare, width), BF)
        total_v = jnp.sum(dv.astype(F32), axis=0, keepdims=True)
        total_q = jnp.sum(dq.astype(F32), axis=0, keepdims=True)
        row = iota(sums_ref.shape, 0)
        total = jnp.where(row == 6, total_q, jnp.where(row == 11, total_v, sums_ref[...])).astype(BF)
        mine[base : base + 16, :] = total
        send[base : base + 16, :] = total


def last(info, q_parts, da_parts, k, v, low, dqs, dz1, sums, wq, wk, wv, quarter, table):
    rows, width = k.shape
    count = len(q_parts)
    cols = count * rows
    outs = [
        jax.ShapeDtypeStruct((4 * quarter, width), BF),
        jax.ShapeDtypeStruct((4 * quarter, width), BF),
        jax.ShapeDtypeStruct((rows, width), BF),
    ]
    rest = (low, *dqs, dz1, sums, *wq, *wk, *wv)
    return pl.pallas_call(
        functools.partial(last_kernel, reach=count // 2, quarter=quarter, table=table),
        grid_spec=pltpu.PrefetchScalarGridSpec(
            num_scalar_prefetch=1,
            grid=(width // 128,),
            in_specs=[paired(x.shape[0]) for x in (*q_parts, *da_parts, k, v)] + [fixed(x.shape) for x in rest],
            out_specs=[fixed(x.shape) for x in outs],
            scratch_shapes=[
                bias_scratch(rows, cols),
                pltpu.VMEM((cols, 128), BF),
                pltpu.VMEM((cols, 128), BF),
                pltpu.VMEM((rows, width), BF),
                pltpu.VMEM((rows, width), BF),
                pltpu.VMEM((width, width), BF),
                pltpu.VMEM((width, width), BF),
                pltpu.VMEM((width, width), BF),
            ],
        ),
        out_shape=outs,
        compiler_params=params(cols),
        cost_estimate=lasting(15),
        name="last",
    )(info, *q_parts, *da_parts, k, v, *rest)


def cut_kernel(digit_ref, *refs, terms, radix):
    ins, outs = refs[: terms * radix], refs[terms * radix :]
    for k in range(radix):
        total = ins[k * terms][...].astype(F32)
        for n in range(1, terms):
            total = total + ins[k * terms + n][...].astype(F32)
        outs[k][...] = total.astype(outs[k].dtype)


def rows_of(terms):
    return terms[0][0].shape[0] // (1 + max(block for _, block in terms))


def cut(terms, digit, radix, kept):
    rows, width = rows_of(terms) // radix, terms[0][0].shape[1]
    subs = max(n for n in (1, 2, 3, 4) if rows % (8 * n) == 0 and rows // n >= 64 or n == 1)
    specs = [
        pl.BlockSpec((rows // subs, width), lambda n, d, k=k, b=b: ((b * radix + (d[0] ^ k)) * subs + n, 0))
        for k in range(radix)
        for _, b in terms
    ]
    return pl.pallas_call(
        functools.partial(cut_kernel, terms=len(terms), radix=radix),
        grid_spec=pltpu.PrefetchScalarGridSpec(
            num_scalar_prefetch=1,
            grid=(subs,),
            in_specs=specs,
            out_specs=[pl.BlockSpec((rows // subs, width), lambda n, d: (n, 0))] * radix,
        ),
        out_shape=[jax.ShapeDtypeStruct((rows, width), BF if k else kept) for k in range(radix)],
        compiler_params=params(),
        cost_estimate=lasting(3),
        name="cut",
    )(digit.reshape(1), *([x for x, _ in terms] * radix))


def total_of(refs):
    total = refs[0][...].astype(F32)
    for ref in refs[1:]:
        total = total + ref[...].astype(F32)
    return total


def join_kernel(digit_ref, *refs, ones, twos, radix):
    done, held, *messages = refs[ones + twos * radix :]
    rows = done.shape[0]
    whole = total_of(refs[:ones]).astype(BF)
    done[...] = whole
    for k in range(radix):
        piece = total_of(refs[ones + k * twos : ones + (k + 1) * twos])
        if k:
            messages[k - 1][0:rows, :] = whole
            messages[k - 1][rows:, :] = piece.astype(BF)
        else:
            held[...] = piece


def join(first, second, digit, radix):
    (rows, width), part = first[0].shape, rows_of(second) // radix
    specs = [
        pl.BlockSpec((part, width), lambda n, d, k=k, b=b: (b * radix + (d[0] ^ k), 0))
        for k in range(radix)
        for _, b in second
    ]
    outs = [jax.ShapeDtypeStruct((rows, width), BF), jax.ShapeDtypeStruct((part, width), F32)]
    outs += [jax.ShapeDtypeStruct((rows + part, width), BF)] * (radix - 1)
    return pl.pallas_call(
        functools.partial(join_kernel, ones=len(first), twos=len(second), radix=radix),
        grid_spec=pltpu.PrefetchScalarGridSpec(
            num_scalar_prefetch=1,
            grid=(1,),
            in_specs=[fixed((rows, width))] * len(first) + specs,
            out_specs=[fixed(x.shape) for x in outs],
        ),
        out_shape=outs,
        compiler_params=params(),
        cost_estimate=lasting(3),
        name="join",
    )(digit.reshape(1), *first, *([x for x, _ in second] * radix))


def below_kernel(held_ref, *refs, copies):
    *parts, out = refs
    rows = held_ref.shape[0]
    total = held_ref[...]
    for part in parts:
        total = total + part[part.shape[0] - rows :, :].astype(F32)
    for n in range(copies):
        out[n * rows : n * rows + rows, :] = total.astype(BF)


def add_below(held, messages, copies):
    out = jax.ShapeDtypeStruct((copies * held.shape[0], held.shape[1]), BF)
    return pl.pallas_call(
        functools.partial(below_kernel, copies=copies),
        grid=(1,),
        in_specs=[fixed(x.shape) for x in (held, *messages)],
        out_specs=fixed(out.shape),
        out_shape=out,
        compiler_params=params(),
        cost_estimate=lasting(2),
        name="add_below",
    )(held, *messages)


def place_kernel(digit_ref, *refs, radix, sizes, counts):
    parts, outs, vectors = refs[:radix], refs[radix : radix + len(sizes)], refs[radix + len(sizes) :]
    for k in range(radix):

        @pl.when(pl.program_id(0) == k)
        def _():
            at = 0
            for out, size in zip(outs, sizes):
                out[...] = parts[k][at : at + size, :].astype(out.dtype)
                at += size

            if not counts:
                return

            @pl.when(digit_ref[0] == k)
            def _():
                row = at
                for out, count in zip(vectors, counts):
                    whole = jnp.concatenate([parts[k][row + n : row + n + 1, :] for n in range(count)], axis=1)
                    whole = whole.astype(F32)
                    half = whole.shape[1] // 2
                    out[...] = jnp.where(digit_ref[1] == 0, whole[:, :half], whole[:, half:])
                    row += count


def place(parts, digit, sizes, dtype, across=None, core=None, counts=()):
    radix, width = len(parts), parts[0].shape[1]
    below = lambda k, d: (k ^ d[0], 0)
    beside = lambda k, d: (0, k ^ d[0])
    outs = [
        jax.ShapeDtypeStruct((n, width * radix) if i == across else (n * radix, width), dtype)
        for i, n in enumerate(sizes)
    ]
    halves = [jax.ShapeDtypeStruct((1, n * width // 2), F32) for n in counts]
    return pl.pallas_call(
        functools.partial(place_kernel, radix=radix, sizes=sizes, counts=counts),
        grid_spec=pltpu.PrefetchScalarGridSpec(
            num_scalar_prefetch=1,
            grid=(radix,),
            in_specs=[fixed(x.shape) for x in parts],
            out_specs=[
                pl.BlockSpec((n, width), beside if i == across else below) for i, n in enumerate(sizes)
            ]
            + [fixed(x.shape) for x in halves],
        ),
        out_shape=outs + halves,
        compiler_params=params(),
        cost_estimate=lasting(4),
        name="place",
    )(digit.reshape(1) if core is None else jnp.stack([digit, core]), *parts)


def exchange(pieces, here, stride, ranks):
    return [
        lax.ppermute(piece, "ctx", [(i, i ^ ((k + 1) * stride)) for i in range(ranks)])
        for k, piece in enumerate(pieces)
    ]


def stages_of(ranks):
    stages, stride = [], 1
    while stride < ranks:
        radix = 4 if (ranks // stride) % 4 == 0 else 2
        stages.append((stride, radix))
        stride *= radix
    return stages


def after(first, then):
    return lax.optimization_barrier((first, then))[1]


class Reduction:
    def __init__(self, here, ranks, sizes, across):
        self.here, self.ranks, self.sizes, self.across = here, ranks, sizes, across
        self.stages = stages_of(ranks)

    def digit(self, level):
        stride, radix = self.stages[level]
        return (self.here // stride) % radix

    def cut(self, terms, level):
        return cut([(x, 0) for x in terms], self.digit(level), self.stages[level][1], F32)

    def add(self, terms):
        return cut([(x, 0) for x in terms], self.here * 0, 1, BF)[0]

    def scatter(self, pieces, level):
        return [pieces[0]] + exchange(pieces[1:], self.here, self.stages[level][0], self.ranks)

    def trade(self, blocks, level):
        stride, radix = self.stages[level]
        groups = [
            [i + n * stride for n in range(radix)] for i in range(self.ranks) if (i // stride) % radix == 0
        ]
        return lax.all_to_all(blocks, "ctx", split_axis=0, concat_axis=0, axis_index_groups=groups, tiled=True)

    def gather(self, held, level):
        stride, radix = self.stages[level]
        return [held] + exchange([held] * (radix - 1), self.here, stride, self.ranks)

    def place(self, parts, level):
        if level:
            return place(parts, self.digit(level), [parts[0].shape[0]], BF, None)[0]
        return place(parts, self.digit(0), self.sizes, F32, self.across)


def padded(rows, ranks):
    step = 2 * ranks
    return -(-rows // step) * step


def swap_core(x):
    return lax.ppermute(x, "fsdp", SWAP)


def by_core(core, own, other):
    return jnp.where(core == 0, jnp.stack([own, other]), jnp.stack([other, own]))


def next_chip(block, chips, step):
    pairs = [(i, i + 4) for i in range(4 * (chips - 1))]
    return lax.ppermute(block, "ctx", pairs if step > 0 else [(b, a) for a, b in pairs])


def send_window(own, reach, chips, step):
    far = [own]
    for k in range(1, reach + 1):
        if step > 0:
            pairs = [(i, i + 4 * k) for i in range(4 * (chips - k))]
        else:
            pairs = [(i + 4 * k, i) for i in range(4 * (chips - k))]
        far.append(lax.ppermute(own, "ctx", pairs))
    return far


def both_cores(far, core, step):
    near = core == (0 if step > 0 else 1)
    parts = []
    for k in range(len(far) - 1):
        parts += [swap_core(jnp.where(near, far[k], far[k + 1])), far[k + 1]]
    return parts


def shards(
    tokens,
    cotangent,
    lengths,
    deal_order,
    w_query,
    w_key,
    w_value,
    w_out,
    w_up,
    w_down,
    b_query,
    b_value,
    b_out,
    b_up,
    b_down,
    gain_one,
    shift_one,
    gain_two,
    shift_two,
    positions,
):
    block, width = tokens.shape[2], tokens.shape[3]
    ranks = lax.axis_size("ctx")
    chips = ranks // 4
    slot = block // ranks
    rows = 2 * block
    group = ranks * block
    longest = 2 * positions.shape[0]
    reach = longest // (2 * rows)
    here = lax.axis_index("ctx")
    core = lax.axis_index("fsdp")
    chip, micro, stream = here // 4, here % 2, (here // 2) % 2
    base = chip * (2 * rows) + core * rows

    index = lambda i, t: 2 * i + t
    straight, crossing = [], []
    for i in range(ranks):
        c, a, b = i // 4, (i // 2) % 2, i % 2
        for t in range(2):
            straight.append((index(i, t), index(4 * c + 2 * t + b, a)))
            crossing.append((index(i, t), index(4 * c + 2 * t + 1 - b, a)))
    even = here % 2 == 0
    same = jnp.where(even, tokens[0, 0], tokens[1, 0])
    cross = jnp.where(even, tokens[1, 0], tokens[0, 0])
    got_same = lax.ppermute(same, BOTH, straight)
    got_cross = lax.ppermute(cross, BOTH, crossing)
    first_half = jnp.where(micro == 0, got_same, got_cross)
    second_half = jnp.where(micro == 0, got_cross, got_same)
    own = jnp.concatenate([first_half, second_half], axis=0)

    table = jnp.concatenate([deal_order[:, 0], lengths[:, 0]], axis=1)
    table = jnp.where(micro == 0, table[0], table[1])
    table = jnp.where(stream == core, table, swap_core(table))
    order, lens = table[:group], table[group:]

    head = jnp.stack([core, base, jnp.int32(group)]).astype(jnp.int32)
    info = jnp.concatenate([head, lens])

    whole = lambda x: (x, swap_core(x))
    pos, wq, wk, wv = whole(positions), whole(w_query), whole(w_key), whole(w_value)
    vectors = [b_out, b_down, gain_one, shift_one, gain_two, shift_two, b_query, b_value, b_up]
    vec = whole(stack_vectors(vectors, width // 2))
    wo, wu, wd = whole(w_out), whole(w_up), whole(w_down)

    mine = order.reshape(ranks, ranks, slot)
    mine = lax.dynamic_slice_in_dim(mine, 4 * chip + 2 * core, 2, axis=1).reshape(rows) - base
    mine = (mine.reshape(1, rows), mine.reshape(rows, 1))
    dealt = cotangent[:, 0].reshape(2, chips, 2, 2 * slot, width)
    keep = jnp.where(core == 0, dealt[:, :, 0], dealt[:, :, 1])
    give = jnp.where(core == 0, dealt[:, :, 1], dealt[:, :, 0])
    streams = by_core(core, keep, swap_core(give))
    sends = jnp.transpose(streams, (2, 0, 1, 3, 4)).reshape(rows, width)
    arrived = lax.all_to_all(sends, "ctx", split_axis=0, concat_axis=0, tiled=True)

    fixed_args = (pos, wk, wv, wq, vec)
    far = send_window(own, reach, chips, 1)
    own = after(arrived, own)
    k, v, q, hidden, low = project(info, [own], 0, True, *fixed_args)
    mine, far[1:] = lax.optimization_barrier((mine, after(k, far[1:])))

    earlier = both_cores(far, core, 1)[::-1]
    before = len(earlier) * rows
    kp, vp = project(info, earlier, -before, False, *fixed_args)
    far_q = send_window(after(kp, q), reach, chips, -1)
    att, exact, logs, log_stats = attend_forward(info, q, kp, k, vp, v)
    leaving, da_msg, dz1, active, df, h1, du, do, sums = feed_forward(
        info, att, exact, log_stats, hidden, arrived, mine, wo, wu, wd, vec
    )
    da_msg, do, leaving = after(far_q[1:], (da_msg, do, leaving))
    far_da = [da_msg, next_chip(da_msg, chips, -1)]

    half = width // 2
    units = 2 * b_up.shape[0]
    sizes = [units // 8, half, width // 8]
    quarter = padded(sum(sizes), ranks)
    sizes_last = [width // 8, width // 8, width // 8, longest // 8]
    quarter_last = padded(sum(sizes_last) + 16, ranks)
    one = Reduction(here, ranks, sizes, 1)
    two = Reduction(here, ranks, sizes_last, None)
    levels = len(one.stages)

    pairs = width // 256
    query_args = (q, kp, k, vp, v, logs, da_msg)
    dq_first = attend_query(info, 0, pairs, *query_args, exact)
    do = after(dq_first, do)
    keep, give = ffn_grads(info, att, do, active, df, h1, du, quarter)
    give = after(far_da[1], give)
    for _ in range(reach - 1):
        far_da.append(next_chip(far_da[-1], chips, -1))
    pieces = one.cut([keep, swap_core(give)], 0)
    terms = one.scatter(pieces, 0)
    dq_second = attend_query(info, pairs, pairs, *query_args, after(pieces, exact))
    far_da[1:], far_q[1:] = after(dq_second, (far_da[1:], far_q[1:]))
    later_da = [da_msg] + both_cores(far_da, core, -1)
    later_q = [q] + both_cores(far_q, core, -1)
    dqs = (dq_first, dq_second)
    keep, give, dh0_low = last(
        info, later_q, later_da, k, v, low, dqs, dz1, sums, wq, wk, wv, quarter_last, longest
    )

    keep, give = after(terms[1:], (keep, give))
    terms_last = [keep, swap_core(give)]
    end = levels - 1
    for level in range(end):
        pieces = one.cut(terms, level + 1)
        terms = one.scatter(pieces, level + 1)
        pieces_last = two.cut(after(pieces, terms_last), level)
        terms_last = two.scatter(pieces_last, level)
    terms_last = [(x, 0) for x in terms_last]
    stride, radix = one.stages[end]
    held, held_last, *messages = join(terms, terms_last, one.digit(end), radix)
    got = exchange(messages, here, stride, ranks)
    dh0_low = after(held, dh0_low)

    back_same = jnp.where(micro == 0, dh0_low[:block], dh0_low[block:])
    back_cross = jnp.where(micro == 0, dh0_low[block:], dh0_low[:block])
    home_same = lax.ppermute(back_same, BOTH, [(b, a) for a, b in straight])
    home_cross = lax.ppermute(back_cross, BOTH, [(b, a) for a, b in crossing])
    grad_tokens = jnp.where(
        even, jnp.stack([home_same, home_cross]), jnp.stack([home_cross, home_same])
    )[:, None]

    got = after((home_same, home_cross), got)
    held = place([held] + got, one.digit(end), [held.shape[0]], BF, None)[0]
    held_last = two.trade(add_below(held_last, after(held, got), radix), end)
    for level in reversed(range(1, end)):
        held = one.place(one.gather(held, level), level)
        held_last = two.place(two.gather(held_last, level), level)
    parts = one.gather(held, 0)
    held_last = after(parts[1:], held_last)
    parts_last = two.gather(held_last, 0)
    held = one.place(parts, 0)
    leaving = after(parts[1:], leaving)
    landed = lax.all_to_all(leaving, "ctx", split_axis=0, concat_axis=0, tiled=True)

    landed = landed.reshape(chips, 2, 2, 2 * slot, width)
    keep = jnp.where(core == 0, landed[:, 0], landed[:, 1])
    give = jnp.where(core == 0, landed[:, 1], landed[:, 0])
    sides = by_core(core, keep, swap_core(give))
    output = jnp.transpose(sides, (2, 1, 0, 3, 4)).reshape(2, 1, block, width)
    counts = [1] * 7 + [units // width, 1]
    results = place(parts_last, two.digit(0), sizes_last, F32, None, core, counts)
    g_down, g_up, g_out = held
    g_key, g_value, g_query, g_pos = results[:4]
    gb_down, gg1, gs1, gg2, gs2, gb_out, gb_query, gb_up, gb_value = (x.reshape(-1) for x in results[4:])

    return (
        output,
        grad_tokens,
        g_query,
        g_key,
        g_value,
        g_out,
        g_up,
        g_down,
        gb_query,
        gb_value,
        gb_out,
        gb_up,
        gb_down,
        gg1,
        gs1,
        gg2,
        gs2,
        g_pos,
    )


def solution(mesh):
    data = P(None, "fsdp", "ctx", None)
    groups = P(None, "fsdp", None)
    matrix, vector = P("fsdp", None), P("fsdp")
    return jax.shard_map(
        shards,
        mesh=mesh,
        in_specs=(data, data, groups, groups) + (matrix,) * 6 + (vector,) * 9 + (matrix,),
        out_specs=(data, data) + (matrix,) * 6 + (vector,) * 9 + (matrix,),
        check_vma=False,
    )
```

```python
import functools

import jax
import jax.numpy as jnp
from jax import lax
from jax.experimental import pallas as pl
from jax.experimental.pallas import tpu as pltpu
from jax.sharding import PartitionSpec as P

HEADS = 8
epsilon = 1e-05
gelu_coeff = 0.7978845608028654
cubic_coeff = 0.044715
BF = jnp.bfloat16
F32 = jnp.float32
SWAP = ((0, 1), (1, 0))
BOTH = ("ctx", "fsdp")
FAR = 1 << 30


def dot(a, b):
    return jnp.dot(a, b, preferred_element_type=F32)


def dot_tn(a, b):
    return lax.dot_general(a, b, (((0,), (0,)), ((), ())), preferred_element_type=F32)


def dot_nt(a, b):
    return lax.dot_general(a, b, (((1,), (1,)), ((), ())), preferred_element_type=F32)


def gelu_parts(u):
    inner = gelu_coeff * (u + cubic_coeff * u * u * u)
    bent = jnp.tanh(inner)
    value = 0.5 * u * (1.0 + bent)
    slope = 0.5 * (1.0 + bent) + 0.5 * u * (1.0 - bent * bent) * gelu_coeff * (
        1.0 + 3.0 * cubic_coeff * u * u
    )
    return value, slope


def normalize(z):
    center = z - jnp.mean(z, axis=-1, keepdims=True)
    inv = lax.rsqrt(jnp.mean(center * center, axis=-1, keepdims=True) + epsilon)
    return center * inv, inv


def normalize_back(t, normed, inv):
    return inv * (
        t
        - jnp.mean(t, axis=-1, keepdims=True)
        - normed * jnp.mean(t * normed, axis=-1, keepdims=True)
    )


def first_places(info, spots):
    first, end = jnp.zeros_like(spots), 0
    for n in range(3, info.shape[0]):
        end = end + info[n]
        first = first + jnp.where(spots >= end, info[n], 0)
    return first


def lay(info, whole, own, other):
    n = own.shape[0]
    mine = info[0] == 0
    whole[0:n, :] = jnp.where(mine, own[...], other[...])
    whole[n : 2 * n, :] = jnp.where(mine, other[...], own[...])


def full_row(info, own, other, at, count=1):
    mine = info[0] == 0
    rows = [x[at + n : at + n + 1, :] for x in (own, other) for n in range(count)]
    first = [jnp.where(mine, rows[n], rows[count + n]) for n in range(count)]
    second = [jnp.where(mine, rows[count + n], rows[n]) for n in range(count)]
    return jnp.concatenate(first + second, axis=1)


def stack_vectors(vectors, width):
    row, at = iota((16, width), 0), 0
    table = jnp.zeros((16, width), BF)
    for x in vectors:
        for n in range(x.shape[0] // width):
            part = x[n * width : n * width + width]
            table = jnp.where(row == at, part[None, :], table)
            at += 1
    return table.astype(F32)


def iota(shape, axis):
    return lax.broadcasted_iota(jnp.int32, shape, axis)


def params(cols=0):
    return pltpu.CompilerParams(vmem_limit_bytes=(32 if cols <= 2048 else 56) * 1024 * 1024)


def lasting(us):
    return pl.CostEstimate(flops=us, transcendentals=0, bytes_accessed=us)


def fixed(shape):
    return pl.BlockSpec(shape, lambda *_: (0,) * len(shape), pipeline_mode=pl.Buffered(1))


def paired(rows):
    return pl.BlockSpec((rows, 128), lambda p, *_: (0, p))


def project_kernel(info, *refs, blocks, offset, own):
    toks = refs[:blocks]
    pos_a, pos_b, wk_a, wk_b, wv_a, wv_b, wq_a, wq_b, vec_a, vec_b = refs[blocks : blocks + 10]
    outs = refs[blocks + 10 :]
    k_ref, v_ref = outs[:2]
    wk, wv, wq, tok = outs[-4:]
    step = pl.program_id(0)
    rows = tok.shape[0]

    @pl.when(step == 0)
    def _():
        lay(info, wk, wk_a, wk_b)
        lay(info, wv, wv_a, wv_b)
        if own:
            lay(info, wq, wq_a, wq_b)

    for n in range(blocks):

        @pl.when(step == n)
        def _():
            tok[...] = toks[n][...]

    spots = info[1] + offset + step * rows + iota((rows, 1), 0)
    place = spots - first_places(info, spots)
    hidden = tok[...].astype(F32)
    half = pos_a.shape[0]
    chunk = min(half, 512)
    for part, begin in ((pos_a, info[0] * half), (pos_b, (1 - info[0]) * half)):
        for at in range(0, half, chunk):
            hot = (place - begin - at == iota((rows, chunk), 1)).astype(F32).astype(BF)
            hidden = hidden + dot(hot, part[at : at + chunk, :])
    low = hidden.astype(BF)
    k_ref[...] = dot(low, wk[...]).astype(BF)
    v_ref[...] = (dot(low, wv[...]) + full_row(info, vec_a, vec_b, 7)).astype(BF)
    if own:
        q_ref, hidden_ref, low_ref = outs[2:5]
        q_ref[...] = ((dot(low, wq[...]) + full_row(info, vec_a, vec_b, 6)).astype(BF).astype(F32) * 0.125).astype(BF)
        hidden_ref[...] = hidden
        low_ref[...] = low


def project(info, toks, offset, own, pos, wk, wv, wq, vec):
    rows, width = toks[0].shape
    blocks = len(toks)
    tall = pl.BlockSpec((rows, width), lambda n, *_: (n, 0))
    flat = jax.ShapeDtypeStruct((rows * blocks, width), BF)
    square = pltpu.VMEM((width, width), BF)
    args = (*toks, *pos, *wk, *wv, *wq, *vec)
    return pl.pallas_call(
        functools.partial(project_kernel, blocks=blocks, offset=offset, own=own),
        grid_spec=pltpu.PrefetchScalarGridSpec(
            num_scalar_prefetch=1,
            grid=(blocks,),
            in_specs=[fixed(x.shape) for x in args],
            out_specs=[tall] * (5 if own else 2),
            scratch_shapes=[square, square, square, pltpu.VMEM((rows, width), BF)],
        ),
        out_shape=[flat] * 3 + [jax.ShapeDtypeStruct((rows, width), F32), flat] if own else [flat] * 2,
        compiler_params=pltpu.CompilerParams(vmem_limit_bytes=60 * 1024 * 1024),
        cost_estimate=lasting(2 * blocks + 2),
        name="project",
    )(info, *args)


def stat_rows(table):
    high = table.astype(BF).astype(F32)
    middle = (table - high).astype(BF).astype(F32)
    low = table - high - middle
    count = table.shape[1] // 128
    rows = [
        part[half : half + 1, 128 * n : 128 * n + 128]
        for part in (high, middle, low)
        for half in range(2)
        for n in range(count)
    ]
    rows.append(jnp.zeros((16 - len(rows), 128), F32))
    return jnp.concatenate(rows, axis=0).astype(BF)


def stat_row(rows16, half, queries):
    count = queries // 128
    wide = rows16.astype(F32)
    total = wide[0 : 2 * count] + wide[2 * count : 4 * count] + wide[4 * count : 6 * count]
    return jnp.concatenate([total[half * count + n : half * count + n + 1] for n in range(count)], axis=1)


def chunks_of(cols):
    step = cols if cols <= 2048 else 768
    return [slice(at, min(at + step, cols)) for at in range(0, cols, step)]


def bias_scratch(rows, cols):
    return pltpu.VMEM((rows, cols) if len(chunks_of(cols)) == 1 else (8, 128), F32)


def query_bias(info, rows, before, chunk):
    spots = info[1] + iota((rows, 1), 0)
    first = first_places(info, spots) - (info[1] - before)
    last = iota((rows, 1), 0) + before
    col = iota((rows, chunk.stop - chunk.start), 1) + chunk.start
    return jnp.where((col >= first) & (col <= last), 0.0, -1e30)


def key_bias(info, rows, chunk):
    spots = info[1] + chunk.start + iota((1, chunk.stop - chunk.start), 1)
    first = jnp.where(spots < info[2], first_places(info, spots) - info[1], FAR)
    shape = (rows, chunk.stop - chunk.start)
    row = iota(shape, 0)
    return jnp.where((row >= first) & (row <= iota(shape, 1) + chunk.start), 0.0, -1e30)


def forward_kernel(info, q_ref, kp_ref, k_ref, vp_ref, v_ref, a_ref, exact_ref, log_ref, stat_ref, bias, keys, values):
    rows, before = q_ref.shape[0], kp_ref.shape[0]

    chunks = chunks_of(keys.shape[0])
    make_bias = functools.partial(query_bias, info, rows, before)

    @pl.when(pl.program_id(0) == 0)
    def _():
        if len(chunks) == 1:
            bias[...] = make_bias(chunks[0])

    keys[0:before, :] = kp_ref[...]
    keys[before:, :] = k_ref[...]
    values[0:before, :] = vp_ref[...]
    values[before:, :] = v_ref[...]
    logs = []
    for half in range(2):
        lanes = slice(64 * half, 64 * half + 64)


        def scores_of(chunk):
            mask = bias[...] if len(chunks) == 1 else make_bias(chunk)
            return dot_nt(q_ref[:, lanes], keys[chunk, lanes]) + mask

        if len(chunks) == 1:
            scores = scores_of(chunks[0])
            top = jnp.max(scores, axis=1, keepdims=True)
            raised = jnp.exp(scores - top)
            total = jnp.sum(raised, axis=1, keepdims=True)
            probs = raised * (1.0 / total)
            low = probs.astype(BF)
            attended = dot(low, values[:, lanes])
            weight = jnp.sum(low.astype(F32), axis=1, keepdims=True)
        else:
            top = jnp.full((rows, 1), -1e30, F32)
            for chunk in chunks:
                top = jnp.maximum(top, jnp.max(scores_of(chunk), axis=1, keepdims=True))
            total = jnp.zeros((rows, 1), F32)
            for chunk in chunks:
                total = total + jnp.sum(jnp.exp(scores_of(chunk) - top), axis=1, keepdims=True)
            attended, weight = jnp.zeros((rows, 64), F32), jnp.zeros((rows, 1), F32)
            for chunk in chunks:
                probs = jnp.exp(scores_of(chunk) - top) * (1.0 / total)
                low = probs.astype(BF)
                attended = attended + dot(low, values[chunk, lanes])
                weight = weight + jnp.sum(low.astype(F32), axis=1, keepdims=True)
        a_ref[:, lanes] = attended.astype(BF)
        exact_ref[:, lanes] = attended / weight
        logs.append(jnp.broadcast_to(top + jnp.log(total), (rows, 64)))
    wide = jnp.concatenate(logs, axis=1)
    log_ref[...] = wide
    turned = wide.T
    stat_ref[...] = stat_rows(jnp.concatenate([turned[0:1], turned[64:65]], axis=0))


def attend_forward(info, q, kp, k, vp, v):
    rows, width = q.shape
    before = kp.shape[0]
    cols = before + rows
    return pl.pallas_call(
        forward_kernel,
        grid_spec=pltpu.PrefetchScalarGridSpec(
            num_scalar_prefetch=1,
            grid=(width // 128,),
            in_specs=[paired(x.shape[0]) for x in (q, kp, k, vp, v)],
            out_specs=[paired(rows), paired(rows), paired(rows), paired(16)],
            scratch_shapes=[
                bias_scratch(rows, cols),
                pltpu.VMEM((cols, 128), BF),
                pltpu.VMEM((cols, 128), BF),
            ],
        ),
        out_shape=[
            jax.ShapeDtypeStruct((rows, width), BF),
            jax.ShapeDtypeStruct((rows, width), F32),
            jax.ShapeDtypeStruct((rows, width), F32),
            jax.ShapeDtypeStruct((16, width), BF),
        ],
        compiler_params=params(cols),
        cost_estimate=lasting(12),
        name="attend_forward",
    )(info, q, kp, k, vp, v)


def ffn_kernel(
    info, a_ref, exact_ref, stat_ref, hidden_ref, arrived_ref, row_ref, col_ref, wo_a, wo_b, wu_a, wu_b, wd_a, wd_b, vec_a, vec_b,
    leaving_ref, msg_ref, dz1_ref, active_ref, df_ref, h1_ref, du_ref, do_ref, sums_ref,
    wo, wu, wd, slopes, stats,
):
    lay(info, wo, wo_a, wo_b)
    lay(info, wu, wu_a, wu_b)
    lay(info, wd, wd_a, wd_b)
    rows, width = hidden_ref.shape
    hidden_units = wu.shape[1]
    bo, bd, g1, s1, g2, s2 = (full_row(info, vec_a, vec_b, n) for n in range(6))
    bu = full_row(info, vec_a, vec_b, 8, hidden_units // width)
    pick = (iota((rows, rows), 0) == row_ref[...]).astype(F32).astype(BF)
    pick_back = (col_ref[...] == iota((rows, rows), 1)).astype(F32).astype(BF)
    dy = dot(pick, arrived_ref[...])

    n1, r1 = normalize(hidden_ref[...] + dot(a_ref[...], wo[...]) + bo)
    h1 = n1 * g1 + s1
    h1_low = h1.astype(BF)
    h1_ref[...] = h1_low
    z2 = h1 + bd
    for at in range(0, hidden_units, width):
        block = slice(at, at + width)
        value, slope = gelu_parts(dot(h1_low, wu[:, block]) + bu[:, block])
        slopes[:, block] = slope
        low = value.astype(BF)
        active_ref[:, block] = low
        z2 = z2 + dot(low, wd[block, :])
    n2, r2 = normalize(z2)
    leaving_ref[...] = dot(pick_back, (n2 * g2 + s2).astype(BF)).astype(BF)

    def add(x):
        return jnp.sum(x, axis=0, keepdims=True)

    dz2 = normalize_back(dy * g2, n2, r2)
    df = dz2.astype(BF)
    df_ref[...] = df
    sums_ref[0:1, :] = add(df.astype(F32))
    sums_ref[3:4, :] = add(dy * n2)
    sums_ref[4:5, :] = add(dy)
    dh1 = dz2
    for at in range(0, hidden_units, width):
        block = slice(at, at + width)
        du = (dot_nt(df, wd[block, :]) * slopes[:, block]).astype(BF)
        du_ref[:, block] = du
        n = 7 + at // width
        sums_ref[n : n + 1, :] = add(du.astype(F32))
        dh1 = dh1 + dot_nt(du, wu[:, block])
    dz1 = normalize_back(dh1 * g1, n1, r1)
    dz1_ref[...] = dz1
    sums_ref[1:2, :] = add(dh1 * n1)
    sums_ref[2:3, :] = add(dh1)
    do = dz1.astype(BF)
    do_ref[...] = do
    sums_ref[5:6, :] = add(do.astype(F32))
    sums_ref[6:7, :] = jnp.zeros((1, width), F32)
    sums_ref[11:16, :] = jnp.zeros((5, width), F32)
    da = dot_nt(do, wo[...]).astype(BF)
    msg_ref[0:rows, :] = da
    terms = da.astype(F32) * exact_ref[...]
    head = iota((HEADS, width), 0)
    lane = iota((HEADS, width), 1) // (width // HEADS)
    ones = (head == lane).astype(F32).astype(BF)
    delta = jnp.zeros((HEADS, rows), F32)
    for _ in range(3):
        part = terms.astype(BF)
        terms = terms - part.astype(F32)
        delta = delta + dot_nt(ones, part)
    for p in range(HEADS // 2):
        stats[:, 128 * p : 128 * p + 128] = stat_rows(delta[2 * p : 2 * p + 2, :])
    msg_ref[rows : rows + 16, :] = stat_ref[...]
    msg_ref[rows + 16 : rows + 32, :] = stats[...]


def feed_forward(info, a, exact, log_stats, hidden, arrived, mine, wo, wu, wd, vec):
    rows, width = hidden.shape
    units = wu[0].shape[1]
    args = (a, exact, log_stats, hidden, arrived, *mine, *wo, *wu, *wd, *vec)
    low = jax.ShapeDtypeStruct((rows, width), BF)
    tall = jax.ShapeDtypeStruct((rows, units), BF)
    outs = [
        low,
        jax.ShapeDtypeStruct((rows + 32, width), BF),
        jax.ShapeDtypeStruct((rows, width), F32),
        tall,
        low,
        low,
        tall,
        low,
        jax.ShapeDtypeStruct((16, width), F32),
    ]
    return pl.pallas_call(
        ffn_kernel,
        grid_spec=pltpu.PrefetchScalarGridSpec(
            num_scalar_prefetch=1,
            grid=(1,),
            in_specs=[fixed(x.shape) for x in args],
            out_specs=[fixed(x.shape) for x in outs],
            scratch_shapes=[
                pltpu.VMEM((width, width), BF),
                pltpu.VMEM((width, units), BF),
                pltpu.VMEM((units, width), BF),
                pltpu.VMEM((rows, units), F32),
                pltpu.VMEM((16, width), BF),
            ],
        ),
        out_shape=outs,
        compiler_params=params(),
        cost_estimate=lasting(10),
        name="feed_forward",
    )(info, *args)


def keep_or_send(info, half, mine, send, at, value):
    at, value = pl.multiple_of(at, 8), value.astype(BF)

    @pl.when(info[0] == half)
    def _():
        mine[pl.ds(at, value.shape[0]), :] = value

    @pl.when(info[0] != half)
    def _():
        send[pl.ds(at, value.shape[0]), :] = value


def split_halves(info, mine, send, starts, value):
    half, step = value.shape[0] // 2, value.shape[0] // 8
    first = info[0] == 0
    own = jnp.where(first, value[:half], value[half:]).astype(BF)
    other = jnp.where(first, value[half:], value[:half]).astype(BF)
    for n, at in enumerate(starts):
        mine[at : at + step, :] = own[n * step : n * step + step]
        send[at : at + step, :] = other[n * step : n * step + step]


def grads_kernel(
    info, a_own, a_other, do_ref, active_own, active_other, df_ref, h1_ref, du_ref, mine, send, *, quarter
):
    width = df_ref.shape[1]
    step = pl.program_id(0)
    part = active_own.shape[1]
    mine[0:part, :] = dot_tn(active_own[...], df_ref[...]).astype(BF)
    send[0:part, :] = dot_tn(active_other[...], df_ref[...]).astype(BF)
    up = dot_tn(h1_ref[...], du_ref[...])
    low, high = up[: width // 2].astype(BF), up[width // 2 :].astype(BF)
    at = part + width // 2
    mine[part:at, :] = jnp.where(info[0] == 0, low, high)
    send[part:at, :] = jnp.where(info[0] == 0, high, low)
    for out, a_ref in ((mine, a_own), (send, a_other)):
        both = dot_tn(a_ref[...], do_ref[...]).astype(BF)
        out[at : at + 64, :] = jnp.where(step % 2 == 0, both[:64], both[64:])
        if quarter > at + 64:
            out[at + 64 :, :] = jnp.zeros((quarter - at - 64, width), BF)


def ffn_grads(info, a, do, active, df, h1, du, quarter):
    rows, width = df.shape
    units = active.shape[1]
    out = jax.ShapeDtypeStruct((4 * quarter, width), BF)
    columns = lambda n, index: pl.BlockSpec((rows, n), lambda j, info: (0, index(j, info[0])))
    return pl.pallas_call(
        functools.partial(grads_kernel, quarter=quarter),
        grid_spec=pltpu.PrefetchScalarGridSpec(
            num_scalar_prefetch=1,
            grid=(4,),
            in_specs=[
                columns(128, lambda j, core: core * 2 + j // 2),
                columns(128, lambda j, core: (1 - core) * 2 + j // 2),
                fixed(do.shape),
                columns(units // 8, lambda j, core: core * 4 + j),
                columns(units // 8, lambda j, core: (1 - core) * 4 + j),
                fixed(df.shape),
                fixed(h1.shape),
                columns(units // 4, lambda j, core: j),
            ],
            out_specs=[pl.BlockSpec((quarter, width), lambda j, *_: (j, 0))] * 2,
        ),
        out_shape=[out, out],
        compiler_params=params(),
        cost_estimate=lasting(10),
        name="ffn_grads",
    )(info, a, a, do, active, active, df, h1, du)


def query_kernel(
    info, q_ref, kp_ref, k_ref, vp_ref, v_ref, log_ref, da_ref, exact_ref, dq_ref, bias, keys, values
):
    rows, before = q_ref.shape[0], kp_ref.shape[0]
    chunks = chunks_of(keys.shape[0])
    make_bias = functools.partial(query_bias, info, rows, before)

    @pl.when(pl.program_id(0) == 0)
    def _():
        if len(chunks) == 1:
            bias[...] = make_bias(chunks[0])

    keys[0:before, :] = kp_ref[...]
    keys[before:, :] = k_ref[...]
    values[0:before, :] = vp_ref[...]
    values[before:, :] = v_ref[...]
    for half in range(2):
        lanes = slice(64 * half, 64 * half + 64)
        delta = jnp.sum(da_ref[:, lanes].astype(F32) * exact_ref[:, lanes], axis=1, keepdims=True)
        dq = jnp.zeros((rows, 64), F32)
        for chunk in chunks:
            mask = bias[...] if len(chunks) == 1 else make_bias(chunk)
            scores = dot_nt(q_ref[:, lanes], keys[chunk, lanes]) + mask
            probs = jnp.exp(scores - log_ref[:, 64 * half : 64 * half + 1])
            dp = dot_nt(da_ref[:, lanes], values[chunk, lanes])
            ds = (probs * (dp - delta)).astype(BF)
            dq = dq + dot(ds, keys[chunk, lanes])
        dq_ref[:, lanes] = (dq * 0.125).astype(BF)


def attend_query(info, first, count, q, kp, k, vp, v, logs, da, exact):
    rows = q.shape[0]
    before = kp.shape[0]
    cols = before + rows
    some = lambda n: pl.BlockSpec((n, 128), lambda p, *_: (0, p + first))
    return pl.pallas_call(
        query_kernel,
        grid_spec=pltpu.PrefetchScalarGridSpec(
            num_scalar_prefetch=1,
            grid=(count,),
            in_specs=[some(x.shape[0]) for x in (q, kp, k, vp, v, logs)] + [some(rows), some(rows)],
            out_specs=paired(rows),
            scratch_shapes=[
                bias_scratch(rows, cols),
                pltpu.VMEM((cols, 128), BF),
                pltpu.VMEM((cols, 128), BF),
            ],
        ),
        out_shape=jax.ShapeDtypeStruct((rows, 128 * count), BF),
        compiler_params=params(cols),
        cost_estimate=lasting(5),
        name="attend_query",
    )(info, q, kp, k, vp, v, logs, da, exact)


def last_kernel(info, *refs, reach, quarter, table):
    count = 2 * reach + 1
    q_parts, da_parts = refs[:count], refs[count : 2 * count]
    k_ref, v_ref, low_ref, dq_a, dq_b, dz1_ref, sums_ref, wq_a, wq_b, wk_a, wk_b, wv_a, wv_b = refs[2 * count : 2 * count + 13]
    mine, send, dh_out, bias, queries, grads, dk_all, dv_all, wq, wk, wv = refs[2 * count + 13 :]
    rows, width = low_ref.shape
    cols = queries.shape[0]
    step = pl.program_id(0)

    chunks = chunks_of(cols)
    make_bias = functools.partial(key_bias, info, rows)

    @pl.when(step == 0)
    def _():
        lay(info, wq, wq_a, wq_b)
        lay(info, wk, wk_a, wk_b)
        lay(info, wv, wv_a, wv_b)
        if len(chunks) == 1:
            bias[...] = make_bias(chunks[0])

    for n in range(count):
        queries[n * rows : n * rows + rows, :] = q_parts[n][...]
        grads[n * rows : n * rows + rows, :] = da_parts[n][0:rows, :]
    dks, dvs = [], []
    for half in range(2):
        lanes = slice(64 * half, 64 * half + 64)
        logs = jnp.concatenate([stat_row(x[rows : rows + 16, :], half, rows) for x in da_parts], axis=1)
        delta = jnp.concatenate([stat_row(x[rows + 16 : rows + 32, :], half, rows) for x in da_parts], axis=1)
        dk, dv = jnp.zeros((rows, 64), F32), jnp.zeros((rows, 64), F32)
        for chunk in chunks:
            mask = bias[...] if len(chunks) == 1 else make_bias(chunk)
            scores = dot_nt(k_ref[:, lanes], queries[chunk, lanes]) + mask
            probs = jnp.exp(scores - logs[:, chunk])
            dv = dv + dot(probs.astype(BF), grads[chunk, lanes])
            dp = dot_nt(v_ref[:, lanes], grads[chunk, lanes])
            ds = (probs * (dp - delta[:, chunk])).astype(BF)
            dk = dk + dot(ds, queries[chunk, lanes])
        dks.append(dk.astype(BF))
        dvs.append(dv.astype(BF))
    dk_pair, dv_pair = jnp.concatenate(dks, axis=1), jnp.concatenate(dvs, axis=1)
    for n in range(width // 128):

        @pl.when(step == n)
        def _():
            dk_all[:, 128 * n : 128 * n + 128] = dk_pair
            dv_all[:, 128 * n : 128 * n + 128] = dv_pair

    @pl.when(step == pl.num_programs(0) - 1)
    def _():
        dk, dv = dk_all[...], dv_all[...]
        step_rows = width // 8
        split_halves(info, mine, send, [n * quarter for n in range(4)], dot_tn(low_ref[...], dk))
        split_halves(info, mine, send, [n * quarter + step_rows for n in range(4)], dot_tn(low_ref[...], dv))
        dq = jnp.concatenate([dq_a[...], dq_b[...]], axis=1)
        split_halves(info, mine, send, [n * quarter + 2 * step_rows for n in range(4)], dot_tn(low_ref[...], dq))
        dh = dz1_ref[...] + dot_nt(dq, wq[...]) + dot_nt(dk, wk[...]) + dot_nt(dv, wv[...])
        dh_out[...] = dh.astype(BF)
        parts = []
        for _ in range(3):
            parts.append(dh.astype(BF))
            dh = dh - parts[-1].astype(F32)
        spots = info[1] + iota((1, rows), 1)
        place = spots - first_places(info, spots)
        base = 3 * step_rows
        fourth = table // 8
        for half in range(2):
            for n in range(4):
                hot = (place - (half * 4 + n) * fourth == iota((fourth, rows), 0)).astype(F32).astype(BF)
                total = dot(hot, parts[0]) + dot(hot, parts[1]) + dot(hot, parts[2])
                keep_or_send(info, half, mine, send, n * quarter + base, total)
        base += fourth
        spare = quarter - base
        for n in range(4):
            mine[n * quarter + base : (n + 1) * quarter, :] = jnp.zeros((spare, width), BF)
            send[n * quarter + base : (n + 1) * quarter, :] = jnp.zeros((spare, width), BF)
        total_v = jnp.sum(dv.astype(F32), axis=0, keepdims=True)
        total_q = jnp.sum(dq.astype(F32), axis=0, keepdims=True)
        row = iota(sums_ref.shape, 0)
        total = jnp.where(row == 6, total_q, jnp.where(row == 11, total_v, sums_ref[...])).astype(BF)
        mine[base : base + 16, :] = total
        send[base : base + 16, :] = total


def last(info, q_parts, da_parts, k, v, low, dqs, dz1, sums, wq, wk, wv, quarter, table):
    rows, width = k.shape
    count = len(q_parts)
    cols = count * rows
    outs = [
        jax.ShapeDtypeStruct((4 * quarter, width), BF),
        jax.ShapeDtypeStruct((4 * quarter, width), BF),
        jax.ShapeDtypeStruct((rows, width), BF),
    ]
    rest = (low, *dqs, dz1, sums, *wq, *wk, *wv)
    return pl.pallas_call(
        functools.partial(last_kernel, reach=count // 2, quarter=quarter, table=table),
        grid_spec=pltpu.PrefetchScalarGridSpec(
            num_scalar_prefetch=1,
            grid=(width // 128,),
            in_specs=[paired(x.shape[0]) for x in (*q_parts, *da_parts, k, v)] + [fixed(x.shape) for x in rest],
            out_specs=[fixed(x.shape) for x in outs],
            scratch_shapes=[
                bias_scratch(rows, cols),
                pltpu.VMEM((cols, 128), BF),
                pltpu.VMEM((cols, 128), BF),
                pltpu.VMEM((rows, width), BF),
                pltpu.VMEM((rows, width), BF),
                pltpu.VMEM((width, width), BF),
                pltpu.VMEM((width, width), BF),
                pltpu.VMEM((width, width), BF),
            ],
        ),
        out_shape=outs,
        compiler_params=params(cols),
        cost_estimate=lasting(15),
        name="last",
    )(info, *q_parts, *da_parts, k, v, *rest)


def cut_kernel(digit_ref, *refs, terms, radix):
    ins, outs = refs[: terms * radix], refs[terms * radix :]
    for k in range(radix):
        total = ins[k * terms][...].astype(F32)
        for n in range(1, terms):
            total = total + ins[k * terms + n][...].astype(F32)
        outs[k][...] = total.astype(outs[k].dtype)


def rows_of(terms):
    return terms[0][0].shape[0] // (1 + max(block for _, block in terms))


def cut(terms, digit, radix, kept):
    rows, width = rows_of(terms) // radix, terms[0][0].shape[1]
    subs = max(n for n in (1, 2, 3, 4) if rows % (8 * n) == 0 and rows // n >= 64 or n == 1)
    specs = [
        pl.BlockSpec((rows // subs, width), lambda n, d, k=k, b=b: ((b * radix + (d[0] ^ k)) * subs + n, 0))
        for k in range(radix)
        for _, b in terms
    ]
    return pl.pallas_call(
        functools.partial(cut_kernel, terms=len(terms), radix=radix),
        grid_spec=pltpu.PrefetchScalarGridSpec(
            num_scalar_prefetch=1,
            grid=(subs,),
            in_specs=specs,
            out_specs=[pl.BlockSpec((rows // subs, width), lambda n, d: (n, 0))] * radix,
        ),
        out_shape=[jax.ShapeDtypeStruct((rows, width), BF if k else kept) for k in range(radix)],
        compiler_params=params(),
        cost_estimate=lasting(3),
        name="cut",
    )(digit.reshape(1), *([x for x, _ in terms] * radix))


def total_of(refs):
    total = refs[0][...].astype(F32)
    for ref in refs[1:]:
        total = total + ref[...].astype(F32)
    return total


def join_kernel(digit_ref, *refs, ones, twos, radix):
    done, held, *messages = refs[ones + twos * radix :]
    rows = done.shape[0]
    whole = total_of(refs[:ones]).astype(BF)
    done[...] = whole
    for k in range(radix):
        piece = total_of(refs[ones + k * twos : ones + (k + 1) * twos])
        if k:
            messages[k - 1][0:rows, :] = whole
            messages[k - 1][rows:, :] = piece.astype(BF)
        else:
            held[...] = piece


def join(first, second, digit, radix):
    (rows, width), part = first[0].shape, rows_of(second) // radix
    specs = [
        pl.BlockSpec((part, width), lambda n, d, k=k, b=b: (b * radix + (d[0] ^ k), 0))
        for k in range(radix)
        for _, b in second
    ]
    outs = [jax.ShapeDtypeStruct((rows, width), BF), jax.ShapeDtypeStruct((part, width), F32)]
    outs += [jax.ShapeDtypeStruct((rows + part, width), BF)] * (radix - 1)
    return pl.pallas_call(
        functools.partial(join_kernel, ones=len(first), twos=len(second), radix=radix),
        grid_spec=pltpu.PrefetchScalarGridSpec(
            num_scalar_prefetch=1,
            grid=(1,),
            in_specs=[fixed((rows, width))] * len(first) + specs,
            out_specs=[fixed(x.shape) for x in outs],
        ),
        out_shape=outs,
        compiler_params=params(),
        cost_estimate=lasting(3),
        name="join",
    )(digit.reshape(1), *first, *([x for x, _ in second] * radix))


def below_kernel(held_ref, *refs, copies):
    *parts, out = refs
    rows = held_ref.shape[0]
    total = held_ref[...]
    for part in parts:
        total = total + part[part.shape[0] - rows :, :].astype(F32)
    for n in range(copies):
        out[n * rows : n * rows + rows, :] = total.astype(BF)


def add_below(held, messages, copies):
    out = jax.ShapeDtypeStruct((copies * held.shape[0], held.shape[1]), BF)
    return pl.pallas_call(
        functools.partial(below_kernel, copies=copies),
        grid=(1,),
        in_specs=[fixed(x.shape) for x in (held, *messages)],
        out_specs=fixed(out.shape),
        out_shape=out,
        compiler_params=params(),
        cost_estimate=lasting(2),
        name="add_below",
    )(held, *messages)


def place_kernel(digit_ref, *refs, radix, sizes, counts):
    parts, outs, vectors = refs[:radix], refs[radix : radix + len(sizes)], refs[radix + len(sizes) :]
    for k in range(radix):

        @pl.when(pl.program_id(0) == k)
        def _():
            at = 0
            for out, size in zip(outs, sizes):
                out[...] = parts[k][at : at + size, :].astype(out.dtype)
                at += size

            if not counts:
                return

            @pl.when(digit_ref[0] == k)
            def _():
                row = at
                for out, count in zip(vectors, counts):
                    whole = jnp.concatenate([parts[k][row + n : row + n + 1, :] for n in range(count)], axis=1)
                    whole = whole.astype(F32)
                    half = whole.shape[1] // 2
                    out[...] = jnp.where(digit_ref[1] == 0, whole[:, :half], whole[:, half:])
                    row += count


def place(parts, digit, sizes, dtype, across=None, core=None, counts=()):
    radix, width = len(parts), parts[0].shape[1]
    below = lambda k, d: (k ^ d[0], 0)
    beside = lambda k, d: (0, k ^ d[0])
    outs = [
        jax.ShapeDtypeStruct((n, width * radix) if i == across else (n * radix, width), dtype)
        for i, n in enumerate(sizes)
    ]
    halves = [jax.ShapeDtypeStruct((1, n * width // 2), F32) for n in counts]
    return pl.pallas_call(
        functools.partial(place_kernel, radix=radix, sizes=sizes, counts=counts),
        grid_spec=pltpu.PrefetchScalarGridSpec(
            num_scalar_prefetch=1,
            grid=(radix,),
            in_specs=[fixed(x.shape) for x in parts],
            out_specs=[
                pl.BlockSpec((n, width), beside if i == across else below) for i, n in enumerate(sizes)
            ]
            + [fixed(x.shape) for x in halves],
        ),
        out_shape=outs + halves,
        compiler_params=params(),
        cost_estimate=lasting(4),
        name="place",
    )(digit.reshape(1) if core is None else jnp.stack([digit, core]), *parts)


def exchange(pieces, here, stride, ranks):
    return [
        lax.ppermute(piece, "ctx", [(i, i ^ ((k + 1) * stride)) for i in range(ranks)])
        for k, piece in enumerate(pieces)
    ]


def stages_of(ranks):
    stages, stride = [], 1
    while stride < ranks:
        radix = 4 if (ranks // stride) % 4 == 0 else 2
        stages.append((stride, radix))
        stride *= radix
    return stages


def after(first, then):
    return lax.optimization_barrier((first, then))[1]


class Reduction:
    def __init__(self, here, ranks, sizes, across):
        self.here, self.ranks, self.sizes, self.across = here, ranks, sizes, across
        self.stages = stages_of(ranks)

    def digit(self, level):
        stride, radix = self.stages[level]
        return (self.here // stride) % radix

    def cut(self, terms, level):
        return cut([(x, 0) for x in terms], self.digit(level), self.stages[level][1], F32)

    def add(self, terms):
        return cut([(x, 0) for x in terms], self.here * 0, 1, BF)[0]

    def scatter(self, pieces, level):
        return [pieces[0]] + exchange(pieces[1:], self.here, self.stages[level][0], self.ranks)

    def trade(self, blocks, level):
        stride, radix = self.stages[level]
        groups = [
            [i + n * stride for n in range(radix)] for i in range(self.ranks) if (i // stride) % radix == 0
        ]
        return lax.all_to_all(blocks, "ctx", split_axis=0, concat_axis=0, axis_index_groups=groups, tiled=True)

    def gather(self, held, level):
        stride, radix = self.stages[level]
        return [held] + exchange([held] * (radix - 1), self.here, stride, self.ranks)

    def place(self, parts, level):
        if level:
            return place(parts, self.digit(level), [parts[0].shape[0]], BF, None)[0]
        return place(parts, self.digit(0), self.sizes, F32, self.across)


def padded(rows, ranks):
    step = 2 * ranks
    return -(-rows // step) * step


def swap_core(x):
    return lax.ppermute(x, "fsdp", SWAP)


def by_core(core, own, other):
    return jnp.where(core == 0, jnp.stack([own, other]), jnp.stack([other, own]))


def next_chip(block, chips, step):
    pairs = [(i, i + 4) for i in range(4 * (chips - 1))]
    return lax.ppermute(block, "ctx", pairs if step > 0 else [(b, a) for a, b in pairs])


def send_window(own, reach, chips, step):
    far = [own]
    for k in range(1, reach + 1):
        if step > 0:
            pairs = [(i, i + 4 * k) for i in range(4 * (chips - k))]
        else:
            pairs = [(i + 4 * k, i) for i in range(4 * (chips - k))]
        far.append(lax.ppermute(own, "ctx", pairs))
    return far


def both_cores(far, core, step):
    near = core == (0 if step > 0 else 1)
    parts = []
    for k in range(len(far) - 1):
        parts += [swap_core(jnp.where(near, far[k], far[k + 1])), far[k + 1]]
    return parts


def shards(
    tokens,
    cotangent,
    lengths,
    deal_order,
    w_query,
    w_key,
    w_value,
    w_out,
    w_up,
    w_down,
    b_query,
    b_value,
    b_out,
    b_up,
    b_down,
    gain_one,
    shift_one,
    gain_two,
    shift_two,
    positions,
):
    block, width = tokens.shape[2], tokens.shape[3]
    ranks = lax.axis_size("ctx")
    chips = ranks // 4
    slot = block // ranks
    rows = 2 * block
    group = ranks * block
    longest = 2 * positions.shape[0]
    reach = longest // (2 * rows)
    here = lax.axis_index("ctx")
    core = lax.axis_index("fsdp")
    chip, micro, stream = here // 4, here % 2, (here // 2) % 2
    base = chip * (2 * rows) + core * rows

    index = lambda i, t: 2 * i + t
    straight, crossing = [], []
    for i in range(ranks):
        c, a, b = i // 4, (i // 2) % 2, i % 2
        for t in range(2):
            straight.append((index(i, t), index(4 * c + 2 * t + b, a)))
            crossing.append((index(i, t), index(4 * c + 2 * t + 1 - b, a)))
    even = here % 2 == 0
    same = jnp.where(even, tokens[0, 0], tokens[1, 0])
    cross = jnp.where(even, tokens[1, 0], tokens[0, 0])
    got_same = lax.ppermute(same, BOTH, straight)
    got_cross = lax.ppermute(cross, BOTH, crossing)
    first_half = jnp.where(micro == 0, got_same, got_cross)
    second_half = jnp.where(micro == 0, got_cross, got_same)
    own = jnp.concatenate([first_half, second_half], axis=0)

    table = jnp.concatenate([deal_order[:, 0], lengths[:, 0]], axis=1)
    table = jnp.where(micro == 0, table[0], table[1])
    table = jnp.where(stream == core, table, swap_core(table))
    order, lens = table[:group], table[group:]

    head = jnp.stack([core, base, jnp.int32(group)]).astype(jnp.int32)
    info = jnp.concatenate([head, lens])

    whole = lambda x: (x, swap_core(x))
    pos, wq, wk, wv = whole(positions), whole(w_query), whole(w_key), whole(w_value)
    vectors = [b_out, b_down, gain_one, shift_one, gain_two, shift_two, b_query, b_value, b_up]
    vec = whole(stack_vectors(vectors, width // 2))
    wo, wu, wd = whole(w_out), whole(w_up), whole(w_down)

    fixed_args = (pos, wk, wv, wq, vec)
    far = [own]
    for _ in range(reach):
        far.append(next_chip(far[-1], chips, 1))
    k, v, q, hidden, low = project(info, [own], 0, True, *fixed_args)

    mine = order.reshape(ranks, ranks, slot)
    mine = lax.dynamic_slice_in_dim(mine, 4 * chip + 2 * core, 2, axis=1).reshape(rows) - base
    mine = (mine.reshape(1, rows), mine.reshape(rows, 1))
    dealt = cotangent[:, 0].reshape(2, chips, 2, 2 * slot, width)
    keep = jnp.where(core == 0, dealt[:, :, 0], dealt[:, :, 1])
    give = jnp.where(core == 0, dealt[:, :, 1], dealt[:, :, 0])
    streams = by_core(core, keep, swap_core(give))
    sends = jnp.transpose(streams, (2, 0, 1, 3, 4)).reshape(rows, width)
    sends = after(own, sends)
    arrived = lax.all_to_all(sends, "ctx", split_axis=0, concat_axis=0, tiled=True)

    far[1:] = after((mine, k), far[1:])
    arrived = after(far[1:], arrived)

    earlier = both_cores(far, core, 1)[::-1]
    before = len(earlier) * rows
    kp, vp = project(info, earlier, -before, False, *fixed_args)
    far_q = send_window(after(kp, q), reach, chips, -1)
    att, exact, logs, log_stats = attend_forward(info, after(arrived, q), kp, k, vp, v)
    leaving, da_msg, dz1, active, df, h1, du, do, sums = feed_forward(
        info, att, exact, log_stats, hidden, arrived, mine, wo, wu, wd, vec
    )
    da_msg, do, leaving = after(far_q[1:], (da_msg, do, leaving))
    far_da = [da_msg, next_chip(da_msg, chips, -1)]

    half = width // 2
    units = 2 * b_up.shape[0]
    sizes = [units // 8, half, width // 8]
    quarter = padded(sum(sizes), ranks)
    sizes_last = [width // 8, width // 8, width // 8, longest // 8]
    quarter_last = padded(sum(sizes_last) + 16, ranks)
    one = Reduction(here, ranks, sizes, 1)
    two = Reduction(here, ranks, sizes_last, None)
    levels = len(one.stages)

    pairs = width // 256
    query_args = (q, kp, k, vp, v, logs, da_msg)
    dq_first = attend_query(info, 0, pairs, *query_args, exact)
    do = after(dq_first, do)
    keep, give = ffn_grads(info, att, do, active, df, h1, du, quarter)
    give = after(far_da[1], give)
    for _ in range(reach - 1):
        far_da.append(next_chip(far_da[-1], chips, -1))
    pieces = one.cut([keep, swap_core(give)], 0)
    terms = one.scatter(pieces, 0)
    dq_second = attend_query(info, pairs, pairs, *query_args, after(pieces, exact))
    far_da[1:], far_q[1:] = after(dq_second, (far_da[1:], far_q[1:]))
    later_da = [da_msg] + both_cores(far_da, core, -1)
    later_q = [q] + both_cores(far_q, core, -1)
    dqs = (dq_first, dq_second)
    keep, give, dh0_low = last(
        info, later_q, later_da, k, v, low, dqs, dz1, sums, wq, wk, wv, quarter_last, longest
    )

    keep, give = after(terms[1:], (keep, give))
    terms_last = [keep, swap_core(give)]
    end = levels - 1
    for level in range(end):
        pieces = one.cut(terms, level + 1)
        terms = one.scatter(pieces, level + 1)
        pieces_last = two.cut(after(pieces, terms_last), level)
        terms_last = two.scatter(pieces_last, level)
    terms_last = [(x, 0) for x in terms_last]
    stride, radix = one.stages[end]
    held, held_last, *messages = join(terms, terms_last, one.digit(end), radix)
    got = exchange(messages, here, stride, ranks)
    dh0_low = after(held, dh0_low)

    back_same = jnp.where(micro == 0, dh0_low[:block], dh0_low[block:])
    back_cross = jnp.where(micro == 0, dh0_low[block:], dh0_low[:block])
    home_same = lax.ppermute(back_same, BOTH, [(b, a) for a, b in straight])
    home_cross = lax.ppermute(back_cross, BOTH, [(b, a) for a, b in crossing])
    grad_tokens = jnp.where(
        even, jnp.stack([home_same, home_cross]), jnp.stack([home_cross, home_same])
    )[:, None]

    got = after((home_same, home_cross), got)
    held = place([held] + got, one.digit(end), [held.shape[0]], BF, None)[0]
    held_last = two.trade(add_below(held_last, after(held, got), radix), end)
    for level in reversed(range(1, end)):
        held = one.place(one.gather(held, level), level)
        held_last = two.place(two.gather(held_last, level), level)
    parts = one.gather(held, 0)
    held_last = after(parts[1:], held_last)
    parts_last = two.gather(held_last, 0)
    held = one.place(parts, 0)
    leaving = after(parts[1:], leaving)
    landed = lax.all_to_all(leaving, "ctx", split_axis=0, concat_axis=0, tiled=True)

    landed = landed.reshape(chips, 2, 2, 2 * slot, width)
    keep = jnp.where(core == 0, landed[:, 0], landed[:, 1])
    give = jnp.where(core == 0, landed[:, 1], landed[:, 0])
    sides = by_core(core, keep, swap_core(give))
    output = jnp.transpose(sides, (2, 1, 0, 3, 4)).reshape(2, 1, block, width)
    counts = [1] * 7 + [units // width, 1]
    results = place(parts_last, two.digit(0), sizes_last, F32, None, core, counts)
    g_down, g_up, g_out = held
    g_key, g_value, g_query, g_pos = results[:4]
    gb_down, gg1, gs1, gg2, gs2, gb_out, gb_query, gb_up, gb_value = (x.reshape(-1) for x in results[4:])

    return (
        output,
        grad_tokens,
        g_query,
        g_key,
        g_value,
        g_out,
        g_up,
        g_down,
        gb_query,
        gb_value,
        gb_out,
        gb_up,
        gb_down,
        gg1,
        gs1,
        gg2,
        gs2,
        g_pos,
    )


def solution(mesh):
    data = P(None, "fsdp", "ctx", None)
    groups = P(None, "fsdp", None)
    matrix, vector = P("fsdp", None), P("fsdp")
    return jax.shard_map(
        shards,
        mesh=mesh,
        in_specs=(data, data, groups, groups) + (matrix,) * 6 + (vector,) * 9 + (matrix,),
        out_specs=(data, data) + (matrix,) * 6 + (vector,) * 9 + (matrix,),
        check_vma=False,
    )
```

```python
import functools

import jax
import jax.numpy as jnp
from jax import lax
from jax.experimental import pallas as pl
from jax.experimental.pallas import tpu as pltpu
from jax.sharding import PartitionSpec as P

HEADS = 8
epsilon = 1e-05
gelu_coeff = 0.7978845608028654
cubic_coeff = 0.044715
BF = jnp.bfloat16
F32 = jnp.float32
SWAP = ((0, 1), (1, 0))
BOTH = ("ctx", "fsdp")
FAR = 1 << 30


def dot(a, b):
    return jnp.dot(a, b, preferred_element_type=F32)


def dot_tn(a, b):
    return lax.dot_general(a, b, (((0,), (0,)), ((), ())), preferred_element_type=F32)


def dot_nt(a, b):
    return lax.dot_general(a, b, (((1,), (1,)), ((), ())), preferred_element_type=F32)


def gelu_parts(u):
    inner = gelu_coeff * (u + cubic_coeff * u * u * u)
    bent = jnp.tanh(inner)
    value = 0.5 * u * (1.0 + bent)
    slope = 0.5 * (1.0 + bent) + 0.5 * u * (1.0 - bent * bent) * gelu_coeff * (
        1.0 + 3.0 * cubic_coeff * u * u
    )
    return value, slope


def normalize(z):
    center = z - jnp.mean(z, axis=-1, keepdims=True)
    inv = lax.rsqrt(jnp.mean(center * center, axis=-1, keepdims=True) + epsilon)
    return center * inv, inv


def normalize_back(t, normed, inv):
    return inv * (
        t
        - jnp.mean(t, axis=-1, keepdims=True)
        - normed * jnp.mean(t * normed, axis=-1, keepdims=True)
    )


def first_places(info, spots):
    first, end = jnp.zeros_like(spots), 0
    for n in range(3, info.shape[0]):
        end = end + info[n]
        first = first + jnp.where(spots >= end, info[n], 0)
    return first


def lay(info, whole, own, other):
    n = own.shape[0]
    mine = info[0] == 0
    whole[0:n, :] = jnp.where(mine, own[...], other[...])
    whole[n : 2 * n, :] = jnp.where(mine, other[...], own[...])


def full_row(info, own, other, at, count=1):
    mine = info[0] == 0
    rows = [x[at + n : at + n + 1, :] for x in (own, other) for n in range(count)]
    first = [jnp.where(mine, rows[n], rows[count + n]) for n in range(count)]
    second = [jnp.where(mine, rows[count + n], rows[n]) for n in range(count)]
    return jnp.concatenate(first + second, axis=1)


def stack_vectors(vectors, width):
    row, at = iota((16, width), 0), 0
    table = jnp.zeros((16, width), BF)
    for x in vectors:
        for n in range(x.shape[0] // width):
            part = x[n * width : n * width + width]
            table = jnp.where(row == at, part[None, :], table)
            at += 1
    return table.astype(F32)


def iota(shape, axis):
    return lax.broadcasted_iota(jnp.int32, shape, axis)


def params(cols=0):
    return pltpu.CompilerParams(vmem_limit_bytes=(32 if cols <= 2048 else 56) * 1024 * 1024)


def lasting(us):
    return pl.CostEstimate(flops=us, transcendentals=0, bytes_accessed=us)


def fixed(shape):
    return pl.BlockSpec(shape, lambda *_: (0,) * len(shape), pipeline_mode=pl.Buffered(1))


def paired(rows):
    return pl.BlockSpec((rows, 128), lambda p, *_: (0, p))


def project_kernel(info, *refs, blocks, offset, own):
    toks = refs[:blocks]
    pos_a, pos_b, wk_a, wk_b, wv_a, wv_b, wq_a, wq_b, vec_a, vec_b = refs[blocks : blocks + 10]
    outs = refs[blocks + 10 :]
    k_ref, v_ref = outs[:2]
    wk, wv, wq, tok = outs[-4:]
    step = pl.program_id(0)
    rows = tok.shape[0]

    @pl.when(step == 0)
    def _():
        lay(info, wk, wk_a, wk_b)
        lay(info, wv, wv_a, wv_b)
        if own:
            lay(info, wq, wq_a, wq_b)

    for n in range(blocks):

        @pl.when(step == n)
        def _():
            tok[...] = toks[n][...]

    spots = info[1] + offset + step * rows + iota((rows, 1), 0)
    place = spots - first_places(info, spots)
    hidden = tok[...].astype(F32)
    half = pos_a.shape[0]
    chunk = min(half, 512)
    for part, begin in ((pos_a, info[0] * half), (pos_b, (1 - info[0]) * half)):
        for at in range(0, half, chunk):
            hot = (place - begin - at == iota((rows, chunk), 1)).astype(F32).astype(BF)
            hidden = hidden + dot(hot, part[at : at + chunk, :])
    low = hidden.astype(BF)
    k_ref[...] = dot(low, wk[...]).astype(BF)
    v_ref[...] = (dot(low, wv[...]) + full_row(info, vec_a, vec_b, 7)).astype(BF)
    if own:
        q_ref, hidden_ref, low_ref = outs[2:5]
        q_ref[...] = ((dot(low, wq[...]) + full_row(info, vec_a, vec_b, 6)).astype(BF).astype(F32) * 0.125).astype(BF)
        hidden_ref[...] = hidden
        low_ref[...] = low


def project(info, toks, offset, own, pos, wk, wv, wq, vec):
    rows, width = toks[0].shape
    blocks = len(toks)
    tall = pl.BlockSpec((rows, width), lambda n, *_: (n, 0))
    flat = jax.ShapeDtypeStruct((rows * blocks, width), BF)
    square = pltpu.VMEM((width, width), BF)
    args = (*toks, *pos, *wk, *wv, *wq, *vec)
    return pl.pallas_call(
        functools.partial(project_kernel, blocks=blocks, offset=offset, own=own),
        grid_spec=pltpu.PrefetchScalarGridSpec(
            num_scalar_prefetch=1,
            grid=(blocks,),
            in_specs=[fixed(x.shape) for x in args],
            out_specs=[tall] * (5 if own else 2),
            scratch_shapes=[square, square, square, pltpu.VMEM((rows, width), BF)],
        ),
        out_shape=[flat] * 3 + [jax.ShapeDtypeStruct((rows, width), F32), flat] if own else [flat] * 2,
        compiler_params=pltpu.CompilerParams(vmem_limit_bytes=60 * 1024 * 1024),
        cost_estimate=lasting(2 * blocks + 2),
        name="project",
    )(info, *args)


def stat_rows(table):
    high = table.astype(BF).astype(F32)
    middle = (table - high).astype(BF).astype(F32)
    low = table - high - middle
    count = table.shape[1] // 128
    rows = [
        part[half : half + 1, 128 * n : 128 * n + 128]
        for part in (high, middle, low)
        for half in range(2)
        for n in range(count)
    ]
    rows.append(jnp.zeros((16 - len(rows), 128), F32))
    return jnp.concatenate(rows, axis=0).astype(BF)


def stat_row(rows16, half, queries):
    count = queries // 128
    wide = rows16.astype(F32)
    total = wide[0 : 2 * count] + wide[2 * count : 4 * count] + wide[4 * count : 6 * count]
    return jnp.concatenate([total[half * count + n : half * count + n + 1] for n in range(count)], axis=1)


def chunks_of(cols):
    step = cols if cols <= 2048 else 768
    return [slice(at, min(at + step, cols)) for at in range(0, cols, step)]


def bias_scratch(rows, cols):
    return pltpu.VMEM((rows, cols) if len(chunks_of(cols)) == 1 else (8, 128), F32)


def query_bias(info, rows, before, chunk):
    spots = info[1] + iota((rows, 1), 0)
    first = first_places(info, spots) - (info[1] - before)
    last = iota((rows, 1), 0) + before
    col = iota((rows, chunk.stop - chunk.start), 1) + chunk.start
    return jnp.where((col >= first) & (col <= last), 0.0, -1e30)


def key_bias(info, rows, chunk):
    spots = info[1] + chunk.start + iota((1, chunk.stop - chunk.start), 1)
    first = jnp.where(spots < info[2], first_places(info, spots) - info[1], FAR)
    shape = (rows, chunk.stop - chunk.start)
    row = iota(shape, 0)
    return jnp.where((row >= first) & (row <= iota(shape, 1) + chunk.start), 0.0, -1e30)


def forward_kernel(info, q_ref, kp_ref, k_ref, vp_ref, v_ref, a_ref, exact_ref, log_ref, stat_ref, bias, keys, values):
    rows, before = q_ref.shape[0], kp_ref.shape[0]

    chunks = chunks_of(keys.shape[0])
    make_bias = functools.partial(query_bias, info, rows, before)

    @pl.when(pl.program_id(0) == 0)
    def _():
        if len(chunks) == 1:
            bias[...] = make_bias(chunks[0])

    keys[0:before, :] = kp_ref[...]
    keys[before:, :] = k_ref[...]
    values[0:before, :] = vp_ref[...]
    values[before:, :] = v_ref[...]
    logs = []
    for half in range(2):
        lanes = slice(64 * half, 64 * half + 64)


        def scores_of(chunk):
            mask = bias[...] if len(chunks) == 1 else make_bias(chunk)
            return dot_nt(q_ref[:, lanes], keys[chunk, lanes]) + mask

        if len(chunks) == 1:
            scores = scores_of(chunks[0])
            top = jnp.max(scores, axis=1, keepdims=True)
            raised = jnp.exp(scores - top)
            total = jnp.sum(raised, axis=1, keepdims=True)
            probs = raised * (1.0 / total)
            low = probs.astype(BF)
            attended = dot(low, values[:, lanes])
            weight = jnp.sum(low.astype(F32), axis=1, keepdims=True)
        else:
            top = jnp.full((rows, 1), -1e30, F32)
            for chunk in chunks:
                top = jnp.maximum(top, jnp.max(scores_of(chunk), axis=1, keepdims=True))
            total = jnp.zeros((rows, 1), F32)
            for chunk in chunks:
                total = total + jnp.sum(jnp.exp(scores_of(chunk) - top), axis=1, keepdims=True)
            attended, weight = jnp.zeros((rows, 64), F32), jnp.zeros((rows, 1), F32)
            for chunk in chunks:
                probs = jnp.exp(scores_of(chunk) - top) * (1.0 / total)
                low = probs.astype(BF)
                attended = attended + dot(low, values[chunk, lanes])
                weight = weight + jnp.sum(low.astype(F32), axis=1, keepdims=True)
        a_ref[:, lanes] = attended.astype(BF)
        exact_ref[:, lanes] = attended / weight
        logs.append(jnp.broadcast_to(top + jnp.log(total), (rows, 64)))
    wide = jnp.concatenate(logs, axis=1)
    log_ref[...] = wide
    turned = wide.T
    stat_ref[...] = stat_rows(jnp.concatenate([turned[0:1], turned[64:65]], axis=0))


def attend_forward(info, q, kp, k, vp, v):
    rows, width = q.shape
    before = kp.shape[0]
    cols = before + rows
    return pl.pallas_call(
        forward_kernel,
        grid_spec=pltpu.PrefetchScalarGridSpec(
            num_scalar_prefetch=1,
            grid=(width // 128,),
            in_specs=[paired(x.shape[0]) for x in (q, kp, k, vp, v)],
            out_specs=[paired(rows), paired(rows), paired(rows), paired(16)],
            scratch_shapes=[
                bias_scratch(rows, cols),
                pltpu.VMEM((cols, 128), BF),
                pltpu.VMEM((cols, 128), BF),
            ],
        ),
        out_shape=[
            jax.ShapeDtypeStruct((rows, width), BF),
            jax.ShapeDtypeStruct((rows, width), F32),
            jax.ShapeDtypeStruct((rows, width), F32),
            jax.ShapeDtypeStruct((16, width), BF),
        ],
        compiler_params=params(cols),
        cost_estimate=lasting(12),
        name="attend_forward",
    )(info, q, kp, k, vp, v)


def ffn_kernel(
    info, a_ref, exact_ref, stat_ref, hidden_ref, arrived_ref, row_ref, col_ref, wo_a, wo_b, wu_a, wu_b, wd_a, wd_b, vec_a, vec_b,
    leaving_ref, msg_ref, dz1_ref, active_ref, df_ref, h1_ref, du_ref, do_ref, sums_ref,
    wo, wu, wd, slopes, stats,
):
    lay(info, wo, wo_a, wo_b)
    lay(info, wu, wu_a, wu_b)
    lay(info, wd, wd_a, wd_b)
    rows, width = hidden_ref.shape
    hidden_units = wu.shape[1]
    bo, bd, g1, s1, g2, s2 = (full_row(info, vec_a, vec_b, n) for n in range(6))
    bu = full_row(info, vec_a, vec_b, 8, hidden_units // width)
    pick = (iota((rows, rows), 0) == row_ref[...]).astype(F32).astype(BF)
    pick_back = (col_ref[...] == iota((rows, rows), 1)).astype(F32).astype(BF)
    dy = dot(pick, arrived_ref[...])

    n1, r1 = normalize(hidden_ref[...] + dot(a_ref[...], wo[...]) + bo)
    h1 = n1 * g1 + s1
    h1_low = h1.astype(BF)
    h1_ref[...] = h1_low
    z2 = h1 + bd
    for at in range(0, hidden_units, width):
        block = slice(at, at + width)
        value, slope = gelu_parts(dot(h1_low, wu[:, block]) + bu[:, block])
        slopes[:, block] = slope
        low = value.astype(BF)
        active_ref[:, block] = low
        z2 = z2 + dot(low, wd[block, :])
    n2, r2 = normalize(z2)
    leaving_ref[...] = dot(pick_back, (n2 * g2 + s2).astype(BF)).astype(BF)

    def add(x):
        return jnp.sum(x, axis=0, keepdims=True)

    dz2 = normalize_back(dy * g2, n2, r2)
    df = dz2.astype(BF)
    df_ref[...] = df
    sums_ref[0:1, :] = add(df.astype(F32))
    sums_ref[3:4, :] = add(dy * n2)
    sums_ref[4:5, :] = add(dy)
    dh1 = dz2
    for at in range(0, hidden_units, width):
        block = slice(at, at + width)
        du = (dot_nt(df, wd[block, :]) * slopes[:, block]).astype(BF)
        du_ref[:, block] = du
        n = 7 + at // width
        sums_ref[n : n + 1, :] = add(du.astype(F32))
        dh1 = dh1 + dot_nt(du, wu[:, block])
    dz1 = normalize_back(dh1 * g1, n1, r1)
    dz1_ref[...] = dz1
    sums_ref[1:2, :] = add(dh1 * n1)
    sums_ref[2:3, :] = add(dh1)
    do = dz1.astype(BF)
    do_ref[...] = do
    sums_ref[5:6, :] = add(do.astype(F32))
    sums_ref[6:7, :] = jnp.zeros((1, width), F32)
    sums_ref[11:16, :] = jnp.zeros((5, width), F32)
    da = dot_nt(do, wo[...]).astype(BF)
    msg_ref[0:rows, :] = da
    terms = da.astype(F32) * exact_ref[...]
    head = iota((HEADS, width), 0)
    lane = iota((HEADS, width), 1) // (width // HEADS)
    ones = (head == lane).astype(F32).astype(BF)
    delta = jnp.zeros((HEADS, rows), F32)
    for _ in range(3):
        part = terms.astype(BF)
        terms = terms - part.astype(F32)
        delta = delta + dot_nt(ones, part)
    for p in range(HEADS // 2):
        stats[:, 128 * p : 128 * p + 128] = stat_rows(delta[2 * p : 2 * p + 2, :])
    msg_ref[rows : rows + 16, :] = stat_ref[...]
    msg_ref[rows + 16 : rows + 32, :] = stats[...]


def feed_forward(info, a, exact, log_stats, hidden, arrived, mine, wo, wu, wd, vec):
    rows, width = hidden.shape
    units = wu[0].shape[1]
    args = (a, exact, log_stats, hidden, arrived, *mine, *wo, *wu, *wd, *vec)
    low = jax.ShapeDtypeStruct((rows, width), BF)
    tall = jax.ShapeDtypeStruct((rows, units), BF)
    outs = [
        low,
        jax.ShapeDtypeStruct((rows + 32, width), BF),
        jax.ShapeDtypeStruct((rows, width), F32),
        tall,
        low,
        low,
        tall,
        low,
        jax.ShapeDtypeStruct((16, width), F32),
    ]
    return pl.pallas_call(
        ffn_kernel,
        grid_spec=pltpu.PrefetchScalarGridSpec(
            num_scalar_prefetch=1,
            grid=(1,),
            in_specs=[fixed(x.shape) for x in args],
            out_specs=[fixed(x.shape) for x in outs],
            scratch_shapes=[
                pltpu.VMEM((width, width), BF),
                pltpu.VMEM((width, units), BF),
                pltpu.VMEM((units, width), BF),
                pltpu.VMEM((rows, units), F32),
                pltpu.VMEM((16, width), BF),
            ],
        ),
        out_shape=outs,
        compiler_params=params(),
        cost_estimate=lasting(10),
        name="feed_forward",
    )(info, *args)


def keep_or_send(info, half, mine, send, at, value):
    at, value = pl.multiple_of(at, 8), value.astype(BF)

    @pl.when(info[0] == half)
    def _():
        mine[pl.ds(at, value.shape[0]), :] = value

    @pl.when(info[0] != half)
    def _():
        send[pl.ds(at, value.shape[0]), :] = value


def split_halves(info, mine, send, starts, value):
    half, step = value.shape[0] // 2, value.shape[0] // 8
    first = info[0] == 0
    own = jnp.where(first, value[:half], value[half:]).astype(BF)
    other = jnp.where(first, value[half:], value[:half]).astype(BF)
    for n, at in enumerate(starts):
        mine[at : at + step, :] = own[n * step : n * step + step]
        send[at : at + step, :] = other[n * step : n * step + step]


def grads_kernel(
    info, a_own, a_other, do_ref, active_own, active_other, df_ref, h1_ref, du_ref, mine, send, *, quarter
):
    width = df_ref.shape[1]
    step = pl.program_id(0)
    part = active_own.shape[1]
    mine[0:part, :] = dot_tn(active_own[...], df_ref[...]).astype(BF)
    send[0:part, :] = dot_tn(active_other[...], df_ref[...]).astype(BF)
    up = dot_tn(h1_ref[...], du_ref[...])
    low, high = up[: width // 2].astype(BF), up[width // 2 :].astype(BF)
    at = part + width // 2
    mine[part:at, :] = jnp.where(info[0] == 0, low, high)
    send[part:at, :] = jnp.where(info[0] == 0, high, low)
    for out, a_ref in ((mine, a_own), (send, a_other)):
        both = dot_tn(a_ref[...], do_ref[...]).astype(BF)
        out[at : at + 64, :] = jnp.where(step % 2 == 0, both[:64], both[64:])
        if quarter > at + 64:
            out[at + 64 :, :] = jnp.zeros((quarter - at - 64, width), BF)


def ffn_grads(info, a, do, active, df, h1, du, quarter):
    rows, width = df.shape
    units = active.shape[1]
    out = jax.ShapeDtypeStruct((4 * quarter, width), BF)
    columns = lambda n, index: pl.BlockSpec((rows, n), lambda j, info: (0, index(j, info[0])))
    return pl.pallas_call(
        functools.partial(grads_kernel, quarter=quarter),
        grid_spec=pltpu.PrefetchScalarGridSpec(
            num_scalar_prefetch=1,
            grid=(4,),
            in_specs=[
                columns(128, lambda j, core: core * 2 + j // 2),
                columns(128, lambda j, core: (1 - core) * 2 + j // 2),
                fixed(do.shape),
                columns(units // 8, lambda j, core: core * 4 + j),
                columns(units // 8, lambda j, core: (1 - core) * 4 + j),
                fixed(df.shape),
                fixed(h1.shape),
                columns(units // 4, lambda j, core: j),
            ],
            out_specs=[pl.BlockSpec((quarter, width), lambda j, *_: (j, 0))] * 2,
        ),
        out_shape=[out, out],
        compiler_params=params(),
        cost_estimate=lasting(10),
        name="ffn_grads",
    )(info, a, a, do, active, active, df, h1, du)


def query_kernel(
    info, q_ref, kp_ref, k_ref, vp_ref, v_ref, log_ref, da_ref, exact_ref, dq_ref, bias, keys, values
):
    rows, before = q_ref.shape[0], kp_ref.shape[0]
    chunks = chunks_of(keys.shape[0])
    make_bias = functools.partial(query_bias, info, rows, before)

    @pl.when(pl.program_id(0) == 0)
    def _():
        if len(chunks) == 1:
            bias[...] = make_bias(chunks[0])

    keys[0:before, :] = kp_ref[...]
    keys[before:, :] = k_ref[...]
    values[0:before, :] = vp_ref[...]
    values[before:, :] = v_ref[...]
    for half in range(2):
        lanes = slice(64 * half, 64 * half + 64)
        delta = jnp.sum(da_ref[:, lanes].astype(F32) * exact_ref[:, lanes], axis=1, keepdims=True)
        dq = jnp.zeros((rows, 64), F32)
        for chunk in chunks:
            mask = bias[...] if len(chunks) == 1 else make_bias(chunk)
            scores = dot_nt(q_ref[:, lanes], keys[chunk, lanes]) + mask
            probs = jnp.exp(scores - log_ref[:, 64 * half : 64 * half + 1])
            dp = dot_nt(da_ref[:, lanes], values[chunk, lanes])
            ds = (probs * (dp - delta)).astype(BF)
            dq = dq + dot(ds, keys[chunk, lanes])
        dq_ref[:, lanes] = (dq * 0.125).astype(BF)


def attend_query(info, first, count, q, kp, k, vp, v, logs, da, exact):
    rows = q.shape[0]
    before = kp.shape[0]
    cols = before + rows
    some = lambda n: pl.BlockSpec((n, 128), lambda p, *_: (0, p + first))
    return pl.pallas_call(
        query_kernel,
        grid_spec=pltpu.PrefetchScalarGridSpec(
            num_scalar_prefetch=1,
            grid=(count,),
            in_specs=[some(x.shape[0]) for x in (q, kp, k, vp, v, logs)] + [some(rows), some(rows)],
            out_specs=paired(rows),
            scratch_shapes=[
                bias_scratch(rows, cols),
                pltpu.VMEM((cols, 128), BF),
                pltpu.VMEM((cols, 128), BF),
            ],
        ),
        out_shape=jax.ShapeDtypeStruct((rows, 128 * count), BF),
        compiler_params=params(cols),
        cost_estimate=lasting(5),
        name="attend_query",
    )(info, q, kp, k, vp, v, logs, da, exact)


def last_kernel(info, *refs, reach, quarter, table):
    count = 2 * reach + 1
    q_parts, da_parts = refs[:count], refs[count : 2 * count]
    k_ref, v_ref, low_ref, dq_a, dq_b, dz1_ref, sums_ref, wq_a, wq_b, wk_a, wk_b, wv_a, wv_b = refs[2 * count : 2 * count + 13]
    mine, send, dh_out, bias, queries, grads, dk_all, dv_all, wq, wk, wv = refs[2 * count + 13 :]
    rows, width = low_ref.shape
    cols = queries.shape[0]
    step = pl.program_id(0)

    chunks = chunks_of(cols)
    make_bias = functools.partial(key_bias, info, rows)

    @pl.when(step == 0)
    def _():
        lay(info, wq, wq_a, wq_b)
        lay(info, wk, wk_a, wk_b)
        lay(info, wv, wv_a, wv_b)
        if len(chunks) == 1:
            bias[...] = make_bias(chunks[0])

    for n in range(count):
        queries[n * rows : n * rows + rows, :] = q_parts[n][...]
        grads[n * rows : n * rows + rows, :] = da_parts[n][0:rows, :]
    dks, dvs = [], []
    for half in range(2):
        lanes = slice(64 * half, 64 * half + 64)
        logs = jnp.concatenate([stat_row(x[rows : rows + 16, :], half, rows) for x in da_parts], axis=1)
        delta = jnp.concatenate([stat_row(x[rows + 16 : rows + 32, :], half, rows) for x in da_parts], axis=1)
        dk, dv = jnp.zeros((rows, 64), F32), jnp.zeros((rows, 64), F32)
        for chunk in chunks:
            mask = bias[...] if len(chunks) == 1 else make_bias(chunk)
            scores = dot_nt(k_ref[:, lanes], queries[chunk, lanes]) + mask
            probs = jnp.exp(scores - logs[:, chunk])
            dv = dv + dot(probs.astype(BF), grads[chunk, lanes])
            dp = dot_nt(v_ref[:, lanes], grads[chunk, lanes])
            ds = (probs * (dp - delta[:, chunk])).astype(BF)
            dk = dk + dot(ds, queries[chunk, lanes])
        dks.append(dk.astype(BF))
        dvs.append(dv.astype(BF))
    dk_pair, dv_pair = jnp.concatenate(dks, axis=1), jnp.concatenate(dvs, axis=1)
    for n in range(width // 128):

        @pl.when(step == n)
        def _():
            dk_all[:, 128 * n : 128 * n + 128] = dk_pair
            dv_all[:, 128 * n : 128 * n + 128] = dv_pair

    @pl.when(step == pl.num_programs(0) - 1)
    def _():
        dk, dv = dk_all[...], dv_all[...]
        step_rows = width // 8
        turned = low_ref[...].T
        split_halves(info, mine, send, [n * quarter for n in range(4)], dot(turned, dk))
        split_halves(info, mine, send, [n * quarter + step_rows for n in range(4)], dot(turned, dv))
        dq = jnp.concatenate([dq_a[...], dq_b[...]], axis=1)
        split_halves(info, mine, send, [n * quarter + 2 * step_rows for n in range(4)], dot(turned, dq))
        dh = dz1_ref[...] + dot_nt(dq, wq[...]) + dot_nt(dk, wk[...]) + dot_nt(dv, wv[...])
        dh_out[...] = dh.astype(BF)
        parts = []
        for _ in range(2):
            parts.append(dh.astype(BF))
            dh = dh - parts[-1].astype(F32)
        spots = info[1] + iota((1, rows), 1)
        place = spots - first_places(info, spots)
        base = 3 * step_rows
        fourth = table // 8
        for half in range(2):
            for n in range(4):
                hot = (place - (half * 4 + n) * fourth == iota((fourth, rows), 0)).astype(F32).astype(BF)
                total = dot(hot, parts[0]) + dot(hot, parts[1])
                keep_or_send(info, half, mine, send, n * quarter + base, total)
        base += fourth
        spare = quarter - base
        for n in range(4):
            mine[n * quarter + base : (n + 1) * quarter, :] = jnp.zeros((spare, width), BF)
            send[n * quarter + base : (n + 1) * quarter, :] = jnp.zeros((spare, width), BF)
        total_v = jnp.sum(dv.astype(F32), axis=0, keepdims=True)
        total_q = jnp.sum(dq.astype(F32), axis=0, keepdims=True)
        row = iota(sums_ref.shape, 0)
        total = jnp.where(row == 6, total_q, jnp.where(row == 11, total_v, sums_ref[...])).astype(BF)
        mine[base : base + 16, :] = total
        send[base : base + 16, :] = total


def last(info, q_parts, da_parts, k, v, low, dqs, dz1, sums, wq, wk, wv, quarter, table):
    rows, width = k.shape
    count = len(q_parts)
    cols = count * rows
    outs = [
        jax.ShapeDtypeStruct((4 * quarter, width), BF),
        jax.ShapeDtypeStruct((4 * quarter, width), BF),
        jax.ShapeDtypeStruct((rows, width), BF),
    ]
    rest = (low, *dqs, dz1, sums, *wq, *wk, *wv)
    return pl.pallas_call(
        functools.partial(last_kernel, reach=count // 2, quarter=quarter, table=table),
        grid_spec=pltpu.PrefetchScalarGridSpec(
            num_scalar_prefetch=1,
            grid=(width // 128,),
            in_specs=[paired(x.shape[0]) for x in (*q_parts, *da_parts, k, v)] + [fixed(x.shape) for x in rest],
            out_specs=[fixed(x.shape) for x in outs],
            scratch_shapes=[
                bias_scratch(rows, cols),
                pltpu.VMEM((cols, 128), BF),
                pltpu.VMEM((cols, 128), BF),
                pltpu.VMEM((rows, width), BF),
                pltpu.VMEM((rows, width), BF),
                pltpu.VMEM((width, width), BF),
                pltpu.VMEM((width, width), BF),
                pltpu.VMEM((width, width), BF),
            ],
        ),
        out_shape=outs,
        compiler_params=params(cols),
        cost_estimate=lasting(15),
        name="last",
    )(info, *q_parts, *da_parts, k, v, *rest)


def cut_kernel(digit_ref, *refs, terms, radix):
    ins, outs = refs[: terms * radix], refs[terms * radix :]
    for k in range(radix):
        total = ins[k * terms][...].astype(F32)
        for n in range(1, terms):
            total = total + ins[k * terms + n][...].astype(F32)
        outs[k][...] = total.astype(outs[k].dtype)


def rows_of(terms):
    return terms[0][0].shape[0] // (1 + max(block for _, block in terms))


def cut(terms, digit, radix, kept):
    rows, width = rows_of(terms) // radix, terms[0][0].shape[1]
    subs = 1
    specs = [
        pl.BlockSpec((rows // subs, width), lambda n, d, k=k, b=b: ((b * radix + (d[0] ^ k)) * subs + n, 0))
        for k in range(radix)
        for _, b in terms
    ]
    return pl.pallas_call(
        functools.partial(cut_kernel, terms=len(terms), radix=radix),
        grid_spec=pltpu.PrefetchScalarGridSpec(
            num_scalar_prefetch=1,
            grid=(subs,),
            in_specs=specs,
            out_specs=[pl.BlockSpec((rows // subs, width), lambda n, d: (n, 0))] * radix,
        ),
        out_shape=[jax.ShapeDtypeStruct((rows, width), BF if k else kept) for k in range(radix)],
        compiler_params=params(),
        cost_estimate=lasting(3),
        name="cut",
    )(digit.reshape(1), *([x for x, _ in terms] * radix))


def total_of(refs):
    total = refs[0][...].astype(F32)
    for ref in refs[1:]:
        total = total + ref[...].astype(F32)
    return total


def join_kernel(digit_ref, *refs, ones, twos, radix):
    done, held, *messages = refs[ones + twos * radix :]
    rows = done.shape[0]
    whole = total_of(refs[:ones]).astype(BF)
    done[...] = whole
    for k in range(radix):
        piece = total_of(refs[ones + k * twos : ones + (k + 1) * twos])
        if k:
            messages[k - 1][0:rows, :] = whole
            messages[k - 1][rows:, :] = piece.astype(BF)
        else:
            held[...] = piece


def join(first, second, digit, radix):
    (rows, width), part = first[0].shape, rows_of(second) // radix
    specs = [
        pl.BlockSpec((part, width), lambda n, d, k=k, b=b: (b * radix + (d[0] ^ k), 0))
        for k in range(radix)
        for _, b in second
    ]
    outs = [jax.ShapeDtypeStruct((rows, width), BF), jax.ShapeDtypeStruct((part, width), F32)]
    outs += [jax.ShapeDtypeStruct((rows + part, width), BF)] * (radix - 1)
    return pl.pallas_call(
        functools.partial(join_kernel, ones=len(first), twos=len(second), radix=radix),
        grid_spec=pltpu.PrefetchScalarGridSpec(
            num_scalar_prefetch=1,
            grid=(1,),
            in_specs=[fixed((rows, width))] * len(first) + specs,
            out_specs=[fixed(x.shape) for x in outs],
        ),
        out_shape=outs,
        compiler_params=params(),
        cost_estimate=lasting(3),
        name="join",
    )(digit.reshape(1), *first, *([x for x, _ in second] * radix))


def below_kernel(held_ref, *refs, copies):
    *parts, out = refs
    rows = held_ref.shape[0]
    total = held_ref[...]
    for part in parts:
        total = total + part[part.shape[0] - rows :, :].astype(F32)
    for n in range(copies):
        out[n * rows : n * rows + rows, :] = total.astype(BF)


def add_below(held, messages, copies):
    out = jax.ShapeDtypeStruct((copies * held.shape[0], held.shape[1]), BF)
    return pl.pallas_call(
        functools.partial(below_kernel, copies=copies),
        grid=(1,),
        in_specs=[fixed(x.shape) for x in (held, *messages)],
        out_specs=fixed(out.shape),
        out_shape=out,
        compiler_params=params(),
        cost_estimate=lasting(2),
        name="add_below",
    )(held, *messages)


def place_kernel(digit_ref, *refs, radix, sizes, counts):
    parts, outs, vectors = refs[:radix], refs[radix : radix + len(sizes)], refs[radix + len(sizes) :]
    for k in range(radix):

        @pl.when(pl.program_id(0) == k)
        def _():
            at = 0
            for out, size in zip(outs, sizes):
                out[...] = parts[k][at : at + size, :].astype(out.dtype)
                at += size

            if not counts:
                return

            @pl.when(digit_ref[0] == k)
            def _():
                row = at
                for out, count in zip(vectors, counts):
                    whole = jnp.concatenate([parts[k][row + n : row + n + 1, :] for n in range(count)], axis=1)
                    whole = whole.astype(F32)
                    half = whole.shape[1] // 2
                    out[...] = jnp.where(digit_ref[1] == 0, whole[:, :half], whole[:, half:])
                    row += count


def place(parts, digit, sizes, dtype, across=None, core=None, counts=()):
    radix, width = len(parts), parts[0].shape[1]
    below = lambda k, d: (k ^ d[0], 0)
    beside = lambda k, d: (0, k ^ d[0])
    outs = [
        jax.ShapeDtypeStruct((n, width * radix) if i == across else (n * radix, width), dtype)
        for i, n in enumerate(sizes)
    ]
    halves = [jax.ShapeDtypeStruct((1, n * width // 2), F32) for n in counts]
    return pl.pallas_call(
        functools.partial(place_kernel, radix=radix, sizes=sizes, counts=counts),
        grid_spec=pltpu.PrefetchScalarGridSpec(
            num_scalar_prefetch=1,
            grid=(radix,),
            in_specs=[fixed(x.shape) for x in parts],
            out_specs=[
                pl.BlockSpec((n, width), beside if i == across else below) for i, n in enumerate(sizes)
            ]
            + [fixed(x.shape) for x in halves],
        ),
        out_shape=outs + halves,
        compiler_params=params(),
        cost_estimate=lasting(4),
        name="place",
    )(digit.reshape(1) if core is None else jnp.stack([digit, core]), *parts)


def exchange(pieces, here, stride, ranks):
    return [
        lax.ppermute(piece, "ctx", [(i, i ^ ((k + 1) * stride)) for i in range(ranks)])
        for k, piece in enumerate(pieces)
    ]


def stages_of(ranks):
    stages, stride = [], 1
    while stride < ranks:
        radix = 4 if (ranks // stride) % 4 == 0 else 2
        stages.append((stride, radix))
        stride *= radix
    return stages


def after(first, then):
    return lax.optimization_barrier((first, then))[1]


class Reduction:
    def __init__(self, here, ranks, sizes, across):
        self.here, self.ranks, self.sizes, self.across = here, ranks, sizes, across
        self.stages = stages_of(ranks)

    def digit(self, level):
        stride, radix = self.stages[level]
        return (self.here // stride) % radix

    def cut(self, terms, level):
        return cut([(x, 0) for x in terms], self.digit(level), self.stages[level][1], F32)

    def add(self, terms):
        return cut([(x, 0) for x in terms], self.here * 0, 1, BF)[0]

    def scatter(self, pieces, level):
        return [pieces[0]] + exchange(pieces[1:], self.here, self.stages[level][0], self.ranks)

    def trade(self, blocks, level):
        stride, radix = self.stages[level]
        groups = [
            [i + n * stride for n in range(radix)] for i in range(self.ranks) if (i // stride) % radix == 0
        ]
        return lax.all_to_all(blocks, "ctx", split_axis=0, concat_axis=0, axis_index_groups=groups, tiled=True)

    def gather(self, held, level):
        stride, radix = self.stages[level]
        return [held] + exchange([held] * (radix - 1), self.here, stride, self.ranks)

    def place(self, parts, level):
        if level:
            return place(parts, self.digit(level), [parts[0].shape[0]], BF, None)[0]
        return place(parts, self.digit(0), self.sizes, F32, self.across)


def padded(rows, ranks):
    step = 2 * ranks
    return -(-rows // step) * step


def swap_core(x):
    return lax.ppermute(x, "fsdp", SWAP)


def by_core(core, own, other):
    return jnp.where(core == 0, jnp.stack([own, other]), jnp.stack([other, own]))


def next_chip(block, chips, step):
    pairs = [(i, i + 4) for i in range(4 * (chips - 1))]
    return lax.ppermute(block, "ctx", pairs if step > 0 else [(b, a) for a, b in pairs])


def send_window(own, reach, chips, step):
    far = [own]
    for k in range(1, reach + 1):
        if step > 0:
            pairs = [(i, i + 4 * k) for i in range(4 * (chips - k))]
        else:
            pairs = [(i + 4 * k, i) for i in range(4 * (chips - k))]
        far.append(lax.ppermute(own, "ctx", pairs))
    return far


def both_cores(far, core, step):
    near = core == (0 if step > 0 else 1)
    parts = []
    for k in range(len(far) - 1):
        parts += [swap_core(jnp.where(near, far[k], far[k + 1])), far[k + 1]]
    return parts


def shards(
    tokens,
    cotangent,
    lengths,
    deal_order,
    w_query,
    w_key,
    w_value,
    w_out,
    w_up,
    w_down,
    b_query,
    b_value,
    b_out,
    b_up,
    b_down,
    gain_one,
    shift_one,
    gain_two,
    shift_two,
    positions,
):
    block, width = tokens.shape[2], tokens.shape[3]
    ranks = lax.axis_size("ctx")
    chips = ranks // 4
    slot = block // ranks
    rows = 2 * block
    group = ranks * block
    longest = 2 * positions.shape[0]
    reach = longest // (2 * rows)
    here = lax.axis_index("ctx")
    core = lax.axis_index("fsdp")
    chip, micro, stream = here // 4, here % 2, (here // 2) % 2
    base = chip * (2 * rows) + core * rows

    index = lambda i, t: 2 * i + t
    straight, crossing = [], []
    for i in range(ranks):
        c, a, b = i // 4, (i // 2) % 2, i % 2
        for t in range(2):
            straight.append((index(i, t), index(4 * c + 2 * t + b, a)))
            crossing.append((index(i, t), index(4 * c + 2 * t + 1 - b, a)))
    even = here % 2 == 0
    same = jnp.where(even, tokens[0, 0], tokens[1, 0])
    cross = jnp.where(even, tokens[1, 0], tokens[0, 0])
    got_same = lax.ppermute(same, BOTH, straight)
    got_cross = lax.ppermute(cross, BOTH, crossing)
    first_half = jnp.where(micro == 0, got_same, got_cross)
    second_half = jnp.where(micro == 0, got_cross, got_same)
    own = jnp.concatenate([first_half, second_half], axis=0)

    table = jnp.concatenate([deal_order[:, 0], lengths[:, 0]], axis=1)
    table = jnp.where(micro == 0, table[0], table[1])
    table = jnp.where(stream == core, table, swap_core(table))
    order, lens = table[:group], table[group:]

    head = jnp.stack([core, base, jnp.int32(group)]).astype(jnp.int32)
    info = jnp.concatenate([head, lens])

    whole = lambda x: (x, swap_core(x))
    pos, wq, wk, wv = whole(positions), whole(w_query), whole(w_key), whole(w_value)
    vectors = [b_out, b_down, gain_one, shift_one, gain_two, shift_two, b_query, b_value, b_up]
    vec = whole(stack_vectors(vectors, width // 2))
    wo, wu, wd = whole(w_out), whole(w_up), whole(w_down)

    fixed_args = (pos, wk, wv, wq, vec)
    far = [own]
    for _ in range(reach):
        far.append(next_chip(far[-1], chips, 1))
    k, v, q, hidden, low = project(info, [own], 0, True, *fixed_args)

    mine = order.reshape(ranks, ranks, slot)
    mine = lax.dynamic_slice_in_dim(mine, 4 * chip + 2 * core, 2, axis=1).reshape(rows) - base
    mine = (mine.reshape(1, rows), mine.reshape(rows, 1))
    dealt = cotangent[:, 0].reshape(2, chips, 2, 2 * slot, width)
    keep = jnp.where(core == 0, dealt[:, :, 0], dealt[:, :, 1])
    give = jnp.where(core == 0, dealt[:, :, 1], dealt[:, :, 0])
    streams = by_core(core, keep, swap_core(give))
    sends = jnp.transpose(streams, (2, 0, 1, 3, 4)).reshape(rows, width)
    sends = after(own, sends)
    arrived = lax.all_to_all(sends, "ctx", split_axis=0, concat_axis=0, tiled=True)

    far[1:] = after((mine, k), far[1:])
    arrived = after(far[1:], arrived)

    earlier = both_cores(far, core, 1)[::-1]
    before = len(earlier) * rows
    kp, vp = project(info, earlier, -before, False, *fixed_args)
    far_q = send_window(after(kp, q), reach, chips, -1)
    att, exact, logs, log_stats = attend_forward(info, after(arrived, q), kp, k, vp, v)
    leaving, da_msg, dz1, active, df, h1, du, do, sums = feed_forward(
        info, att, exact, log_stats, hidden, arrived, mine, wo, wu, wd, vec
    )
    da_msg, do, leaving = after(far_q[1:], (da_msg, do, leaving))
    far_da = [da_msg, next_chip(da_msg, chips, -1)]

    half = width // 2
    units = 2 * b_up.shape[0]
    sizes = [units // 8, half, width // 8]
    quarter = padded(sum(sizes), ranks)
    sizes_last = [width // 8, width // 8, width // 8, longest // 8]
    quarter_last = padded(sum(sizes_last) + 16, ranks)
    one = Reduction(here, ranks, sizes, 1)
    two = Reduction(here, ranks, sizes_last, None)
    levels = len(one.stages)

    pairs = width // 256
    query_args = (q, kp, k, vp, v, logs, da_msg)
    dq_first = attend_query(info, 0, pairs, *query_args, exact)
    do = after(dq_first, do)
    keep, give = ffn_grads(info, att, do, active, df, h1, du, quarter)
    give = after(far_da[1], give)
    for _ in range(reach - 1):
        far_da.append(next_chip(far_da[-1], chips, -1))
    pieces = one.cut([keep, swap_core(give)], 0)
    terms = one.scatter(pieces, 0)
    dq_second = attend_query(info, pairs, pairs, *query_args, after(pieces, exact))
    far_da[1:], far_q[1:] = after(dq_second, (far_da[1:], far_q[1:]))
    later_da = [da_msg] + both_cores(far_da, core, -1)
    later_q = [q] + both_cores(far_q, core, -1)
    dqs = (dq_first, dq_second)
    keep, give, dh0_low = last(
        info, later_q, later_da, k, v, low, dqs, dz1, sums, wq, wk, wv, quarter_last, longest
    )

    keep, give = after(terms[1:], (keep, give))
    terms_last = [keep, swap_core(give)]
    end = levels - 1
    for level in range(end):
        pieces = one.cut(terms, level + 1)
        terms = one.scatter(pieces, level + 1)
        pieces_last = two.cut(after(pieces, terms_last), level)
        terms_last = two.scatter(pieces_last, level)
    terms_last = [(x, 0) for x in terms_last]
    leaving = after(terms_last[1][0], leaving)
    stride, radix = one.stages[end]
    held, held_last, *messages = join(terms, terms_last, one.digit(end), radix)
    got = exchange(messages, here, stride, ranks)
    dh0_low = after(held, dh0_low)

    back_same = jnp.where(micro == 0, dh0_low[:block], dh0_low[block:])
    back_cross = jnp.where(micro == 0, dh0_low[block:], dh0_low[:block])
    home_same = lax.ppermute(back_same, BOTH, [(b, a) for a, b in straight])
    home_cross = lax.ppermute(back_cross, BOTH, [(b, a) for a, b in crossing])
    grad_tokens = jnp.where(
        even, jnp.stack([home_same, home_cross]), jnp.stack([home_cross, home_same])
    )[:, None]

    got = after((home_same, home_cross), got)
    held = place([held] + got, one.digit(end), [held.shape[0]], BF, None)[0]
    held_last = two.trade(add_below(held_last, after(held, got), radix), end)
    for level in reversed(range(1, end)):
        held = one.place(one.gather(held, level), level)
        held_last = two.place(two.gather(held_last, level), level)
    parts = one.gather(held, 0)
    held_last = after(parts[1:], held_last)
    parts_last = two.gather(held_last, 0)
    held = one.place(parts, 0)
    landed = lax.all_to_all(leaving, "ctx", split_axis=0, concat_axis=0, tiled=True)

    landed = landed.reshape(chips, 2, 2, 2 * slot, width)
    keep = jnp.where(core == 0, landed[:, 0], landed[:, 1])
    give = jnp.where(core == 0, landed[:, 1], landed[:, 0])
    sides = by_core(core, keep, swap_core(give))
    output = jnp.transpose(sides, (2, 1, 0, 3, 4)).reshape(2, 1, block, width)
    counts = [1] * 7 + [units // width, 1]
    results = place(parts_last, two.digit(0), sizes_last, F32, None, core, counts)
    g_down, g_up, g_out = held
    g_key, g_value, g_query, g_pos = results[:4]
    gb_down, gg1, gs1, gg2, gs2, gb_out, gb_query, gb_up, gb_value = (x.reshape(-1) for x in results[4:])

    return (
        output,
        grad_tokens,
        g_query,
        g_key,
        g_value,
        g_out,
        g_up,
        g_down,
        gb_query,
        gb_value,
        gb_out,
        gb_up,
        gb_down,
        gg1,
        gs1,
        gg2,
        gs2,
        g_pos,
    )


def solution(mesh):
    data = P(None, "fsdp", "ctx", None)
    groups = P(None, "fsdp", None)
    matrix, vector = P("fsdp", None), P("fsdp")
    return jax.shard_map(
        shards,
        mesh=mesh,
        in_specs=(data, data, groups, groups) + (matrix,) * 6 + (vector,) * 9 + (matrix,),
        out_specs=(data, data) + (matrix,) * 6 + (vector,) * 9 + (matrix,),
        check_vma=False,
    )
```

```python
import functools

import jax
import jax.numpy as jnp
from jax import lax
from jax.experimental import pallas as pl
from jax.experimental.pallas import tpu as pltpu
from jax.sharding import PartitionSpec as P

HEADS = 8
epsilon = 1e-05
gelu_coeff = 0.7978845608028654
cubic_coeff = 0.044715
BF = jnp.bfloat16
F32 = jnp.float32
SWAP = ((0, 1), (1, 0))
BOTH = ("ctx", "fsdp")
FAR = 1 << 30


def dot(a, b):
    return jnp.dot(a, b, preferred_element_type=F32)


def dot_tn(a, b):
    return lax.dot_general(a, b, (((0,), (0,)), ((), ())), preferred_element_type=F32)


def dot_nt(a, b):
    return lax.dot_general(a, b, (((1,), (1,)), ((), ())), preferred_element_type=F32)


def gelu_parts(u):
    inner = gelu_coeff * (u + cubic_coeff * u * u * u)
    bent = jnp.tanh(inner)
    value = 0.5 * u * (1.0 + bent)
    slope = 0.5 * (1.0 + bent) + 0.5 * u * (1.0 - bent * bent) * gelu_coeff * (
        1.0 + 3.0 * cubic_coeff * u * u
    )
    return value, slope


def normalize(z):
    center = z - jnp.mean(z, axis=-1, keepdims=True)
    inv = lax.rsqrt(jnp.mean(center * center, axis=-1, keepdims=True) + epsilon)
    return center * inv, inv


def normalize_back(t, normed, inv):
    return inv * (
        t
        - jnp.mean(t, axis=-1, keepdims=True)
        - normed * jnp.mean(t * normed, axis=-1, keepdims=True)
    )


def first_places(info, spots):
    first, end = jnp.zeros_like(spots), 0
    for n in range(3, info.shape[0]):
        end = end + info[n]
        first = first + jnp.where(spots >= end, info[n], 0)
    return first


def lay(info, whole, own, other):
    n = own.shape[0]
    mine = info[0] == 0
    whole[0:n, :] = jnp.where(mine, own[...], other[...])
    whole[n : 2 * n, :] = jnp.where(mine, other[...], own[...])


def full_row(info, own, other, at, count=1):
    mine = info[0] == 0
    rows = [x[at + n : at + n + 1, :] for x in (own, other) for n in range(count)]
    first = [jnp.where(mine, rows[n], rows[count + n]) for n in range(count)]
    second = [jnp.where(mine, rows[count + n], rows[n]) for n in range(count)]
    return jnp.concatenate(first + second, axis=1)


def stack_vectors(vectors, width):
    row, at = iota((16, width), 0), 0
    table = jnp.zeros((16, width), BF)
    for x in vectors:
        for n in range(x.shape[0] // width):
            part = x[n * width : n * width + width]
            table = jnp.where(row == at, part[None, :], table)
            at += 1
    return table.astype(F32)


def iota(shape, axis):
    return lax.broadcasted_iota(jnp.int32, shape, axis)


def params(cols=0):
    return pltpu.CompilerParams(vmem_limit_bytes=(32 if cols <= 2048 else 56) * 1024 * 1024)


def lasting(us):
    return pl.CostEstimate(flops=us, transcendentals=0, bytes_accessed=us)


def fixed(shape):
    return pl.BlockSpec(shape, lambda *_: (0,) * len(shape), pipeline_mode=pl.Buffered(1))


def paired(rows):
    return pl.BlockSpec((rows, 128), lambda p, *_: (0, p))


def project_kernel(info, *refs, blocks, offset, own):
    toks = refs[:blocks]
    pos_a, pos_b, wk_a, wk_b, wv_a, wv_b, wq_a, wq_b, vec_a, vec_b = refs[blocks : blocks + 10]
    outs = refs[blocks + 10 :]
    k_ref, v_ref = outs[:2]
    wk, wv, wq, tok = outs[-4:]
    step = pl.program_id(0)
    rows = tok.shape[0]

    @pl.when(step == 0)
    def _():
        lay(info, wk, wk_a, wk_b)
        lay(info, wv, wv_a, wv_b)
        if own:
            lay(info, wq, wq_a, wq_b)

    for n in range(blocks):

        @pl.when(step == n)
        def _():
            tok[...] = toks[n][...]

    spots = info[1] + offset + step * rows + iota((rows, 1), 0)
    place = spots - first_places(info, spots)
    hidden = tok[...].astype(F32)
    half = pos_a.shape[0]
    chunk = min(half, 512)
    for part, begin in ((pos_a, info[0] * half), (pos_b, (1 - info[0]) * half)):
        for at in range(0, half, chunk):
            hot = (place - begin - at == iota((rows, chunk), 1)).astype(F32).astype(BF)
            hidden = hidden + dot(hot, part[at : at + chunk, :])
    low = hidden.astype(BF)
    k_ref[...] = dot(low, wk[...]).astype(BF)
    v_ref[...] = (dot(low, wv[...]) + full_row(info, vec_a, vec_b, 7)).astype(BF)
    if own:
        q_ref, hidden_ref, low_ref = outs[2:5]
        q_ref[...] = ((dot(low, wq[...]) + full_row(info, vec_a, vec_b, 6)).astype(BF).astype(F32) * 0.125).astype(BF)
        hidden_ref[...] = hidden
        low_ref[...] = low


def project(info, toks, offset, own, pos, wk, wv, wq, vec):
    rows, width = toks[0].shape
    blocks = len(toks)
    tall = pl.BlockSpec((rows, width), lambda n, *_: (n, 0))
    flat = jax.ShapeDtypeStruct((rows * blocks, width), BF)
    square = pltpu.VMEM((width, width), BF)
    args = (*toks, *pos, *wk, *wv, *wq, *vec)
    return pl.pallas_call(
        functools.partial(project_kernel, blocks=blocks, offset=offset, own=own),
        grid_spec=pltpu.PrefetchScalarGridSpec(
            num_scalar_prefetch=1,
            grid=(blocks,),
            in_specs=[fixed(x.shape) for x in args],
            out_specs=[tall] * (5 if own else 2),
            scratch_shapes=[square, square, square, pltpu.VMEM((rows, width), BF)],
        ),
        out_shape=[flat] * 3 + [jax.ShapeDtypeStruct((rows, width), F32), flat] if own else [flat] * 2,
        compiler_params=pltpu.CompilerParams(vmem_limit_bytes=60 * 1024 * 1024),
        cost_estimate=lasting(2 * blocks + 2),
        name="project",
    )(info, *args)


def stat_rows(table):
    high = table.astype(BF).astype(F32)
    middle = (table - high).astype(BF).astype(F32)
    low = table - high - middle
    count = table.shape[1] // 128
    rows = [
        part[half : half + 1, 128 * n : 128 * n + 128]
        for part in (high, middle, low)
        for half in range(2)
        for n in range(count)
    ]
    rows.append(jnp.zeros((16 - len(rows), 128), F32))
    return jnp.concatenate(rows, axis=0).astype(BF)


def stat_row(rows16, half, queries):
    count = queries // 128
    wide = rows16.astype(F32)
    total = wide[0 : 2 * count] + wide[2 * count : 4 * count] + wide[4 * count : 6 * count]
    return jnp.concatenate([total[half * count + n : half * count + n + 1] for n in range(count)], axis=1)


def chunks_of(cols):
    step = cols if cols <= 2048 else 768
    return [slice(at, min(at + step, cols)) for at in range(0, cols, step)]


def bias_scratch(rows, cols):
    return pltpu.VMEM((rows, cols) if len(chunks_of(cols)) == 1 else (8, 128), F32)


def query_bias(info, rows, before, chunk):
    spots = info[1] + iota((rows, 1), 0)
    first = first_places(info, spots) - (info[1] - before)
    last = iota((rows, 1), 0) + before
    col = iota((rows, chunk.stop - chunk.start), 1) + chunk.start
    return jnp.where((col >= first) & (col <= last), 0.0, -1e30)


def key_bias(info, rows, chunk):
    spots = info[1] + chunk.start + iota((1, chunk.stop - chunk.start), 1)
    first = jnp.where(spots < info[2], first_places(info, spots) - info[1], FAR)
    shape = (rows, chunk.stop - chunk.start)
    row = iota(shape, 0)
    return jnp.where((row >= first) & (row <= iota(shape, 1) + chunk.start), 0.0, -1e30)


def forward_kernel(info, q_ref, kp_ref, k_ref, vp_ref, v_ref, a_ref, exact_ref, log_ref, stat_ref, bias, keys, values):
    rows, before = q_ref.shape[0], kp_ref.shape[0]

    chunks = chunks_of(keys.shape[0])
    make_bias = functools.partial(query_bias, info, rows, before)

    @pl.when(pl.program_id(0) == 0)
    def _():
        if len(chunks) == 1:
            bias[...] = make_bias(chunks[0])

    keys[0:before, :] = kp_ref[...]
    keys[before:, :] = k_ref[...]
    values[0:before, :] = vp_ref[...]
    values[before:, :] = v_ref[...]
    logs = []
    for half in range(2):
        lanes = slice(64 * half, 64 * half + 64)


        def scores_of(chunk):
            mask = bias[...] if len(chunks) == 1 else make_bias(chunk)
            return dot_nt(q_ref[:, lanes], keys[chunk, lanes]) + mask

        if len(chunks) == 1:
            scores = scores_of(chunks[0])
            top = jnp.max(scores, axis=1, keepdims=True)
            raised = jnp.exp(scores - top)
            total = jnp.sum(raised, axis=1, keepdims=True)
            probs = raised * (1.0 / total)
            low = probs.astype(BF)
            attended = dot(low, values[:, lanes])
            weight = jnp.sum(low.astype(F32), axis=1, keepdims=True)
        else:
            top = jnp.full((rows, 1), -1e30, F32)
            for chunk in chunks:
                top = jnp.maximum(top, jnp.max(scores_of(chunk), axis=1, keepdims=True))
            total = jnp.zeros((rows, 1), F32)
            for chunk in chunks:
                total = total + jnp.sum(jnp.exp(scores_of(chunk) - top), axis=1, keepdims=True)
            attended, weight = jnp.zeros((rows, 64), F32), jnp.zeros((rows, 1), F32)
            for chunk in chunks:
                probs = jnp.exp(scores_of(chunk) - top) * (1.0 / total)
                low = probs.astype(BF)
                attended = attended + dot(low, values[chunk, lanes])
                weight = weight + jnp.sum(low.astype(F32), axis=1, keepdims=True)
        a_ref[:, lanes] = attended.astype(BF)
        exact_ref[:, lanes] = attended / weight
        logs.append(jnp.broadcast_to(top + jnp.log(total), (rows, 64)))
    wide = jnp.concatenate(logs, axis=1)
    log_ref[...] = wide
    turned = wide.T
    stat_ref[...] = stat_rows(jnp.concatenate([turned[0:1], turned[64:65]], axis=0))


def attend_forward(info, q, kp, k, vp, v):
    rows, width = q.shape
    before = kp.shape[0]
    cols = before + rows
    return pl.pallas_call(
        forward_kernel,
        grid_spec=pltpu.PrefetchScalarGridSpec(
            num_scalar_prefetch=1,
            grid=(width // 128,),
            in_specs=[paired(x.shape[0]) for x in (q, kp, k, vp, v)],
            out_specs=[paired(rows), paired(rows), paired(rows), paired(16)],
            scratch_shapes=[
                bias_scratch(rows, cols),
                pltpu.VMEM((cols, 128), BF),
                pltpu.VMEM((cols, 128), BF),
            ],
        ),
        out_shape=[
            jax.ShapeDtypeStruct((rows, width), BF),
            jax.ShapeDtypeStruct((rows, width), F32),
            jax.ShapeDtypeStruct((rows, width), F32),
            jax.ShapeDtypeStruct((16, width), BF),
        ],
        compiler_params=params(cols),
        cost_estimate=lasting(12),
        name="attend_forward",
    )(info, q, kp, k, vp, v)


def ffn_kernel(
    info, a_ref, exact_ref, stat_ref, hidden_ref, arrived_ref, row_ref, col_ref, wo_a, wo_b, wu_a, wu_b, wd_a, wd_b, vec_a, vec_b,
    leaving_ref, msg_ref, dz1_ref, active_ref, df_ref, h1_ref, du_ref, do_ref, sums_ref,
    wo, wu, wd, slopes, stats,
):
    lay(info, wo, wo_a, wo_b)
    lay(info, wu, wu_a, wu_b)
    lay(info, wd, wd_a, wd_b)
    rows, width = hidden_ref.shape
    hidden_units = wu.shape[1]
    bo, bd, g1, s1, g2, s2 = (full_row(info, vec_a, vec_b, n) for n in range(6))
    bu = full_row(info, vec_a, vec_b, 8, hidden_units // width)
    pick = (iota((rows, rows), 0) == row_ref[...]).astype(F32).astype(BF)
    pick_back = (col_ref[...] == iota((rows, rows), 1)).astype(F32).astype(BF)
    dy = dot(pick, arrived_ref[...])

    n1, r1 = normalize(hidden_ref[...] + dot(a_ref[...], wo[...]) + bo)
    h1 = n1 * g1 + s1
    h1_low = h1.astype(BF)
    h1_ref[...] = h1_low
    z2 = h1 + bd
    for at in range(0, hidden_units, width):
        block = slice(at, at + width)
        value, slope = gelu_parts(dot(h1_low, wu[:, block]) + bu[:, block])
        slopes[:, block] = slope
        low = value.astype(BF)
        active_ref[:, block] = low
        z2 = z2 + dot(low, wd[block, :])
    n2, r2 = normalize(z2)
    leaving_ref[...] = dot(pick_back, (n2 * g2 + s2).astype(BF)).astype(BF)

    def add(x):
        return jnp.sum(x, axis=0, keepdims=True)

    dz2 = normalize_back(dy * g2, n2, r2)
    df = dz2.astype(BF)
    df_ref[...] = df
    sums_ref[0:1, :] = add(df.astype(F32))
    sums_ref[3:4, :] = add(dy * n2)
    sums_ref[4:5, :] = add(dy)
    dh1 = dz2
    for at in range(0, hidden_units, width):
        block = slice(at, at + width)
        du = (dot_nt(df, wd[block, :]) * slopes[:, block]).astype(BF)
        du_ref[:, block] = du
        n = 7 + at // width
        sums_ref[n : n + 1, :] = add(du.astype(F32))
        dh1 = dh1 + dot_nt(du, wu[:, block])
    dz1 = normalize_back(dh1 * g1, n1, r1)
    dz1_ref[...] = dz1
    sums_ref[1:2, :] = add(dh1 * n1)
    sums_ref[2:3, :] = add(dh1)
    do = dz1.astype(BF)
    do_ref[...] = do
    sums_ref[5:6, :] = add(do.astype(F32))
    sums_ref[6:7, :] = jnp.zeros((1, width), F32)
    sums_ref[11:16, :] = jnp.zeros((5, width), F32)
    da = dot_nt(do, wo[...]).astype(BF)
    msg_ref[0:rows, :] = da
    terms = da.astype(F32) * exact_ref[...]
    head = iota((HEADS, width), 0)
    lane = iota((HEADS, width), 1) // (width // HEADS)
    ones = (head == lane).astype(F32).astype(BF)
    delta = jnp.zeros((HEADS, rows), F32)
    for _ in range(3):
        part = terms.astype(BF)
        terms = terms - part.astype(F32)
        delta = delta + dot_nt(ones, part)
    for p in range(HEADS // 2):
        stats[:, 128 * p : 128 * p + 128] = stat_rows(delta[2 * p : 2 * p + 2, :])
    msg_ref[rows : rows + 16, :] = stat_ref[...]
    msg_ref[rows + 16 : rows + 32, :] = stats[...]


def feed_forward(info, a, exact, log_stats, hidden, arrived, mine, wo, wu, wd, vec):
    rows, width = hidden.shape
    units = wu[0].shape[1]
    args = (a, exact, log_stats, hidden, arrived, *mine, *wo, *wu, *wd, *vec)
    low = jax.ShapeDtypeStruct((rows, width), BF)
    tall = jax.ShapeDtypeStruct((rows, units), BF)
    outs = [
        low,
        jax.ShapeDtypeStruct((rows + 32, width), BF),
        jax.ShapeDtypeStruct((rows, width), F32),
        tall,
        low,
        low,
        tall,
        low,
        jax.ShapeDtypeStruct((16, width), F32),
    ]
    return pl.pallas_call(
        ffn_kernel,
        grid_spec=pltpu.PrefetchScalarGridSpec(
            num_scalar_prefetch=1,
            grid=(1,),
            in_specs=[fixed(x.shape) for x in args],
            out_specs=[fixed(x.shape) for x in outs],
            scratch_shapes=[
                pltpu.VMEM((width, width), BF),
                pltpu.VMEM((width, units), BF),
                pltpu.VMEM((units, width), BF),
                pltpu.VMEM((rows, units), F32),
                pltpu.VMEM((16, width), BF),
            ],
        ),
        out_shape=outs,
        compiler_params=params(),
        cost_estimate=lasting(10),
        name="feed_forward",
    )(info, *args)


def keep_or_send(info, half, mine, send, at, value):
    at, value = pl.multiple_of(at, 8), value.astype(BF)

    @pl.when(info[0] == half)
    def _():
        mine[pl.ds(at, value.shape[0]), :] = value

    @pl.when(info[0] != half)
    def _():
        send[pl.ds(at, value.shape[0]), :] = value


def split_halves(info, mine, send, starts, value):
    half, step = value.shape[0] // 2, value.shape[0] // 8
    first = info[0] == 0
    own = jnp.where(first, value[:half], value[half:]).astype(BF)
    other = jnp.where(first, value[half:], value[:half]).astype(BF)
    for n, at in enumerate(starts):
        mine[at : at + step, :] = own[n * step : n * step + step]
        send[at : at + step, :] = other[n * step : n * step + step]


def grads_kernel(
    info, a_own, a_other, do_ref, active_own, active_other, df_ref, h1_ref, du_ref, mine, send, *, quarter
):
    width = df_ref.shape[1]
    step = pl.program_id(0)
    part = active_own.shape[1]
    mine[0:part, :] = dot_tn(active_own[...], df_ref[...]).astype(BF)
    send[0:part, :] = dot_tn(active_other[...], df_ref[...]).astype(BF)
    up = dot_tn(h1_ref[...], du_ref[...])
    low, high = up[: width // 2].astype(BF), up[width // 2 :].astype(BF)
    at = part + width // 2
    mine[part:at, :] = jnp.where(info[0] == 0, low, high)
    send[part:at, :] = jnp.where(info[0] == 0, high, low)
    for out, a_ref in ((mine, a_own), (send, a_other)):
        both = dot_tn(a_ref[...], do_ref[...]).astype(BF)
        out[at : at + 64, :] = jnp.where(step % 2 == 0, both[:64], both[64:])
        if quarter > at + 64:
            out[at + 64 :, :] = jnp.zeros((quarter - at - 64, width), BF)


def ffn_grads(info, a, do, active, df, h1, du, quarter):
    rows, width = df.shape
    units = active.shape[1]
    out = jax.ShapeDtypeStruct((4 * quarter, width), BF)
    columns = lambda n, index: pl.BlockSpec((rows, n), lambda j, info: (0, index(j, info[0])))
    return pl.pallas_call(
        functools.partial(grads_kernel, quarter=quarter),
        grid_spec=pltpu.PrefetchScalarGridSpec(
            num_scalar_prefetch=1,
            grid=(4,),
            in_specs=[
                columns(128, lambda j, core: core * 2 + j // 2),
                columns(128, lambda j, core: (1 - core) * 2 + j // 2),
                fixed(do.shape),
                columns(units // 8, lambda j, core: core * 4 + j),
                columns(units // 8, lambda j, core: (1 - core) * 4 + j),
                fixed(df.shape),
                fixed(h1.shape),
                columns(units // 4, lambda j, core: j),
            ],
            out_specs=[pl.BlockSpec((quarter, width), lambda j, *_: (j, 0))] * 2,
        ),
        out_shape=[out, out],
        compiler_params=params(),
        cost_estimate=lasting(10),
        name="ffn_grads",
    )(info, a, a, do, active, active, df, h1, du)


def query_kernel(
    info, q_ref, kp_ref, k_ref, vp_ref, v_ref, log_ref, da_ref, exact_ref, dq_ref, bias, keys, values
):
    rows, before = q_ref.shape[0], kp_ref.shape[0]
    chunks = chunks_of(keys.shape[0])
    make_bias = functools.partial(query_bias, info, rows, before)

    @pl.when(pl.program_id(0) == 0)
    def _():
        if len(chunks) == 1:
            bias[...] = make_bias(chunks[0])

    keys[0:before, :] = kp_ref[...]
    keys[before:, :] = k_ref[...]
    values[0:before, :] = vp_ref[...]
    values[before:, :] = v_ref[...]
    for half in range(2):
        lanes = slice(64 * half, 64 * half + 64)
        delta = jnp.sum(da_ref[:, lanes].astype(F32) * exact_ref[:, lanes], axis=1, keepdims=True)
        dq = jnp.zeros((rows, 64), F32)
        for chunk in chunks:
            mask = bias[...] if len(chunks) == 1 else make_bias(chunk)
            scores = dot_nt(q_ref[:, lanes], keys[chunk, lanes]) + mask
            probs = jnp.exp(scores - log_ref[:, 64 * half : 64 * half + 1])
            dp = dot_nt(da_ref[:, lanes], values[chunk, lanes])
            ds = (probs * (dp - delta)).astype(BF)
            dq = dq + dot(ds, keys[chunk, lanes])
        dq_ref[:, lanes] = (dq * 0.125).astype(BF)


def attend_query(info, first, count, q, kp, k, vp, v, logs, da, exact):
    rows = q.shape[0]
    before = kp.shape[0]
    cols = before + rows
    some = lambda n: pl.BlockSpec((n, 128), lambda p, *_: (0, p + first))
    return pl.pallas_call(
        query_kernel,
        grid_spec=pltpu.PrefetchScalarGridSpec(
            num_scalar_prefetch=1,
            grid=(count,),
            in_specs=[some(x.shape[0]) for x in (q, kp, k, vp, v, logs)] + [some(rows), some(rows)],
            out_specs=paired(rows),
            scratch_shapes=[
                bias_scratch(rows, cols),
                pltpu.VMEM((cols, 128), BF),
                pltpu.VMEM((cols, 128), BF),
            ],
        ),
        out_shape=jax.ShapeDtypeStruct((rows, 128 * count), BF),
        compiler_params=params(cols),
        cost_estimate=lasting(5),
        name="attend_query",
    )(info, q, kp, k, vp, v, logs, da, exact)


def last_kernel(info, *refs, reach, quarter, table):
    count = 2 * reach + 1
    q_parts, da_parts = refs[:count], refs[count : 2 * count]
    k_ref, v_ref, low_ref, dq_a, dq_b, dz1_ref, sums_ref, wq_a, wq_b, wk_a, wk_b, wv_a, wv_b = refs[2 * count : 2 * count + 13]
    mine, send, dh_out, bias, queries, grads, dk_all, dv_all, wq, wk, wv = refs[2 * count + 13 :]
    rows, width = low_ref.shape
    cols = queries.shape[0]
    step = pl.program_id(0)

    chunks = chunks_of(cols)
    make_bias = functools.partial(key_bias, info, rows)

    @pl.when(step == 0)
    def _():
        lay(info, wq, wq_a, wq_b)
        lay(info, wk, wk_a, wk_b)
        lay(info, wv, wv_a, wv_b)
        if len(chunks) == 1:
            bias[...] = make_bias(chunks[0])

    for n in range(count):
        queries[n * rows : n * rows + rows, :] = q_parts[n][...]
        grads[n * rows : n * rows + rows, :] = da_parts[n][0:rows, :]
    dks, dvs = [], []
    for half in range(2):
        lanes = slice(64 * half, 64 * half + 64)
        logs = jnp.concatenate([stat_row(x[rows : rows + 16, :], half, rows) for x in da_parts], axis=1)
        delta = jnp.concatenate([stat_row(x[rows + 16 : rows + 32, :], half, rows) for x in da_parts], axis=1)
        dk, dv = jnp.zeros((rows, 64), F32), jnp.zeros((rows, 64), F32)
        for chunk in chunks:
            mask = bias[...] if len(chunks) == 1 else make_bias(chunk)
            scores = dot_nt(k_ref[:, lanes], queries[chunk, lanes]) + mask
            probs = jnp.exp(scores - logs[:, chunk])
            dv = dv + dot(probs.astype(BF), grads[chunk, lanes])
            dp = dot_nt(v_ref[:, lanes], grads[chunk, lanes])
            ds = (probs * (dp - delta[:, chunk])).astype(BF)
            dk = dk + dot(ds, queries[chunk, lanes])
        dks.append(dk.astype(BF))
        dvs.append(dv.astype(BF))
    dk_pair, dv_pair = jnp.concatenate(dks, axis=1), jnp.concatenate(dvs, axis=1)
    for n in range(width // 128):

        @pl.when(step == n)
        def _():
            dk_all[:, 128 * n : 128 * n + 128] = dk_pair
            dv_all[:, 128 * n : 128 * n + 128] = dv_pair

    @pl.when(step == pl.num_programs(0) - 1)
    def _():
        dk, dv = dk_all[...], dv_all[...]
        step_rows = width // 8
        turned = low_ref[...].T
        split_halves(info, mine, send, [n * quarter for n in range(4)], dot(turned, dk))
        split_halves(info, mine, send, [n * quarter + step_rows for n in range(4)], dot(turned, dv))
        dq = jnp.concatenate([dq_a[...], dq_b[...]], axis=1)
        split_halves(info, mine, send, [n * quarter + 2 * step_rows for n in range(4)], dot(turned, dq))
        dh = dz1_ref[...] + dot_nt(dq, wq[...]) + dot_nt(dk, wk[...]) + dot_nt(dv, wv[...])
        dh_out[...] = dh.astype(BF)
        parts = []
        for _ in range(2):
            parts.append(dh.astype(BF))
            dh = dh - parts[-1].astype(F32)
        spots = info[1] + iota((1, rows), 1)
        place = spots - first_places(info, spots)
        base = 3 * step_rows
        fourth = table // 8
        for half in range(2):
            for n in range(4):
                hot = (place - (half * 4 + n) * fourth == iota((fourth, rows), 0)).astype(F32).astype(BF)
                total = dot(hot, parts[0]) + dot(hot, parts[1])
                keep_or_send(info, half, mine, send, n * quarter + base, total)
        base += fourth
        spare = quarter - base
        for n in range(4):
            mine[n * quarter + base : (n + 1) * quarter, :] = jnp.zeros((spare, width), BF)
            send[n * quarter + base : (n + 1) * quarter, :] = jnp.zeros((spare, width), BF)
        total_v = jnp.sum(dv.astype(F32), axis=0, keepdims=True)
        total_q = jnp.sum(dq.astype(F32), axis=0, keepdims=True)
        row = iota(sums_ref.shape, 0)
        total = jnp.where(row == 6, total_q, jnp.where(row == 11, total_v, sums_ref[...])).astype(BF)
        mine[base : base + 16, :] = total
        send[base : base + 16, :] = total


def last(info, q_parts, da_parts, k, v, low, dqs, dz1, sums, wq, wk, wv, quarter, table):
    rows, width = k.shape
    count = len(q_parts)
    cols = count * rows
    outs = [
        jax.ShapeDtypeStruct((4 * quarter, width), BF),
        jax.ShapeDtypeStruct((4 * quarter, width), BF),
        jax.ShapeDtypeStruct((rows, width), BF),
    ]
    rest = (low, *dqs, dz1, sums, *wq, *wk, *wv)
    return pl.pallas_call(
        functools.partial(last_kernel, reach=count // 2, quarter=quarter, table=table),
        grid_spec=pltpu.PrefetchScalarGridSpec(
            num_scalar_prefetch=1,
            grid=(width // 128,),
            in_specs=[paired(x.shape[0]) for x in (*q_parts, *da_parts, k, v)] + [fixed(x.shape) for x in rest],
            out_specs=[fixed(x.shape) for x in outs],
            scratch_shapes=[
                bias_scratch(rows, cols),
                pltpu.VMEM((cols, 128), BF),
                pltpu.VMEM((cols, 128), BF),
                pltpu.VMEM((rows, width), BF),
                pltpu.VMEM((rows, width), BF),
                pltpu.VMEM((width, width), BF),
                pltpu.VMEM((width, width), BF),
                pltpu.VMEM((width, width), BF),
            ],
        ),
        out_shape=outs,
        compiler_params=params(cols),
        cost_estimate=lasting(15),
        name="last",
    )(info, *q_parts, *da_parts, k, v, *rest)


def cut_kernel(digit_ref, *refs, terms, radix):
    ins, outs = refs[: terms * radix], refs[terms * radix :]
    for k in range(radix):
        total = ins[k * terms][...].astype(F32)
        for n in range(1, terms):
            total = total + ins[k * terms + n][...].astype(F32)
        outs[k][...] = total.astype(outs[k].dtype)


def rows_of(terms):
    return terms[0][0].shape[0] // (1 + max(block for _, block in terms))


def cut(terms, digit, radix, kept):
    rows, width = rows_of(terms) // radix, terms[0][0].shape[1]
    subs = 1
    specs = [
        pl.BlockSpec((rows // subs, width), lambda n, d, k=k, b=b: ((b * radix + (d[0] ^ k)) * subs + n, 0))
        for k in range(radix)
        for _, b in terms
    ]
    return pl.pallas_call(
        functools.partial(cut_kernel, terms=len(terms), radix=radix),
        grid_spec=pltpu.PrefetchScalarGridSpec(
            num_scalar_prefetch=1,
            grid=(subs,),
            in_specs=specs,
            out_specs=[pl.BlockSpec((rows // subs, width), lambda n, d: (n, 0))] * radix,
        ),
        out_shape=[jax.ShapeDtypeStruct((rows, width), BF if k else kept) for k in range(radix)],
        compiler_params=params(),
        cost_estimate=lasting(3),
        name="cut",
    )(digit.reshape(1), *([x for x, _ in terms] * radix))


def total_of(refs):
    total = refs[0][...].astype(F32)
    for ref in refs[1:]:
        total = total + ref[...].astype(F32)
    return total


def join_kernel(digit_ref, *refs, ones, twos, radix):
    done, held, *messages = refs[ones + twos * radix :]
    rows = done.shape[0]
    whole = total_of(refs[:ones]).astype(BF)
    done[...] = whole
    for k in range(radix):
        piece = total_of(refs[ones + k * twos : ones + (k + 1) * twos])
        if k:
            messages[k - 1][0:rows, :] = whole
            messages[k - 1][rows:, :] = piece.astype(BF)
        else:
            held[...] = piece


def join(first, second, digit, radix):
    (rows, width), part = first[0].shape, rows_of(second) // radix
    specs = [
        pl.BlockSpec((part, width), lambda n, d, k=k, b=b: (b * radix + (d[0] ^ k), 0))
        for k in range(radix)
        for _, b in second
    ]
    outs = [jax.ShapeDtypeStruct((rows, width), BF), jax.ShapeDtypeStruct((part, width), F32)]
    outs += [jax.ShapeDtypeStruct((rows + part, width), BF)] * (radix - 1)
    return pl.pallas_call(
        functools.partial(join_kernel, ones=len(first), twos=len(second), radix=radix),
        grid_spec=pltpu.PrefetchScalarGridSpec(
            num_scalar_prefetch=1,
            grid=(1,),
            in_specs=[fixed((rows, width))] * len(first) + specs,
            out_specs=[fixed(x.shape) for x in outs],
        ),
        out_shape=outs,
        compiler_params=params(),
        cost_estimate=lasting(3),
        name="join",
    )(digit.reshape(1), *first, *([x for x, _ in second] * radix))


def below_kernel(held_ref, *refs, copies):
    *parts, out = refs
    rows = held_ref.shape[0]
    total = held_ref[...]
    for part in parts:
        total = total + part[part.shape[0] - rows :, :].astype(F32)
    for n in range(copies):
        out[n * rows : n * rows + rows, :] = total.astype(BF)


def add_below(held, messages, copies):
    out = jax.ShapeDtypeStruct((copies * held.shape[0], held.shape[1]), BF)
    return pl.pallas_call(
        functools.partial(below_kernel, copies=copies),
        grid=(1,),
        in_specs=[fixed(x.shape) for x in (held, *messages)],
        out_specs=fixed(out.shape),
        out_shape=out,
        compiler_params=params(),
        cost_estimate=lasting(2),
        name="add_below",
    )(held, *messages)


def place_kernel(digit_ref, *refs, radix, sizes, counts):
    parts, outs, vectors = refs[:radix], refs[radix : radix + len(sizes)], refs[radix + len(sizes) :]
    for k in range(radix):

        @pl.when(pl.program_id(0) == k)
        def _():
            at = 0
            for out, size in zip(outs, sizes):
                out[...] = parts[k][at : at + size, :].astype(out.dtype)
                at += size

            if not counts:
                return

            @pl.when(digit_ref[0] == k)
            def _():
                row = at
                for out, count in zip(vectors, counts):
                    whole = jnp.concatenate([parts[k][row + n : row + n + 1, :] for n in range(count)], axis=1)
                    whole = whole.astype(F32)
                    half = whole.shape[1] // 2
                    out[...] = jnp.where(digit_ref[1] == 0, whole[:, :half], whole[:, half:])
                    row += count


def place(parts, digit, sizes, dtype, across=None, core=None, counts=()):
    radix, width = len(parts), parts[0].shape[1]
    below = lambda k, d: (k ^ d[0], 0)
    beside = lambda k, d: (0, k ^ d[0])
    outs = [
        jax.ShapeDtypeStruct((n, width * radix) if i == across else (n * radix, width), dtype)
        for i, n in enumerate(sizes)
    ]
    halves = [jax.ShapeDtypeStruct((1, n * width // 2), F32) for n in counts]
    return pl.pallas_call(
        functools.partial(place_kernel, radix=radix, sizes=sizes, counts=counts),
        grid_spec=pltpu.PrefetchScalarGridSpec(
            num_scalar_prefetch=1,
            grid=(radix,),
            in_specs=[fixed(x.shape) for x in parts],
            out_specs=[
                pl.BlockSpec((n, width), beside if i == across else below) for i, n in enumerate(sizes)
            ]
            + [fixed(x.shape) for x in halves],
        ),
        out_shape=outs + halves,
        compiler_params=params(),
        cost_estimate=lasting(4),
        name="place",
    )(digit.reshape(1) if core is None else jnp.stack([digit, core]), *parts)


def exchange(pieces, here, stride, ranks):
    return [
        lax.ppermute(piece, "ctx", [(i, i ^ ((k + 1) * stride)) for i in range(ranks)])
        for k, piece in enumerate(pieces)
    ]


def stages_of(ranks):
    stages, stride = [], 1
    while stride < ranks:
        radix = 4 if (ranks // stride) % 4 == 0 else 2
        stages.append((stride, radix))
        stride *= radix
    return stages


def after(first, then):
    return lax.optimization_barrier((first, then))[1]


class Reduction:
    def __init__(self, here, ranks, sizes, across):
        self.here, self.ranks, self.sizes, self.across = here, ranks, sizes, across
        self.stages = stages_of(ranks)

    def digit(self, level):
        stride, radix = self.stages[level]
        return (self.here // stride) % radix

    def cut(self, terms, level):
        return cut([(x, 0) for x in terms], self.digit(level), self.stages[level][1], F32)

    def add(self, terms):
        return cut([(x, 0) for x in terms], self.here * 0, 1, BF)[0]

    def scatter(self, pieces, level):
        return [pieces[0]] + exchange(pieces[1:], self.here, self.stages[level][0], self.ranks)

    def trade(self, blocks, level):
        stride, radix = self.stages[level]
        groups = [
            [i + n * stride for n in range(radix)] for i in range(self.ranks) if (i // stride) % radix == 0
        ]
        return lax.all_to_all(blocks, "ctx", split_axis=0, concat_axis=0, axis_index_groups=groups, tiled=True)

    def gather(self, held, level):
        stride, radix = self.stages[level]
        return [held] + exchange([held] * (radix - 1), self.here, stride, self.ranks)

    def place(self, parts, level):
        if level:
            return place(parts, self.digit(level), [parts[0].shape[0]], BF, None)[0]
        return place(parts, self.digit(0), self.sizes, F32, self.across)


def padded(rows, ranks):
    step = 2 * ranks
    return -(-rows // step) * step


def swap_core(x):
    return lax.ppermute(x, "fsdp", SWAP)


def by_core(core, own, other):
    return jnp.where(core == 0, jnp.stack([own, other]), jnp.stack([other, own]))


def next_chip(block, chips, step):
    pairs = [(i, i + 4) for i in range(4 * (chips - 1))]
    return lax.ppermute(block, "ctx", pairs if step > 0 else [(b, a) for a, b in pairs])


def send_window(own, reach, chips, step):
    far = [own]
    for k in range(1, reach + 1):
        if step > 0:
            pairs = [(i, i + 4 * k) for i in range(4 * (chips - k))]
        else:
            pairs = [(i + 4 * k, i) for i in range(4 * (chips - k))]
        far.append(lax.ppermute(own, "ctx", pairs))
    return far


def both_cores(far, core, step):
    near = core == (0 if step > 0 else 1)
    parts = []
    for k in range(len(far) - 1):
        parts += [swap_core(jnp.where(near, far[k], far[k + 1])), far[k + 1]]
    return parts


def shards(
    tokens,
    cotangent,
    lengths,
    deal_order,
    w_query,
    w_key,
    w_value,
    w_out,
    w_up,
    w_down,
    b_query,
    b_value,
    b_out,
    b_up,
    b_down,
    gain_one,
    shift_one,
    gain_two,
    shift_two,
    positions,
):
    block, width = tokens.shape[2], tokens.shape[3]
    ranks = lax.axis_size("ctx")
    chips = ranks // 4
    slot = block // ranks
    rows = 2 * block
    group = ranks * block
    longest = 2 * positions.shape[0]
    reach = longest // (2 * rows)
    here = lax.axis_index("ctx")
    core = lax.axis_index("fsdp")
    chip, micro, stream = here // 4, here % 2, (here // 2) % 2
    base = chip * (2 * rows) + core * rows

    index = lambda i, t: 2 * i + t
    straight, crossing = [], []
    for i in range(ranks):
        c, a, b = i // 4, (i // 2) % 2, i % 2
        for t in range(2):
            straight.append((index(i, t), index(4 * c + 2 * t + b, a)))
            crossing.append((index(i, t), index(4 * c + 2 * t + 1 - b, a)))
    even = here % 2 == 0
    same = jnp.where(even, tokens[0, 0], tokens[1, 0])
    cross = jnp.where(even, tokens[1, 0], tokens[0, 0])
    got_same = lax.ppermute(same, BOTH, straight)
    got_cross = lax.ppermute(cross, BOTH, crossing)
    first_half = jnp.where(micro == 0, got_same, got_cross)
    second_half = jnp.where(micro == 0, got_cross, got_same)
    own = jnp.concatenate([first_half, second_half], axis=0)

    table = jnp.concatenate([deal_order[:, 0], lengths[:, 0]], axis=1)
    table = jnp.where(micro == 0, table[0], table[1])
    table = jnp.where(stream == core, table, swap_core(table))
    order, lens = table[:group], table[group:]

    head = jnp.stack([core, base, jnp.int32(group)]).astype(jnp.int32)
    info = jnp.concatenate([head, lens])

    whole = lambda x: (x, swap_core(x))
    pos, wq, wk, wv = whole(positions), whole(w_query), whole(w_key), whole(w_value)
    vectors = [b_out, b_down, gain_one, shift_one, gain_two, shift_two, b_query, b_value, b_up]
    vec = whole(stack_vectors(vectors, width // 2))
    wo, wu, wd = whole(w_out), whole(w_up), whole(w_down)

    fixed_args = (pos, wk, wv, wq, vec)
    far = [own]
    for _ in range(reach):
        far.append(next_chip(far[-1], chips, 1))
    k, v, q, hidden, low = project(info, [own], 0, True, *fixed_args)

    mine = order.reshape(ranks, ranks, slot)
    mine = lax.dynamic_slice_in_dim(mine, 4 * chip + 2 * core, 2, axis=1).reshape(rows) - base
    mine = (mine.reshape(1, rows), mine.reshape(rows, 1))
    dealt = cotangent[:, 0].reshape(2, chips, 2, 2 * slot, width)
    keep = jnp.where(core == 0, dealt[:, :, 0], dealt[:, :, 1])
    give = jnp.where(core == 0, dealt[:, :, 1], dealt[:, :, 0])
    streams = by_core(core, keep, swap_core(give))
    sends = jnp.transpose(streams, (2, 0, 1, 3, 4)).reshape(rows, width)
    sends = after(own, sends)
    arrived = lax.all_to_all(sends, "ctx", split_axis=0, concat_axis=0, tiled=True)

    far[1:] = after((mine, k), far[1:])
    arrived = after(far[1:], arrived)

    earlier = both_cores(far, core, 1)[::-1]
    before = len(earlier) * rows
    kp, vp = project(info, earlier, -before, False, *fixed_args)
    far_q = send_window(after(kp, q), reach, chips, -1)
    att, exact, logs, log_stats = attend_forward(info, after(arrived, q), kp, k, vp, v)
    leaving, da_msg, dz1, active, df, h1, du, do, sums = feed_forward(
        info, att, exact, log_stats, hidden, arrived, mine, wo, wu, wd, vec
    )
    da_msg, do, leaving = after(far_q[1:], (da_msg, do, leaving))
    far_da = [da_msg, next_chip(da_msg, chips, -1)]

    half = width // 2
    units = 2 * b_up.shape[0]
    sizes = [units // 8, half, width // 8]
    quarter = padded(sum(sizes), ranks)
    sizes_last = [width // 8, width // 8, width // 8, longest // 8]
    quarter_last = padded(sum(sizes_last) + 16, ranks)
    one = Reduction(here, ranks, sizes, 1)
    two = Reduction(here, ranks, sizes_last, None)
    levels = len(one.stages)

    pairs = width // 256
    query_args = (q, kp, k, vp, v, logs, da_msg)
    dq_first = attend_query(info, 0, pairs, *query_args, exact)
    do = after(dq_first, do)
    keep, give = ffn_grads(info, att, do, active, df, h1, du, quarter)
    give = after(far_da[1], give)
    for _ in range(reach - 1):
        far_da.append(next_chip(far_da[-1], chips, -1))
    pieces = one.cut([keep, swap_core(give)], 0)
    terms = one.scatter(pieces, 0)
    dq_second = attend_query(info, pairs, pairs, *query_args, after(pieces, exact))
    far_da[1:], far_q[1:] = after(dq_second, (far_da[1:], far_q[1:]))
    later_da = [da_msg] + both_cores(far_da, core, -1)
    later_q = [q] + both_cores(far_q, core, -1)
    dqs = (dq_first, dq_second)
    keep, give, dh0_low = last(
        info, later_q, later_da, k, v, low, dqs, dz1, sums, wq, wk, wv, quarter_last, longest
    )

    keep, give = after(terms[1:], (keep, give))
    terms_last = [keep, swap_core(give)]
    end = levels - 1
    for level in range(end):
        pieces = one.cut(terms, level + 1)
        terms = one.scatter(pieces, level + 1)
        pieces_last = two.cut(after(pieces, terms_last), level)
        terms_last = two.scatter(pieces_last, level)
    terms_last = [(x, 0) for x in terms_last]
    leaving = after(terms_last[1][0], leaving)
    stride, radix = one.stages[end]
    held, held_last, *messages = join(terms, terms_last, one.digit(end), radix)
    got = exchange(messages, here, stride, ranks)
    dh0_low = after(held, dh0_low)

    back_same = jnp.where(micro == 0, dh0_low[:block], dh0_low[block:])
    back_cross = jnp.where(micro == 0, dh0_low[block:], dh0_low[:block])
    home_same = lax.ppermute(back_same, BOTH, [(b, a) for a, b in straight])
    home_cross = lax.ppermute(back_cross, BOTH, [(b, a) for a, b in crossing])
    grad_tokens = jnp.where(
        even, jnp.stack([home_same, home_cross]), jnp.stack([home_cross, home_same])
    )[:, None]

    got = after((home_same, home_cross), got)
    held = place([held] + got, one.digit(end), [held.shape[0]], BF, None)[0]
    held_last = two.trade(add_below(held_last, after(held, got), radix), end)
    for level in reversed(range(1, end)):
        held = one.place(one.gather(held, level), level)
        held_last = two.place(two.gather(held_last, level), level)
    parts = one.gather(held, 0)
    held_last = after(parts[1], held_last)
    parts_last = two.gather(held_last, 0)
    held = one.place(parts, 0)
    landed = lax.all_to_all(leaving, "ctx", split_axis=0, concat_axis=0, tiled=True)

    landed = landed.reshape(chips, 2, 2, 2 * slot, width)
    keep = jnp.where(core == 0, landed[:, 0], landed[:, 1])
    give = jnp.where(core == 0, landed[:, 1], landed[:, 0])
    sides = by_core(core, keep, swap_core(give))
    output = jnp.transpose(sides, (2, 1, 0, 3, 4)).reshape(2, 1, block, width)
    counts = [1] * 7 + [units // width, 1]
    results = place(parts_last, two.digit(0), sizes_last, F32, None, core, counts)
    g_down, g_up, g_out = held
    g_key, g_value, g_query, g_pos = results[:4]
    gb_down, gg1, gs1, gg2, gs2, gb_out, gb_query, gb_up, gb_value = (x.reshape(-1) for x in results[4:])

    return (
        output,
        grad_tokens,
        g_query,
        g_key,
        g_value,
        g_out,
        g_up,
        g_down,
        gb_query,
        gb_value,
        gb_out,
        gb_up,
        gb_down,
        gg1,
        gs1,
        gg2,
        gs2,
        g_pos,
    )


def solution(mesh):
    data = P(None, "fsdp", "ctx", None)
    groups = P(None, "fsdp", None)
    matrix, vector = P("fsdp", None), P("fsdp")
    return jax.shard_map(
        shards,
        mesh=mesh,
        in_specs=(data, data, groups, groups) + (matrix,) * 6 + (vector,) * 9 + (matrix,),
        out_specs=(data, data) + (matrix,) * 6 + (vector,) * 9 + (matrix,),
        check_vma=False,
    )
```
